128 devices in a mesh: ctx: 32 (over y, x, core), tp: 4 (over z).
Axes of the slice: x: 4, y: 4, z: 4, core: 2. Of those that a mesh axis runs over, the one named last changes fastest.
Arguments:
- hidden: bfloat16 [8192, 5120], P('ctx', 'tp'), may hold values from -6 to 6
- queries: bfloat16 [8192, 5120], P('ctx', 'tp'), may hold values from -28 to 28
- key_weight: bfloat16 [5120, 1024], P(None, 'tp'), may hold values from -0.078125 to 0.078125
- value_weight: bfloat16 [5120, 1024], P(None, 'tp'), may hold values from -0.078125 to 0.078125
- parents: int32 [64], replicated, may hold values from -1 to 62, as said below
- upstream: bfloat16 [8192, 5120], P('ctx', 'tp'), may hold values from -6 to 6
Outputs:
- attention: bfloat16 [8192, 5120], P('ctx', 'tp')
- query_grad: bfloat16 [8192, 5120], P('ctx', 'tp')
- hidden_grad: bfloat16 [8192, 5120], P('ctx', 'tp')
- key_weight_grad: float32 [5120, 1024], P('ctx', 'tp')
- value_weight_grad: float32 [5120, 1024], P('ctx', 'tp')
The draws below stay inside these ranges and needn't reach their ends.
Inputs may be any that keep to these rules, and one draw needn't show every extreme that they name: Node blocks lie in depth-first order: parents[b] < b is the parent of block b for b > 0, parents[0] = -1 and block 0 is the only root; no root-to-leaf path holds more than 8 blocks; the last 7 blocks form one chain below block 0, so that the last block's path holds exactly 8 blocks.
All inputs are finite; a program needn't handle non-finite values.
Results may differ from the reference program's by a relative error of at most 0.023.
The reference program's roundings to bfloat16 on the way count: a program that leaves them out, or rounds other values in their place, can miss the bound.
Values may be sent and summed in bfloat16 or wider, within the bound.
No kernel may reach another device: no remote copies, remote signals or barrier semaphores. Data moves between devices by JAX's collectives and lax.ppermute only.
A program may use at most 128 MiB of HBM per device.

```python
import math
import jax
import jax.numpy as jnp
from jax import lax

D = 5120
QH = 40
KVH = 8
HD = 128
BLOCK = 128
DEPTH = 8
NBLK = 64
TOKENS = 8192
N_TP = 4


def draw_parents(key, part):
    coin_key = jax.random.fold_in(key, 1)
    jump_key = jax.random.fold_in(key, 2)
    coin_flips = jax.random.randint(coin_key, (NBLK,), 0, 4, dtype=jnp.int32)
    jump_draws = jax.random.randint(jump_key, (NBLK,), 0, 1 << 20, dtype=jnp.int32)
    forced_start = NBLK - DEPTH + 1

    def advance(previous, inputs):
        position, coin_flip, jump_draw = inputs
        deeper = jnp.minimum(previous + 1, DEPTH - 1)
        jumped = 1 + jump_draw % jnp.maximum(deeper, 1)
        forced = position >= forced_start
        chosen = jnp.where(coin_flip < 2, deeper, jumped)
        chosen = jnp.where(forced, position - forced_start + 1, chosen)
        chosen = jnp.where(position == 0, 0, chosen).astype(jnp.int32)
        return (chosen, chosen)
    positions = jnp.arange(NBLK, dtype=jnp.int32)
    final_depth, depths = lax.scan(advance, jnp.int32(0), (positions, coin_flips, jump_draws))
    earlier = positions[None, :] < positions[:, None]
    matches = earlier & (depths[None, :] == depths[:, None] - 1)
    return jnp.max(jnp.where(matches, positions[None, :], -1), axis=1).astype(jnp.int32)


def draw_queries(key, part):
    base_key = jax.random.fold_in(key, 5)
    return jnp.clip(jax.random.normal(base_key, (TOKENS, QH * HD), jnp.float32), -6.0, 6.0).astype(jnp.bfloat16)


def raised(entries, own_key, source, target, blocks, factor):
    def block_of(dim):
        return (jnp.arange(entries.shape[dim]) // (entries.shape[dim] // blocks)).reshape((-1,) + (1,) * (entries.ndim - 1 - dim))

    first = jax.random.permutation(own_key, blocks)[block_of(target)]
    far = (block_of(target) + blocks // 2) % blocks
    return jnp.where((block_of(source) == first) | (block_of(source) == far), factor * entries, entries)


def block_levels(own_key, extent, split, smallest, largest):
    gain, own = 1.0, jax.random.fold_in(own_key, 6)
    for dim, shards_of in split:
        draws = jnp.exp(jax.random.uniform(jax.random.fold_in(own, dim), (shards_of,), jnp.float32, smallest / len(split), largest / len(split)))
        gain = gain * jnp.repeat(draws, extent[dim] // shards_of).reshape([-1 if axis == dim else 1 for axis in range(len(extent))])
    return gain


def gaussian(own_key, extent, width, bound, pieces=(), held_as=jnp.bfloat16):
    factor_of = block_levels(own_key, extent, pieces, -0.22, 0.18) if pieces else 1.0
    values = jax.random.normal(own_key, extent, jnp.float32) * width * factor_of
    return jnp.minimum(jnp.maximum(values, -bound), bound).astype(held_as)


def heavy_noise(key, shape, scale, most, shards, heavy, kind=jnp.bfloat16):
    array = scale * jax.random.normal(key, shape, jnp.float32)
    if shards:
        array = array * block_levels(key, shape, shards, -0.22, 0.18)
    return jnp.clip(raised(array, jax.random.fold_in(key, 3), *heavy), -most, most).astype(kind)


def setup_inputs(seed: int = 0) -> dict:
    key_of = jax.random.split(jax.random.key(seed), 7)
    hidden = heavy_noise(key_of[0], (TOKENS, D), 1.0, 6.0, ((0, 32), (1, 4)), (0, 1, 32, 2.75))
    queries = draw_queries(jax.random.fold_in(key_of[6], 71), 0)
    key_weight = gaussian(key_of[2], (D, KVH * HD), D ** -0.5, 0.078125, ((1, 4),))
    value_weight = gaussian(key_of[3], (D, KVH * HD), D ** -0.5, 0.078125, ((1, 4),))
    parents = draw_parents(jax.random.fold_in(key_of[6], 71), 0)
    upstream = gaussian(key_of[5], (TOKENS, QH * HD), 1.0, 6.0, ((0, 32), (1, 4)))
    return {"hidden": hidden, "queries": queries, "key_weight": key_weight, "value_weight": value_weight, "parents": parents, "upstream": upstream}


THETA = 1000000.0
NEGATIVE = -1e+30
HIGHEST = lax.Precision.HIGHEST

def tree_tables(parents, block_total, depth_slots):
    indices = jnp.arange(block_total, dtype=jnp.int32)
    parent_link = (parents[:, None] == indices[None, :]).astype(jnp.float32)
    closure = jnp.eye(block_total, dtype=jnp.float32) + parent_link
    for repeat in range(depth_slots.bit_length()):
        closure = jnp.minimum(jnp.dot(closure, closure, precision=HIGHEST, preferred_element_type=jnp.float32), 1.0)
    closure_int = closure.astype(jnp.int32)
    depths = (lax.optimization_barrier(jnp.sum(closure_int, axis=1)) - 1).astype(jnp.int32)
    levels = jnp.arange(depth_slots, dtype=jnp.int32)
    select = closure_int[:, :, None] * (depths[None, :, None] == levels[None, None, :]).astype(jnp.int32)
    path_ids = (lax.optimization_barrier(jnp.sum(select * indices[None, :, None], axis=1)) + lax.optimization_barrier(jnp.sum(select, axis=1)) - 1).astype(jnp.int32)
    return (depths, path_ids)

def rope_angles(depths, block_len, head_width):
    offset = jnp.arange(block_len, dtype=jnp.int32)
    position = (depths[:, None] * block_len + offset[None, :]).astype(jnp.float32)
    midpoint = head_width // 2
    frequency = jnp.exp(jnp.arange(midpoint, dtype=jnp.float32) * (-2.0 * math.log(THETA) / head_width))
    angles = position[:, :, None] * frequency[None, None, :]
    return (jnp.cos(angles), jnp.sin(angles))

def rotate_pairs(fields, cosine, sine_table, direction):
    midpoint = fields.shape[-1] // 2
    leading = fields[..., :midpoint]
    trailing = fields[..., midpoint:]
    cos_part = cosine[:, :, None, :]
    sin_part = direction * sine_table[:, :, None, :]
    return jnp.concatenate([leading * cos_part - trailing * sin_part, trailing * cos_part + leading * sin_part], axis=-1)

def allowed_mask(depths, block_len, slot_count):
    query_pos = jnp.arange(block_len, dtype=jnp.int32)
    key_index = jnp.arange(slot_count * block_len, dtype=jnp.int32)
    key_slot = key_index // block_len
    key_offset = key_index % block_len
    earlier = key_slot[None, None, :] < depths[:, None, None]
    itself = (key_slot[None, None, :] == depths[:, None, None]) & (key_offset[None, None, :] <= query_pos[None, :, None])
    return earlier | itself

def attend_reference(query_blocks, key_rows, value_rows, allowed, upstream_blocks, score_scale):
    query_float = query_blocks.astype(jnp.float32)
    key_float = key_rows.astype(jnp.float32)
    value_float = value_rows.astype(jnp.float32)
    upstream_float = upstream_blocks.astype(jnp.float32)
    scores = jnp.einsum('bqhgd,bkhd->bhgqk', query_float, key_float, precision=HIGHEST) * score_scale
    scores = jnp.where(allowed[:, None, None], scores, NEGATIVE)
    maximum = lax.optimization_barrier(jnp.max(scores, axis=-1, keepdims=True))
    weights = jnp.exp(scores - maximum)
    totals = lax.optimization_barrier(jnp.sum(weights, axis=-1, keepdims=True))
    weights_round = lax.optimization_barrier(weights.astype(jnp.bfloat16)).astype(jnp.float32)
    mixed_rows = jnp.einsum('bhgqk,bkhd->bqhgd', weights_round, value_float, precision=HIGHEST)
    totals_rows = jnp.transpose(totals, (0, 3, 1, 2, 4))
    output = (mixed_rows / totals_rows).astype(jnp.bfloat16)
    output_float = lax.optimization_barrier(output).astype(jnp.float32)
    logsum = maximum + jnp.log(totals)
    deltas = jnp.transpose(lax.optimization_barrier(jnp.sum(upstream_float * output_float, axis=-1)), (0, 2, 3, 1))[..., None]
    probabilities = jnp.exp(scores - logsum)
    prob_round = lax.optimization_barrier(probabilities.astype(jnp.bfloat16)).astype(jnp.float32)
    value_grad = jnp.einsum('bhgqk,bqhgd->bkhd', prob_round, upstream_float, precision=HIGHEST)
    prob_grad = jnp.einsum('bqhgd,bkhd->bhgqk', upstream_float, value_float, precision=HIGHEST)
    score_grad = lax.optimization_barrier((probabilities * (prob_grad - deltas)).astype(jnp.bfloat16)).astype(jnp.float32)
    query_grad = (jnp.einsum('bhgqk,bkhd->bqhgd', score_grad, key_float, precision=HIGHEST) * score_scale).astype(jnp.bfloat16)
    key_grad = jnp.einsum('bhgqk,bqhgd->bkhd', score_grad, query_float, precision=HIGHEST) * score_scale
    return (output, query_grad, key_grad, value_grad)

def reference(hidden, queries, key_weight, value_weight, parents, upstream):
    groups = QH // KVH
    key_width = KVH * HD
    pair_width = 2 * key_width
    score_scale = 1.0 / math.sqrt(HD)
    depth_all, path_all = tree_tables(parents, NBLK, DEPTH)
    cosine, sine_table = rope_angles(depth_all, BLOCK, HD)
    key_linear = jnp.dot(hidden, key_weight, preferred_element_type=jnp.float32).reshape(NBLK, BLOCK, KVH, HD)
    key_rotated = rotate_pairs(key_linear, cosine, sine_table, 1.0).astype(jnp.bfloat16).reshape(NBLK, BLOCK, key_width)
    value_rows = jnp.dot(hidden, value_weight, preferred_element_type=jnp.float32).astype(jnp.bfloat16).reshape(NBLK, BLOCK, key_width)
    key_value = jnp.concatenate([key_rotated, value_rows], axis=-1)
    query_all = queries.reshape(NBLK, BLOCK, KVH, groups, HD)
    upstream_all = upstream.reshape(NBLK, BLOCK, KVH, groups, HD)

    def visit(accumulated, block_id):
        path_ids = jnp.clip(path_all[block_id], 0, NBLK - 1).astype(jnp.int32)
        slot_rows = key_value[path_ids].reshape(1, DEPTH * BLOCK, pair_width)
        key_part = slot_rows[..., :key_width].reshape(1, DEPTH * BLOCK, KVH, HD)
        value_part = slot_rows[..., key_width:].reshape(1, DEPTH * BLOCK, KVH, HD)
        allowed = allowed_mask(depth_all[block_id][None], BLOCK, DEPTH)
        output, query_grad, key_grad, value_grad = attend_reference(query_all[block_id][None], key_part, value_part, allowed, upstream_all[block_id][None], score_scale)
        slot_grads = jnp.concatenate([key_grad.reshape(DEPTH, BLOCK, key_width), value_grad.reshape(DEPTH, BLOCK, key_width)], axis=-1)
        accumulated = accumulated.at[path_ids].add(slot_grads)
        return (accumulated, (output[0], query_grad[0]))
    start_grads = jnp.zeros((NBLK, BLOCK, pair_width), jnp.float32)
    pair_grads, outputs = lax.scan(visit, start_grads, jnp.arange(NBLK, dtype=jnp.int32))
    attention = outputs[0].reshape(TOKENS, QH * HD)
    query_grad = outputs[1].reshape(TOKENS, QH * HD)
    key_total = pair_grads[..., :key_width].reshape(NBLK, BLOCK, KVH, HD)
    key_linear_grad = rotate_pairs(key_total, cosine, sine_table, -1.0).astype(jnp.bfloat16).reshape(TOKENS, key_width)
    value_grad_rows = pair_grads[..., key_width:].reshape(TOKENS, key_width).astype(jnp.bfloat16)
    key_weight_grad = jnp.dot(hidden.T, key_linear_grad, preferred_element_type=jnp.float32)
    value_weight_grad = jnp.dot(hidden.T, value_grad_rows, preferred_element_type=jnp.float32)
    share_width = key_width // N_TP
    total_grad = jnp.zeros((TOKENS, D), jnp.float32)
    for member in range(N_TP):
        low_col = member * share_width
        high_col = low_col + share_width
        partial_rows = jnp.dot(key_linear_grad[:, low_col:high_col], key_weight[:, low_col:high_col].T, preferred_element_type=jnp.float32)
        partial_rows = partial_rows + jnp.dot(value_grad_rows[:, low_col:high_col], value_weight[:, low_col:high_col].T, preferred_element_type=jnp.float32)
        total_grad = total_grad + lax.optimization_barrier(partial_rows.astype(jnp.bfloat16)).astype(jnp.float32)
    hidden_grad = total_grad.astype(jnp.bfloat16)
    return (attention, query_grad, hidden_grad, key_weight_grad, value_weight_grad)
```

```python
import math

import jax
import jax.numpy as jnp
from jax import lax
from jax.experimental import pallas as pl
from jax.experimental.pallas import tpu as pltpu
from jax.sharding import PartitionSpec as P

HD = 128
BLOCK = 128
DEPTH = 8
THETA = 1000000.0
NEGATIVE = -1e30
HIGHEST = lax.Precision.HIGHEST
BF = jnp.bfloat16
F32 = jnp.float32
SCALE = 1.0 / math.sqrt(HD)
STACK = DEPTH - 1
SLOTS = STACK + 4
OFFSETS = (0, 3, 1, 2)
VMEM_LIMIT = 56 * 1024 * 1024


def tree_tables(parents, block_total, depth_slots):
    indices = jnp.arange(block_total, dtype=jnp.int32)
    parent_link = (parents[:, None] == indices[None, :]).astype(F32)
    closure = jnp.eye(block_total, dtype=F32) + parent_link
    for repeat in range(depth_slots.bit_length()):
        closure = jnp.minimum(
            jnp.dot(closure, closure, precision=HIGHEST, preferred_element_type=F32), 1.0
        )
    closure_int = closure.astype(jnp.int32)
    depths = jnp.sum(closure_int, axis=1) - 1
    levels = jnp.arange(depth_slots, dtype=jnp.int32)
    select = closure_int[:, :, None] * (depths[None, :, None] == levels[None, None, :]).astype(
        jnp.int32
    )
    path_ids = jnp.sum(select * indices[None, :, None], axis=1) + jnp.sum(select, axis=1) - 1
    return (depths, path_ids)


def side(delta):
    return jnp.where(delta == 0, 0, jnp.where(delta == 3, 1, jnp.where(delta == 1, 2, 3)))


def device_tables(parents, y, x, core):
    block_total = parents.shape[0]
    depth_all, path_all = tree_tables(parents, block_total, DEPTH)
    first = 16 * y + 4 * x
    rows = jnp.where(
        jnp.arange(block_total)[None, :] == (first + (2 * core + jnp.arange(4)) % 4)[:, None], 1, 0
    )
    depths = jnp.sum(rows * depth_all[None, :], axis=1)
    paths = jnp.sum(rows[:, :, None] * path_all[None, :, :], axis=1)
    lead = jnp.where(core == 0, 0, 2)
    lead_row = jnp.where(jnp.arange(4) == lead, 1, 0)
    lead_depth = jnp.sum(lead_row * depths)
    lead_path = jnp.sum(lead_row[:, None] * paths, axis=0)[:STACK]
    level = jnp.arange(STACK, dtype=jnp.int32)
    block = jnp.clip(lead_path, 0, block_total - 1)
    column = side((block // 4 - x) % 4)
    line = side((block // 16 - y) % 4)
    same = (block // 2) % 2 == core
    parity = block % 2
    outer = jnp.where(same, line, column)
    inner = jnp.where(same, column, line)
    piece = jnp.where(same, 0, 5) + jnp.where(outer < 3, outer, 3 + parity)
    piece = jnp.where(level < lead_depth, piece, -1)
    place = jnp.where(outer < 3, inner * 2 + parity, inner)
    step = jnp.arange(DEPTH, dtype=jnp.int32)[None, :]
    local = jnp.arange(4, dtype=jnp.int32)[:, None]
    slots = jnp.where(paths >= first, STACK + (paths - first - 2 * core) % 4, step)
    slots = jnp.where(step <= depths[:, None], slots, STACK + local)
    offset = jnp.arange(4, dtype=jnp.int32)
    delta = jnp.where(offset == 0, 0, jnp.where(offset == 1, 3, jnp.where(offset == 2, 1, 2)))
    ids = (
        ((y + delta) % 4 * 16)[None, :, None]
        + ((x + delta) % 4 * 4)[:, None, None]
        + ((2 * core + offset) % 4)[None, None, :]
    )
    hits = (ids[..., None] == lead_path) & (level < lead_depth)
    dense = jnp.sum(jnp.where(hits, level - SLOTS, 0), axis=-1) + SLOTS
    home = (offset[:, None, None] == 0) & (offset[None, :, None] == 0)
    dense = jnp.where(home, STACK + offset[None, None, :], dense)
    table = jnp.concatenate(
        [
            piece,
            place,
            depths,
            slots.reshape(-1),
            dense.reshape(-1),
            jnp.stack([core, jnp.zeros_like(core)]),
        ]
    ).astype(jnp.int32)
    return depths, table


AT_PLACE = STACK
AT_DEPTH = 2 * STACK
AT_SLOT = AT_DEPTH + 4
AT_DENSE = AT_SLOT + 4 * DEPTH
AT_CORE = AT_DENSE + 64


def rope_tables(depths):
    offset = jnp.arange(BLOCK, dtype=jnp.int32)
    position = (depths[:, None] * BLOCK + offset[None, :]).astype(F32)
    frequency = jnp.exp(jnp.arange(HD // 2, dtype=F32) * (-2.0 * math.log(THETA) / HD))
    angles = (position[:, :, None] * frequency[None, None, :]).reshape(4 * BLOCK, HD // 2)
    cosine, sine = jnp.cos(angles), jnp.sin(angles)
    return (
        jnp.concatenate([cosine, cosine], axis=-1),
        jnp.concatenate([-sine, sine], axis=-1),
    )


def nn(a, b):
    return jnp.dot(a, b, preferred_element_type=F32)


def nt(a, b):
    return lax.dot_general(a, b, (((1,), (1,)), ((), ())), preferred_element_type=F32)


def tn(a, b):
    return lax.dot_general(a, b, (((0,), (0,)), ((), ())), preferred_element_type=F32)


def params():
    return pltpu.CompilerParams(vmem_limit_bytes=VMEM_LIMIT)


def project_near(place, own, left, right, key_weight, value_weight):
    rows, width = own.shape
    cols = key_weight.shape[1]

    def body(place_ref, a, b, c, ka, kb, kc, va, vb, vc, key_out, value_out):
        key_out[...] = nn(a[...], ka[...]) + nn(b[...], kb[...]) + nn(c[...], kc[...])
        value_out[...] = nn(a[...], va[...]) + nn(b[...], vb[...]) + nn(c[...], vc[...])

    whole = pl.BlockSpec((rows, width), lambda i, p: (0, 0))
    weights = [pl.BlockSpec((width, cols), lambda i, p, k=k: (p[k], 0)) for k in range(3)]
    out = pl.BlockSpec((rows, cols), lambda i, p: (0, 0))
    return pl.pallas_call(
        body,
        grid_spec=pltpu.PrefetchScalarGridSpec(
            num_scalar_prefetch=1,
            grid=(1,),
            in_specs=[whole] * 3 + weights + weights,
            out_specs=[out, out],
        ),
        out_shape=[jax.ShapeDtypeStruct((rows, cols), F32)] * 2,
        compiler_params=params(),
        name="project_near",
    )(place, own, left, right, *([key_weight] * 3), *([value_weight] * 3))


def project_far(place, top, bottom, key_weight, value_weight, key_sum, value_sum, cosine, sine):
    rows, cols = key_sum.shape
    width = top.shape[1]
    half = rows // 2

    def body(p, a, b, kw, vw, ks, vs, cs, sn, keep, send):
        far = jnp.concatenate([a[...], b[...]], axis=0)
        key = ks[...] + nn(far, kw[...])
        value = vs[...] + nn(far, vw[...])
        heads = []
        for h in range(2):
            part = key[:, h * HD : (h + 1) * HD]
            turned = part * cs[...] + pltpu.roll(part, HD // 2, 1) * sn[...]
            heads.append(
                jnp.concatenate([turned, value[:, h * HD : (h + 1) * HD]], axis=1).astype(BF)
            )
        swap = p[4] == 1
        keep[...] = jnp.where(swap, heads[1], heads[0])
        send[...] = jnp.where(swap, heads[0], heads[1])

    weight = pl.BlockSpec((width, cols), lambda i, p: (p[3], 0))
    part = pl.BlockSpec((half, width), lambda i, p: (0, 0))
    sums = pl.BlockSpec((rows, cols), lambda i, p: (0, 0))
    angle = pl.BlockSpec((rows, HD), lambda i, p: (0, 0))
    return pl.pallas_call(
        body,
        grid_spec=pltpu.PrefetchScalarGridSpec(
            num_scalar_prefetch=1,
            grid=(1,),
            in_specs=[part, part, weight, weight, sums, sums, angle, angle],
            out_specs=[sums, sums],
        ),
        out_shape=[jax.ShapeDtypeStruct((rows, cols), BF)] * 2,
        compiler_params=params(),
        name="project_far",
    )(place, top, bottom, key_weight, value_weight, key_sum, value_sum, cosine, sine)


def attend(table, queries, query_peer, upstream, upstream_peer, pieces):
    groups = queries.shape[1] // (2 * HD)
    width = groups * HD
    lanes = groups * BLOCK

    def body(t, q_own, q_far, u_own, u_far, *refs):
        parts = refs[:10]
        (out, q_grad, k_home, k_back, k_next, k_far0, k_far1, v_home, v_back, v_next, v_far0,
         v_far1, kv, total, sems) = refs[10:]
        step = pl.program_id(0)

        @pl.when(step == 0)
        def _():
            for s in range(STACK):
                for index in range(10):

                    @pl.when(t[s] == index)
                    def _(s=s, index=index):
                        pltpu.make_async_copy(
                            parts[index].at[t[AT_PLACE + s]], kv.at[s], sems.at[s]
                        ).start()

            for r in range(4):
                pltpu.make_async_copy(
                    parts[0 if r < 2 else 5].at[r % 2], kv.at[STACK + r], sems.at[STACK + r]
                ).start()
            total[...] = jnp.zeros(total.shape, F32)
            for s in range(STACK):

                @pl.when(t[s] >= 0)
                def _(s=s):
                    pltpu.make_async_copy(parts[0].at[0], kv.at[s], sems.at[s]).wait()

            for r in range(4):
                pltpu.make_async_copy(
                    parts[0 if r < 2 else 5].at[r % 2], kv.at[STACK + r], sems.at[STACK + r]
                ).wait()

        own = step < 2
        q = jnp.where(own, q_own[...], q_far[...])
        u = jnp.where(own, u_own[...], u_far[...])
        q = jnp.concatenate([q[:, h * HD : (h + 1) * HD] for h in range(groups)], axis=0)
        u = jnp.concatenate([u[:, h * HD : (h + 1) * HD] for h in range(groups)], axis=0)
        depth = t[AT_DEPTH + step]
        slots = [t[AT_SLOT + step * DEPTH + d] for d in range(DEPTH)]
        keys = jnp.concatenate([kv[s, :, :HD] for s in slots], axis=0)
        values = jnp.concatenate([kv[s, :, HD:] for s in slots], axis=0)
        ahead = lax.broadcasted_iota(jnp.int32, (BLOCK, lanes), 0) - (
            lax.broadcasted_iota(jnp.int32, (BLOCK, lanes), 1) % BLOCK
        )
        raw = nt(keys, q)
        scores = []
        peak = None
        for d in range(DEPTH):
            reach = jnp.where(d < depth, BLOCK, jnp.where(d == depth, 0, -BLOCK))
            tile = jnp.where(
                ahead <= reach, raw[d * BLOCK : (d + 1) * BLOCK] * SCALE, NEGATIVE
            )
            scores.append(tile)
            top = jnp.max(tile, axis=0, keepdims=True)
            peak = top if peak is None else jnp.maximum(peak, top)
        weights = [jnp.exp(tile - peak) for tile in scores]
        mass = None
        for w in weights:
            part = jnp.sum(w, axis=0, keepdims=True)
            mass = part if mass is None else mass + part
        rounded = jnp.concatenate([w.astype(BF) for w in weights], axis=0)
        mixed = (tn(values, rounded) / mass).astype(BF).astype(F32)
        delta = jnp.sum(u.astype(F32).T * mixed, axis=0, keepdims=True)
        for h in range(groups):
            out[:, h * HD : (h + 1) * HD] = mixed[:, h * BLOCK : (h + 1) * BLOCK].T.astype(BF)
        inverse = 1.0 / mass
        slopes = nt(values, u)
        chances = []
        pulls = []
        for d in range(DEPTH):
            p = weights[d] * inverse
            chances.append(p.astype(BF))
            pulls.append((p * (slopes[d * BLOCK : (d + 1) * BLOCK] - delta)).astype(BF))
        chances = jnp.concatenate(chances, axis=0)
        pulls = jnp.concatenate(pulls, axis=0)
        turned = tn(keys, pulls) * SCALE
        for h in range(groups):
            q_grad[:, h * HD : (h + 1) * HD] = turned[:, h * BLOCK : (h + 1) * BLOCK].T.astype(BF)
        v_part = nn(chances, u)
        k_part = nn(pulls, q) * SCALE
        for d in range(DEPTH):
            low = d * BLOCK
            total[slots[d], :, :HD] += k_part[low : low + BLOCK]
            total[slots[d], :, HD:] += v_part[low : low + BLOCK]

        @pl.when(step == 3)
        def _():
            for dx in range(4):
                for dy in range(4):
                    for r in range(4):
                        s = t[AT_DENSE + (dx * 4 + dy) * 4 + r]
                        k = total[s, :, :HD]
                        v = total[s, :, HD:]
                        if dx < 3:
                            (k_home, k_back, k_next)[dx][dy, r] = k
                        else:
                            (k_far0, k_far1)[r // 2][dy, r % 2] = k.astype(BF)
                        if dy < 3:
                            (v_home, v_back, v_next)[dy][dx, r] = v
                        else:
                            (v_far0, v_far1)[r // 2][dx, r % 2] = v.astype(BF)

    mine = pl.BlockSpec((BLOCK, width), lambda i, t: (jnp.minimum(i, 1), t[AT_CORE]))
    peer = pl.BlockSpec((BLOCK, width), lambda i, t: (jnp.maximum(i - 2, 0), 0))
    rows = pl.BlockSpec((BLOCK, width), lambda i, t: (i, 0))

    def full(shape):
        return pl.BlockSpec(shape, lambda i, t: (0,) * len(shape))

    wide = (4, 4, BLOCK, HD)
    half = (4, 2, BLOCK, HD)
    grads = [(wide, F32)] * 3 + [(half, BF)] * 2
    return pl.pallas_call(
        body,
        grid_spec=pltpu.PrefetchScalarGridSpec(
            num_scalar_prefetch=1,
            grid=(4,),
            in_specs=[mine, peer, mine, peer] + [pl.BlockSpec(memory_space=pl.ANY)] * 10,
            out_specs=[rows, rows] + [full(s) for s, _ in grads + grads],
            scratch_shapes=[
                pltpu.VMEM((SLOTS, BLOCK, 2 * HD), BF),
                pltpu.VMEM((SLOTS + 1, BLOCK, 2 * HD), F32),
                pltpu.SemaphoreType.DMA((SLOTS,)),
            ],
        ),
        out_shape=[jax.ShapeDtypeStruct((4 * BLOCK, width), BF)] * 2
        + [jax.ShapeDtypeStruct(s, d) for s, d in grads + grads],
        compiler_params=params(),
        name="attend",
    )(table, queries, query_peer, upstream, upstream_peer, *pieces)


def input_partials(place, mine, other, key_weight, value_weight):
    rows = mine.shape[0]
    cols = key_weight.shape[1]
    width = key_weight.shape[0] // 4

    def body(p, a, b, kw, vw, *outs):
        swap = p[4] == 1
        first = jnp.where(swap, b[...], a[...])
        second = jnp.where(swap, a[...], b[...])
        key = jnp.concatenate([first[:, :HD], second[:, :HD]], axis=1)
        value = jnp.concatenate([first[:, HD:], second[:, HD:]], axis=1)
        result = (nt(key, kw[...]) + nt(value, vw[...])).astype(BF)
        for k in range(4):

            @pl.when(pl.program_id(0) == k)
            def _(k=k):
                outs[k][...] = result

    grads = pl.BlockSpec((rows, 2 * HD), lambda i, p: (0, 0))
    weight = pl.BlockSpec((width, cols), lambda i, p: (p[5 + i], 0))
    out = pl.BlockSpec((rows, width), lambda i, p: (0, 0))
    return pl.pallas_call(
        body,
        grid_spec=pltpu.PrefetchScalarGridSpec(
            num_scalar_prefetch=1,
            grid=(4,),
            in_specs=[grads, grads, weight, weight],
            out_specs=[out] * 4,
        ),
        out_shape=[jax.ShapeDtypeStruct((rows, width), BF)] * 4,
        compiler_params=params(),
        name="input_partials",
    )(place, mine, other, key_weight, value_weight)


def weight_partials(place, grads, own, peer):
    width = own[0].shape[1]
    share = width // 8

    def body(p, g, a0, a1, a2, a3, a4, b0, b1, b2, b3, b4, k_home, k_back, k_next, k_far0, k_far1,
             v_home, v_back, v_next, v_far0, v_far1, result):
        core = p[4]
        grad = g[...]
        for dy in range(4):
            pick = p[9 + dy]
            for k in range(4):

                @pl.when(pick == k)
                def _(k=k):
                    if k < 3:
                        top, low = (a0, a1, a2)[k][...], (b0, b1, b2)[k][...]
                    else:
                        top = jnp.concatenate([a3[...], a4[...]], axis=0)
                        low = jnp.concatenate([b3[...], b4[...]], axis=0)
                    result[...] = tn(jnp.concatenate([top, low], axis=0), grad)

            for dx in range(4):
                base = p[13 + dx] * (2 * share)
                for r in range(2):
                    start = pl.multiple_of(base + ((core + r) % 2) * share, 16)
                    value = result[pl.ds(start, share), :]
                    k, v = value[:, :HD], value[:, HD:]
                    if dx < 3:
                        (k_home, k_back, k_next)[dx][dy, r] = k
                    else:
                        (k_far0, k_far1)[r][dy, 0] = k.astype(BF)
                    if dy < 3:
                        (v_home, v_back, v_next)[dy][dx, r] = v
                    else:
                        (v_far0, v_far1)[r][dx, 0] = v.astype(BF)

    wide = (4, 2, share, HD)
    half = (4, 1, share, HD)
    shapes = [(wide, F32)] * 3 + [(half, BF)] * 2
    return pl.pallas_call(
        body,
        in_specs=[pl.BlockSpec(memory_space=pltpu.SMEM)]
        + [pl.BlockSpec(memory_space=pltpu.VMEM)] * 11,
        out_specs=[pl.BlockSpec(memory_space=pltpu.VMEM)] * 10,
        out_shape=[jax.ShapeDtypeStruct(s, d) for s, d in shapes + shapes],
        scratch_shapes=[pltpu.VMEM((width, 2 * HD), F32)],
        compiler_params=params(),
        name="weight_partials",
    )(place, grads, *own, *peer)


def mover(axis, pairs):
    return lambda value: lax.ppermute(value, axis, pairs)


def ring_gather(value, ahead, behind):
    back = ahead(value)
    forth = behind(value)
    far0 = ahead(back[:, :1])
    far1 = behind(forth[:, 1:])
    return back, forth, far0, far1


def ring_reduce(home, back, forth, far0, far1, ahead, behind, kind):
    half = far0.shape[1]
    in0 = ahead(far0)
    in1 = behind(far1)
    to_next = jnp.concatenate(
        [(forth[:, :half] + in0.astype(F32)).astype(kind), forth[:, half:].astype(kind)], axis=1
    )
    to_back = jnp.concatenate(
        [back[:, :half].astype(kind), (back[:, half:] + in1.astype(F32)).astype(kind)], axis=1
    )
    from_back = ahead(to_next)
    from_next = behind(to_back)
    return home + from_back.astype(F32) + from_next.astype(F32)


def reduce_second(value, ahead, behind):
    half = value.shape[1] // 2
    far = value[3:4]
    return ring_reduce(
        value[0:1], value[1:2], value[2:3], far[:, :half], far[:, half:], ahead, behind, F32
    )[0]


def shards(hidden, queries, key_weight, value_weight, parents, upstream):
    place_ctx = lax.axis_index("ctx")
    tp = lax.axis_index("tp")
    core = place_ctx % 2
    x = (place_ctx // 2) % 4
    y = place_ctx // 8
    xn = mover("ctx", [(i, i // 8 * 8 + (i + 2) % 8) for i in range(32)])
    xb = mover("ctx", [(i, i // 8 * 8 + (i - 2) % 8) for i in range(32)])
    yn = mover("ctx", [(i, (i + 8) % 32) for i in range(32)])
    yb = mover("ctx", [(i, (i - 8) % 32) for i in range(32)])
    swap = mover("ctx", [(i, i ^ 1) for i in range(32)])
    zn = mover("tp", [(i, (i + 1) % 4) for i in range(4)])
    zb = mover("tp", [(i, (i - 1) % 4) for i in range(4)])
    z2 = mover("tp", [(i, (i + 2) % 4) for i in range(4)])

    local_rows = hidden.shape[0]
    half_rows = local_rows // 2
    depths, table = device_tables(parents, y, x, core)
    cosine, sine = rope_tables(depths)
    pick = [(y + o - tp) % 4 for o in OFFSETS]
    place = jnp.stack(
        [tp, (tp + 3) % 4, (tp + 1) % 4, (tp + 2) % 4, core]
        + [(tp + o) % 4 for o in OFFSETS]
        + [side(d) for d in pick]
        + [(x + o) % 4 for o in OFFSETS]
    ).astype(jnp.int32)

    left = zn(hidden)
    right = zb(hidden)
    far_top = zn(left[:half_rows])
    far_low = zb(right[half_rows:])
    key_sum, value_sum = project_near(place, hidden, left, right, key_weight, value_weight)
    keep, send = project_far(
        place, far_top, far_low, key_weight, value_weight, key_sum, value_sum, cosine, sine
    )
    width = queries.shape[1] // 2
    query_peer = swap(lax.dynamic_slice_in_dim(queries, (1 - core) * width, width, 1))
    upstream_peer = swap(lax.dynamic_slice_in_dim(upstream, (1 - core) * width, width, 1))

    mine = keep.reshape(1, 2, BLOCK, 2 * HD)
    other = swap(send).reshape(1, 2, BLOCK, 2 * HD)
    back, forth, far0, far1 = ring_gather(mine, xn, xb)
    mine_line = jnp.concatenate([mine, back, forth, jnp.concatenate([far0, far1], axis=1)], axis=0)
    back, forth, far0, far1 = ring_gather(other, yn, yb)
    other_line = jnp.concatenate(
        [other, back, forth, jnp.concatenate([far0, far1], axis=1)], axis=0
    )
    pieces = [mine_line, *ring_gather(mine_line, yn, yb)]
    pieces += [other_line, *ring_gather(other_line, xn, xb)]
    pieces = [p.reshape(-1, BLOCK, 2 * HD) for p in pieces]

    own_features = [hidden, left, right, far_top, far_low]
    peer_features = [swap(f) for f in own_features]

    out, q_grad, *slot_grads = attend(
        table, queries, query_peer, upstream, upstream_peer, pieces
    )
    out_other = swap(out[local_rows:])
    q_grad_other = swap(q_grad[local_rows:])

    def assemble(a, b):
        first = jnp.where(core == 0, a, b)
        second = jnp.where(core == 0, b, a)
        return jnp.concatenate([first, second], axis=1)

    attention = assemble(out[:local_rows], out_other)
    query_grad = assemble(q_grad[:local_rows], q_grad_other)

    key_total = reduce_second(ring_reduce(*slot_grads[:5], xn, xb, BF), yn, yb)
    value_total = reduce_second(ring_reduce(*slot_grads[5:], yn, yb, BF), xn, xb)
    key_total = key_total.reshape(4 * BLOCK, HD)
    swapped = jnp.concatenate([key_total[:, HD // 2 :], key_total[:, : HD // 2]], axis=1)
    key_back = (key_total * cosine - swapped * sine).astype(BF)
    grads = jnp.concatenate([key_back, value_total.reshape(4 * BLOCK, HD).astype(BF)], axis=1)
    grads_mine = grads[:local_rows]
    grads_other = swap(grads[local_rows:])

    parts = input_partials(place, grads_mine, grads_other, key_weight, value_weight)
    from_back = zn(parts[2])
    from_next = zb(parts[1])
    from_far = z2(parts[3])
    hidden_grad = (
        parts[0].astype(F32)
        + from_back.astype(F32)
        + from_next.astype(F32)
        + from_far.astype(F32)
    ).astype(BF)

    w_parts = weight_partials(place, grads, own_features, peer_features)
    key_w = reduce_second(ring_reduce(*w_parts[:5], xn, xb, BF), yn, yb)
    value_w = reduce_second(ring_reduce(*w_parts[5:], yn, yb, BF), xn, xb)
    both = jnp.concatenate([key_w, value_w], axis=-1)
    both_other = swap(both[1])
    key_weight_grad = assemble(both[0, :, :HD], both_other[:, :HD])
    value_weight_grad = assemble(both[0, :, HD:], both_other[:, HD:])
    return (attention, query_grad, hidden_grad, key_weight_grad, value_weight_grad)


def solution(mesh):
    return jax.shard_map(
        shards,
        mesh=mesh,
        in_specs=(
            P("ctx", "tp"),
            P("ctx", "tp"),
            P(None, "tp"),
            P(None, "tp"),
            P(),
            P("ctx", "tp"),
        ),
        out_specs=(P("ctx", "tp"), P("ctx", "tp"), P("ctx", "tp"), P("ctx", "tp"), P("ctx", "tp")),
        check_vma=False,
    )
```

```python
import math

import jax
import jax.numpy as jnp
from jax import lax
from jax.experimental import pallas as pl
from jax.experimental.pallas import tpu as pltpu
from jax.sharding import PartitionSpec as P

HD = 128
BLOCK = 128
DEPTH = 8
THETA = 1000000.0
NEGATIVE = -1e30
HIGHEST = lax.Precision.HIGHEST
BF = jnp.bfloat16
F32 = jnp.float32
SCALE = 1.0 / math.sqrt(HD)
STACK = DEPTH - 1
SLOTS = STACK + 4
OFFSETS = (0, 3, 1, 2)
VMEM_LIMIT = 56 * 1024 * 1024


def tree_tables(parents, block_total, depth_slots):
    indices = jnp.arange(block_total, dtype=jnp.int32)
    parent_link = (parents[:, None] == indices[None, :]).astype(F32)
    closure = jnp.eye(block_total, dtype=F32) + parent_link
    for repeat in range(depth_slots.bit_length()):
        closure = jnp.minimum(
            jnp.dot(closure, closure, precision=HIGHEST, preferred_element_type=F32), 1.0
        )
    closure_int = closure.astype(jnp.int32)
    depths = jnp.sum(closure_int, axis=1) - 1
    levels = jnp.arange(depth_slots, dtype=jnp.int32)
    select = closure_int[:, :, None] * (depths[None, :, None] == levels[None, None, :]).astype(
        jnp.int32
    )
    path_ids = jnp.sum(select * indices[None, :, None], axis=1) + jnp.sum(select, axis=1) - 1
    return (depths, path_ids)


def side(delta):
    return jnp.where(delta == 0, 0, jnp.where(delta == 3, 1, jnp.where(delta == 1, 2, 3)))


def device_tables(parents, y, x, core):
    block_total = parents.shape[0]
    depth_all, path_all = tree_tables(parents, block_total, DEPTH)
    first = 16 * y + 4 * x
    rows = jnp.where(
        jnp.arange(block_total)[None, :] == (first + (2 * core + jnp.arange(4)) % 4)[:, None], 1, 0
    )
    depths = jnp.sum(rows * depth_all[None, :], axis=1)
    paths = jnp.sum(rows[:, :, None] * path_all[None, :, :], axis=1)
    lead = jnp.where(core == 0, 0, 2)
    lead_row = jnp.where(jnp.arange(4) == lead, 1, 0)
    lead_depth = jnp.sum(lead_row * depths)
    lead_path = jnp.sum(lead_row[:, None] * paths, axis=0)[:STACK]
    level = jnp.arange(STACK, dtype=jnp.int32)
    block = jnp.clip(lead_path, 0, block_total - 1)
    column = side((block // 4 - x) % 4)
    line = side((block // 16 - y) % 4)
    same = (block // 2) % 2 == core
    parity = block % 2
    outer = jnp.where(same, line, column)
    inner = jnp.where(same, column, line)
    piece = jnp.where(same, 0, 5) + jnp.where(outer < 3, outer, 3 + parity)
    piece = jnp.where(level < lead_depth, piece, -1)
    place = jnp.where(outer < 3, inner * 2 + parity, inner)
    step = jnp.arange(DEPTH, dtype=jnp.int32)[None, :]
    local = jnp.arange(4, dtype=jnp.int32)[:, None]
    slots = jnp.where(paths >= first, STACK + (paths - first - 2 * core) % 4, step)
    slots = jnp.where(step <= depths[:, None], slots, STACK + local)
    offset = jnp.arange(4, dtype=jnp.int32)
    delta = jnp.where(offset == 0, 0, jnp.where(offset == 1, 3, jnp.where(offset == 2, 1, 2)))
    ids = (
        ((y + delta) % 4 * 16)[None, :, None]
        + ((x + delta) % 4 * 4)[:, None, None]
        + ((2 * core + offset) % 4)[None, None, :]
    )
    hits = (ids[..., None] == lead_path) & (level < lead_depth)
    dense = jnp.sum(jnp.where(hits, level - SLOTS, 0), axis=-1) + SLOTS
    home = (offset[:, None, None] == 0) & (offset[None, :, None] == 0)
    dense = jnp.where(home, STACK + offset[None, None, :], dense)
    table = jnp.concatenate(
        [
            piece,
            place,
            depths,
            slots.reshape(-1),
            dense.reshape(-1),
            jnp.stack([core, jnp.zeros_like(core)]),
        ]
    ).astype(jnp.int32)
    return depths, table


AT_PLACE = STACK
AT_DEPTH = 2 * STACK
AT_SLOT = AT_DEPTH + 4
AT_DENSE = AT_SLOT + 4 * DEPTH
AT_CORE = AT_DENSE + 64


def rope_tables(depths):
    offset = jnp.arange(BLOCK, dtype=jnp.int32)
    position = (depths[:, None] * BLOCK + offset[None, :]).astype(F32)
    frequency = jnp.exp(jnp.arange(HD // 2, dtype=F32) * (-2.0 * math.log(THETA) / HD))
    angles = (position[:, :, None] * frequency[None, None, :]).reshape(4 * BLOCK, HD // 2)
    cosine, sine = jnp.cos(angles), jnp.sin(angles)
    return (
        jnp.concatenate([cosine, cosine], axis=-1),
        jnp.concatenate([-sine, sine], axis=-1),
    )


def nn(a, b):
    return jnp.dot(a, b, preferred_element_type=F32)


def nt(a, b):
    return lax.dot_general(a, b, (((1,), (1,)), ((), ())), preferred_element_type=F32)


def tn(a, b):
    return lax.dot_general(a, b, (((0,), (0,)), ((), ())), preferred_element_type=F32)


def params():
    return pltpu.CompilerParams(vmem_limit_bytes=VMEM_LIMIT)


def project_near(place, own, left, right, key_weight, value_weight):
    rows, width = own.shape
    cols = key_weight.shape[1]

    def body(place_ref, a, b, c, ka, kb, kc, va, vb, vc, key_out, value_out):
        key_out[...] = nn(a[...], ka[...]) + nn(b[...], kb[...]) + nn(c[...], kc[...])
        value_out[...] = nn(a[...], va[...]) + nn(b[...], vb[...]) + nn(c[...], vc[...])

    whole = pl.BlockSpec((rows, width), lambda i, p: (0, 0))
    weights = [pl.BlockSpec((width, cols), lambda i, p, k=k: (p[k], 0)) for k in range(3)]
    out = pl.BlockSpec((rows, cols), lambda i, p: (0, 0))
    return pl.pallas_call(
        body,
        grid_spec=pltpu.PrefetchScalarGridSpec(
            num_scalar_prefetch=1,
            grid=(1,),
            in_specs=[whole] * 3 + weights + weights,
            out_specs=[out, out],
        ),
        out_shape=[jax.ShapeDtypeStruct((rows, cols), F32)] * 2,
        compiler_params=params(),
        name="project_near",
    )(place, own, left, right, *([key_weight] * 3), *([value_weight] * 3))


def project_far(place, top, bottom, key_weight, value_weight, key_sum, value_sum, cosine, sine):
    rows, cols = key_sum.shape
    width = top.shape[1]
    half = rows // 2

    def body(p, a, b, kw, vw, ks, vs, cs, sn, keep, send):
        far = jnp.concatenate([a[...], b[...]], axis=0)
        key = ks[...] + nn(far, kw[...])
        value = vs[...] + nn(far, vw[...])
        heads = []
        for h in range(2):
            part = key[:, h * HD : (h + 1) * HD]
            turned = part * cs[...] + pltpu.roll(part, HD // 2, 1) * sn[...]
            heads.append(
                jnp.concatenate([turned, value[:, h * HD : (h + 1) * HD]], axis=1).astype(BF)
            )
        swap = p[4] == 1
        keep[...] = jnp.where(swap, heads[1], heads[0])
        send[...] = jnp.where(swap, heads[0], heads[1])

    weight = pl.BlockSpec((width, cols), lambda i, p: (p[3], 0))
    part = pl.BlockSpec((half, width), lambda i, p: (0, 0))
    sums = pl.BlockSpec((rows, cols), lambda i, p: (0, 0))
    angle = pl.BlockSpec((rows, HD), lambda i, p: (0, 0))
    return pl.pallas_call(
        body,
        grid_spec=pltpu.PrefetchScalarGridSpec(
            num_scalar_prefetch=1,
            grid=(1,),
            in_specs=[part, part, weight, weight, sums, sums, angle, angle],
            out_specs=[sums, sums],
        ),
        out_shape=[jax.ShapeDtypeStruct((rows, cols), BF)] * 2,
        compiler_params=params(),
        name="project_far",
    )(place, top, bottom, key_weight, value_weight, key_sum, value_sum, cosine, sine)


def attend(table, queries, query_peer, upstream, upstream_peer, pieces):
    groups = queries.shape[1] // (2 * HD)
    width = groups * HD
    lanes = groups * BLOCK
    pair = 2 * BLOCK

    def body(t, q_own, q_far, u_own, u_far, *refs):
        parts = refs[:10]
        k_outs = refs[11:15]
        v_outs = refs[15:19]
        out = refs[10]
        kv, total, scores, mixed_sum, turned_sum, q_rows, u_rows = refs[19:]
        step = pl.program_id(0)

        @pl.when(step == 0)
        def _():
            for s in range(STACK):
                for index in range(10):

                    @pl.when(t[s] == index)
                    def _(s=s, index=index):
                        kv[s] = parts[index][t[AT_PLACE + s]]

            for r in range(4):
                kv[STACK + r] = parts[0 if r < 2 else 5][r % 2]
            total[...] = jnp.zeros(total.shape, F32)

        own = step < 2
        q = jnp.where(own, q_own[...], q_far[...])
        u = jnp.where(own, u_own[...], u_far[...])
        for h in range(groups):
            q_rows[h * BLOCK : (h + 1) * BLOCK] = q[:, h * HD : (h + 1) * HD]
            u_rows[h * BLOCK : (h + 1) * BLOCK] = u[:, h * HD : (h + 1) * HD]
        depth = t[AT_DEPTH + step]
        ahead = lax.broadcasted_iota(jnp.int32, (BLOCK, lanes), 0) - (
            lax.broadcasted_iota(jnp.int32, (BLOCK, lanes), 1) % BLOCK
        )

        def slots_of(c):
            return [t[AT_SLOT + step * DEPTH + 2 * c + e] for e in range(2)]

        def rows_of(slots, low):
            return jnp.concatenate([kv[s, :, low : low + HD] for s in slots], axis=0)

        def score(c, peak):
            raw = nt(rows_of(slots_of(c), 0), q_rows[...])
            for e in range(2):
                d = 2 * c + e
                reach = jnp.where(d < depth, BLOCK, jnp.where(d == depth, 0, -BLOCK))
                tile = jnp.where(
                    ahead <= reach, raw[e * BLOCK : (e + 1) * BLOCK] * SCALE, NEGATIVE
                )
                scores[pl.ds(pl.multiple_of(d * BLOCK, BLOCK), BLOCK)] = tile
                peak = jnp.maximum(peak, jnp.max(tile, axis=0, keepdims=True))
            return peak

        peak = lax.fori_loop(0, DEPTH // 2, score, jnp.full((1, lanes), NEGATIVE, F32))
        mixed_sum[...] = jnp.zeros(mixed_sum.shape, F32)
        turned_sum[...] = jnp.zeros(turned_sum.shape, F32)

        def weigh(c, mass):
            at = pl.ds(pl.multiple_of(c * pair, pair), pair)
            w = jnp.exp(scores[at] - peak)
            scores[at] = w
            mixed_sum[...] += tn(rows_of(slots_of(c), HD), w.astype(BF))
            return mass + jnp.sum(w, axis=0, keepdims=True)

        mass = lax.fori_loop(0, DEPTH // 2, weigh, jnp.zeros((1, lanes), F32))
        mixed = (mixed_sum[...] / mass).astype(BF).astype(F32)
        delta = jnp.sum(u_rows[...].astype(F32).T * mixed, axis=0, keepdims=True)
        for h in range(groups):
            out[:, h * HD : (h + 1) * HD] = mixed[:, h * BLOCK : (h + 1) * BLOCK].T.astype(BF)
        inverse = 1.0 / mass

        def pull(c, carry):
            at = pl.ds(pl.multiple_of(c * pair, pair), pair)
            slots = slots_of(c)
            p = scores[at] * inverse
            slopes = nt(rows_of(slots, HD), u_rows[...])
            pulls = (p * (slopes - delta)).astype(BF)
            turned_sum[...] += tn(rows_of(slots, 0), pulls)
            v_part = nn(p.astype(BF), u_rows[...])
            k_part = nn(pulls, q_rows[...]) * SCALE
            for e in range(2):
                low = e * BLOCK
                total[slots[e], :, :HD] += k_part[low : low + BLOCK]
                total[slots[e], :, HD:] += v_part[low : low + BLOCK]
            return carry

        lax.fori_loop(0, DEPTH // 2, pull, 0)
        turned = turned_sum[...] * SCALE
        for h in range(groups):
            out[:, width + h * HD : width + (h + 1) * HD] = (
                turned[:, h * BLOCK : (h + 1) * BLOCK].T.astype(BF)
            )

        @pl.when(step == 3)
        def _():
            for outer in range(4):

                def fill(i, carry, outer=outer):
                    k_slot = t[AT_DENSE + outer * 16 + i]
                    v_slot = t[AT_DENSE + (i // 4) * 16 + outer * 4 + i % 4]
                    k = total[k_slot, :, :HD]
                    v = total[v_slot, :, HD:]
                    k_outs[outer][i] = k.astype(k_outs[outer].dtype)
                    v_outs[outer][i] = v.astype(v_outs[outer].dtype)
                    return carry

                lax.fori_loop(0, 16, fill, 0)

    mine = pl.BlockSpec((BLOCK, width), lambda i, t: (jnp.minimum(i, 1), t[AT_CORE]))
    peer = pl.BlockSpec((BLOCK, width), lambda i, t: (jnp.maximum(i - 2, 0), 0))
    rows = pl.BlockSpec((BLOCK, 2 * width), lambda i, t: (i, 0))

    def full(shape):
        return pl.BlockSpec(
            shape, lambda i, t: (0,) * len(shape), pipeline_mode=pl.Buffered(1)
        )

    def held(shape):
        return pl.BlockSpec(shape, lambda i, t: (0,) * len(shape))

    wide = (16, BLOCK, HD)
    grads = [(wide, F32)] + [(wide, BF)] * 3
    return pl.pallas_call(
        body,
        grid_spec=pltpu.PrefetchScalarGridSpec(
            num_scalar_prefetch=1,
            grid=(4,),
            in_specs=[mine, peer, mine, peer] + [full(p.shape) for p in pieces],
            out_specs=[rows] + [held(s) for s, _ in grads + grads],
            scratch_shapes=[
                pltpu.VMEM((SLOTS, BLOCK, 2 * HD), BF),
                pltpu.VMEM((SLOTS + 1, BLOCK, 2 * HD), F32),
                pltpu.VMEM((DEPTH * BLOCK, lanes), F32),
                pltpu.VMEM((HD, lanes), F32),
                pltpu.VMEM((HD, lanes), F32),
                pltpu.VMEM((lanes, HD), BF),
                pltpu.VMEM((lanes, HD), BF),
            ],
        ),
        out_shape=[jax.ShapeDtypeStruct((4 * BLOCK, 2 * width), BF)]
        + [jax.ShapeDtypeStruct(s, d) for s, d in grads + grads],
        compiler_params=params(),
        name="attend",
    )(table, queries, query_peer, upstream, upstream_peer, *pieces)


def combine(sums):
    def body(*refs):
        for side_of in range(2):
            home, a, b, c = refs[4 * side_of : 4 * side_of + 4]
            outs = refs[8 + 4 * side_of : 12 + 4 * side_of]
            rows = outs[0].shape[0]
            for k in range(4):
                at = slice(k * rows, (k + 1) * rows)
                outs[k][...] = (
                    home[at] + a[at].astype(F32) + b[at].astype(F32) + c[at].astype(F32)
                )

    shape = sums[0].shape
    part = (shape[0] // 4,) + shape[1:]
    return pl.pallas_call(
        body,
        in_specs=[pl.BlockSpec(memory_space=pltpu.VMEM)] * 8,
        out_specs=[pl.BlockSpec(memory_space=pltpu.VMEM)] * 8,
        out_shape=[jax.ShapeDtypeStruct(part, F32)] * 8,
        compiler_params=params(),
        name="combine",
    )(*sums)


def finish_grads(sums, cosine, sine):
    rows = 4 * BLOCK

    def body(*refs):
        ks, vs = refs[:4], refs[4:8]
        cs, sn, every, away = refs[8:]
        key = (ks[0][...] + ks[1][...] + ks[2][...] + ks[3][...]).reshape(rows, HD)
        value = (vs[0][...] + vs[1][...] + vs[2][...] + vs[3][...]).reshape(rows, HD)
        key = key * cs[...] - pltpu.roll(key, HD // 2, 1) * sn[...]
        both = jnp.concatenate([key.astype(BF), value.astype(BF)], axis=1)
        every[...] = both
        away[...] = both[rows // 2 :]

    return pl.pallas_call(
        body,
        in_specs=[pl.BlockSpec(memory_space=pltpu.VMEM)] * 10,
        out_specs=[pl.BlockSpec(memory_space=pltpu.VMEM)] * 2,
        out_shape=[
            jax.ShapeDtypeStruct((rows, 2 * HD), BF),
            jax.ShapeDtypeStruct((rows // 2, 2 * HD), BF),
        ],
        compiler_params=params(),
        name="finish_grads",
    )(*sums, cosine, sine)


def finish_weights(sums):
    share = sums[0].shape[1]

    def body(*refs):
        ks, vs = refs[:4], refs[4:8]
        for row, out in enumerate(refs[8:]):
            out[:, :HD] = ks[0][row] + ks[1][row] + ks[2][row] + ks[3][row]
            out[:, HD:] = vs[0][row] + vs[1][row] + vs[2][row] + vs[3][row]

    return pl.pallas_call(
        body,
        in_specs=[pl.BlockSpec(memory_space=pltpu.VMEM)] * 8,
        out_specs=[pl.BlockSpec(memory_space=pltpu.VMEM)] * 2,
        out_shape=[jax.ShapeDtypeStruct((share, 2 * HD), F32)] * 2,
        compiler_params=params(),
        name="finish_weights",
    )(*sums)


def input_partials(place, mine, other, key_weight, value_weight):
    rows = other.shape[0]
    cols = key_weight.shape[1]
    width = key_weight.shape[0] // 4

    def body(p, a, b, kw, vw, *outs):
        swap = p[4] == 1
        first = jnp.where(swap, b[...], a[...])
        second = jnp.where(swap, a[...], b[...])
        key = jnp.concatenate([first[:, :HD], second[:, :HD]], axis=1)
        value = jnp.concatenate([first[:, HD:], second[:, HD:]], axis=1)
        result = (nt(key, kw[...]) + nt(value, vw[...])).astype(BF)
        for k in range(4):

            @pl.when(pl.program_id(0) == k)
            def _(k=k):
                outs[k][...] = result

    grads = pl.BlockSpec((rows, 2 * HD), lambda i, p: (0, 0))
    weight = pl.BlockSpec((width, cols), lambda i, p: (p[5 + i], 0))
    out = pl.BlockSpec((rows, width), lambda i, p: (0, 0))
    return pl.pallas_call(
        body,
        grid_spec=pltpu.PrefetchScalarGridSpec(
            num_scalar_prefetch=1,
            grid=(4,),
            in_specs=[grads, grads, weight, weight],
            out_specs=[out] * 4,
        ),
        out_shape=[jax.ShapeDtypeStruct((rows, width), BF)] * 4,
        compiler_params=params(),
        name="input_partials",
    )(place, mine, other, key_weight, value_weight)


def weight_partials(place, grads, own, peer):
    width = own[0].shape[1]
    share = width // 8

    def body(p, g, a0, a1, a2, a3, a4, b0, b1, b2, b3, b4, *refs):
        k_outs, v_outs, result = refs[:4], refs[4:8], refs[8]
        core = p[4]
        grad = g[...]
        half = a3.shape[0]
        for piece in range(4):
            if piece < 3:
                rows = [(a0, b0), (a1, b1), (a2, b2)][piece]
            else:
                rows = (a3, a4, b3, b4)
            features = jnp.concatenate([r[...] for r in rows], axis=0)
            result[...] = tn(features, grad)
            line = p[9 + piece]
            for dx in range(4):
                base = p[13 + dx] * (2 * share)
                for r in range(2):
                    start = pl.multiple_of(base + ((core + r) % 2) * share, 16)
                    value = result[pl.ds(start, share), :]
                    k_outs[dx][line * 2 + r] = value[:, :HD].astype(k_outs[dx].dtype)
                    for dy in range(4):

                        @pl.when(line == dy)
                        def _(dy=dy, dx=dx, r=r, value=value):
                            v_outs[dy][dx * 2 + r] = value[:, HD:].astype(v_outs[dy].dtype)

    wide = (8, share, HD)
    shapes = [(wide, F32)] + [(wide, BF)] * 3
    return pl.pallas_call(
        body,
        in_specs=[pl.BlockSpec(memory_space=pltpu.SMEM)]
        + [pl.BlockSpec(memory_space=pltpu.VMEM)] * 11,
        out_specs=[pl.BlockSpec(memory_space=pltpu.VMEM)] * 8,
        out_shape=[jax.ShapeDtypeStruct(s, d) for s, d in shapes + shapes],
        scratch_shapes=[pltpu.VMEM((width, 2 * HD), F32)],
        compiler_params=params(),
        name="weight_partials",
    )(place, grads, *own, *peer)


def mover(axis, pairs):
    return lambda value: lax.ppermute(value, axis, pairs)


def ring_gather(value, ahead, behind):
    back = ahead(value)
    forth = behind(value)
    far0 = ahead(back[:, :1])
    far1 = behind(forth[:, 1:])
    return back, forth, far0, far1


def send_all(values, ahead, behind, across):
    home, back, forth, far = values
    return [home, ahead(forth), behind(back), across(far)]


def shards(hidden, queries, key_weight, value_weight, parents, upstream):
    place_ctx = lax.axis_index("ctx")
    tp = lax.axis_index("tp")
    core = place_ctx % 2
    x = (place_ctx // 2) % 4
    y = place_ctx // 8
    xn = mover("ctx", [(i, i // 8 * 8 + (i + 2) % 8) for i in range(32)])
    xb = mover("ctx", [(i, i // 8 * 8 + (i - 2) % 8) for i in range(32)])
    yn = mover("ctx", [(i, (i + 8) % 32) for i in range(32)])
    yb = mover("ctx", [(i, (i - 8) % 32) for i in range(32)])
    swap = mover("ctx", [(i, i ^ 1) for i in range(32)])
    zn = mover("tp", [(i, (i + 1) % 4) for i in range(4)])
    zb = mover("tp", [(i, (i - 1) % 4) for i in range(4)])
    x2 = mover("ctx", [(i, i // 8 * 8 + (i + 4) % 8) for i in range(32)])
    y2 = mover("ctx", [(i, (i + 16) % 32) for i in range(32)])
    z2 = mover("tp", [(i, (i + 2) % 4) for i in range(4)])

    local_rows = hidden.shape[0]
    half_rows = local_rows // 2
    depths, table = device_tables(parents, y, x, core)
    cosine, sine = rope_tables(depths)
    pick = [(tp + o - y) % 4 for o in OFFSETS]
    place = jnp.stack(
        [tp, (tp + 3) % 4, (tp + 1) % 4, (tp + 2) % 4, core]
        + [(tp + o) % 4 for o in OFFSETS]
        + [side(d) for d in pick]
        + [(x + o) % 4 for o in OFFSETS]
    ).astype(jnp.int32)

    left = zn(hidden)
    right = zb(hidden)
    far_top = zn(left[:half_rows])
    far_low = zb(right[half_rows:])
    key_sum, value_sum = project_near(place, hidden, left, right, key_weight, value_weight)
    keep, send = project_far(
        place, far_top, far_low, key_weight, value_weight, key_sum, value_sum, cosine, sine
    )
    width = queries.shape[1] // 2
    query_peer = swap(lax.dynamic_slice_in_dim(queries, (1 - core) * width, width, 1))
    upstream_peer = swap(lax.dynamic_slice_in_dim(upstream, (1 - core) * width, width, 1))

    mine = keep.reshape(1, 2, BLOCK, 2 * HD)
    other = swap(send).reshape(1, 2, BLOCK, 2 * HD)
    mine_line = jnp.concatenate([mine, xn(mine), xb(mine), x2(mine)], axis=0)
    other_line = jnp.concatenate([other, yn(other), yb(other), y2(other)], axis=0)
    pieces = [mine_line, *ring_gather(mine_line, yn, yb)]
    pieces += [other_line, *ring_gather(other_line, xn, xb)]
    pieces = [p.reshape(-1, BLOCK, 2 * HD) for p in pieces]

    own_features = [hidden, left, right, far_top, far_low]
    peer_features = [swap(f) for f in own_features]
    pieces, peer_features = lax.optimization_barrier((pieces, peer_features))

    out, *slot_grads = attend(table, queries, query_peer, upstream, upstream_peer, pieces)
    sums = combine(
        send_all(slot_grads[:4], xn, xb, x2) + send_all(slot_grads[4:], yn, yb, y2)
    )
    grads, grads_away = finish_grads(
        send_all(sums[:4], yn, yb, y2) + send_all(sums[4:], xn, xb, x2), cosine, sine
    )
    grads_other = swap(grads_away)

    out_other = swap(out[local_rows:])

    def assemble(a, b):
        first = jnp.where(core == 0, a, b)
        second = jnp.where(core == 0, b, a)
        return jnp.concatenate([first, second], axis=1)

    attention = assemble(out[:local_rows, :width], out_other[:, :width])
    query_grad = assemble(out[:local_rows, width:], out_other[:, width:])

    parts = input_partials(place, grads, grads_other, key_weight, value_weight)
    from_back = zn(parts[2])
    from_next = zb(parts[1])
    from_far = z2(parts[3])
    hidden_grad = (
        parts[0].astype(F32)
        + from_back.astype(F32)
        + from_next.astype(F32)
        + from_far.astype(F32)
    ).astype(BF)

    w_parts = weight_partials(place, grads, own_features, peer_features)
    w_sums = combine(send_all(w_parts[:4], xn, xb, x2) + send_all(w_parts[4:], yn, yb, y2))
    both, both_away = finish_weights(
        send_all(w_sums[:4], yn, yb, y2) + send_all(w_sums[4:], xn, xb, x2)
    )
    both_other = swap(both_away)
    key_weight_grad = assemble(both[:, :HD], both_other[:, :HD])
    value_weight_grad = assemble(both[:, HD:], both_other[:, HD:])
    return (attention, query_grad, hidden_grad, key_weight_grad, value_weight_grad)


def solution(mesh):
    return jax.shard_map(
        shards,
        mesh=mesh,
        in_specs=(
            P("ctx", "tp"),
            P("ctx", "tp"),
            P(None, "tp"),
            P(None, "tp"),
            P(),
            P("ctx", "tp"),
        ),
        out_specs=(P("ctx", "tp"), P("ctx", "tp"), P("ctx", "tp"), P("ctx", "tp"), P("ctx", "tp")),
        check_vma=False,
    )
```

```python
import math

import jax
import jax.numpy as jnp
from jax import lax
from jax.experimental import pallas as pl
from jax.experimental.pallas import tpu as pltpu
from jax.sharding import PartitionSpec as P

HD = 128
BLOCK = 128
DEPTH = 8
THETA = 1000000.0
NEGATIVE = -1e30
BF = jnp.bfloat16
F32 = jnp.float32
SCALE = 1.0 / math.sqrt(HD)
STACK = DEPTH - 1
SLOTS = STACK + 4
OFFSETS = (0, 3, 1, 2)


def side(delta):
    return jnp.where(delta == 0, 0, jnp.where(delta == 3, 1, jnp.where(delta == 1, 2, 3)))


def device_tables(parents, position):
    block_total = parents.shape[0]

    def body(links, where, table, place, depths, level):
        y, x, core, tp = where[0], where[1], where[2], where[3]
        first = 16 * y + 4 * x
        level[0] = 0

        def descend(b, carry):
            level[b] = level[links[b]] + 1
            return carry

        lax.fori_loop(1, block_total, descend, 0)
        place[0] = tp
        place[1] = (tp + 3) % 4
        place[2] = (tp + 1) % 4
        place[3] = (tp + 2) % 4
        place[4] = core
        for k, o in enumerate(OFFSETS):
            place[5 + k] = (tp + o) % 4
            place[9 + k] = side((tp + o - y + 4) % 4)
            place[13 + k] = (x + o) % 4
        table[AT_CORE] = core

        def blank(i, carry):
            table[AT_DENSE + i] = SLOTS
            return carry

        lax.fori_loop(0, 64, blank, 0)
        for r in range(4):
            table[AT_DENSE + r] = STACK + r
            block = first + (2 * core + r) % 4
            own_depth = level[block]
            depths[r] = own_depth
            table[AT_DEPTH + r] = own_depth
            node = block
            for d in range(DEPTH - 1, -1, -1):
                live = d <= own_depth
                slot = jnp.where(node >= first, STACK + (node - first + 4 - 2 * core) % 4, d)
                table[AT_SLOT + r * DEPTH + d] = jnp.where(live, slot, STACK + r)
                node = jnp.where(live, jnp.maximum(links[node], 0), node)
        lead_depth = level[first]
        node = first
        for d in range(STACK - 1, -1, -1):
            live = d < lead_depth
            node = jnp.where(live, jnp.maximum(links[node], 0), node)
            column = side((node // 4 + 4 - x) % 4)
            line = side((node // 16 + 4 - y) % 4)
            same = (node // 2) % 2 == core
            parity = node % 2
            outer = jnp.where(same, line, column)
            inner = jnp.where(same, column, line)
            piece = jnp.where(same, 0, 5) + jnp.where(outer < 3, outer, 3 + parity)
            table[d] = jnp.where(live, piece, -1)
            table[AT_PLACE + d] = jnp.where(
                live, jnp.where(outer < 3, inner * 2 + parity, inner), 0
            )
            spot = AT_DENSE + (column * 4 + line) * 4 + (node + 4 - 2 * core) % 4

            @pl.when(live)
            def _(spot=spot, d=d):
                table[spot] = d

    smem = pl.BlockSpec(memory_space=pltpu.SMEM)
    return pl.pallas_call(
        body,
        in_specs=[smem, smem],
        out_specs=[smem] * 3,
        out_shape=[
            jax.ShapeDtypeStruct((AT_CORE + 1,), jnp.int32),
            jax.ShapeDtypeStruct((17,), jnp.int32),
            jax.ShapeDtypeStruct((4,), jnp.int32),
        ],
        scratch_shapes=[pltpu.SMEM((block_total,), jnp.int32)],
        name="device_tables",
    )(parents, position)


AT_PLACE = STACK
AT_DEPTH = 2 * STACK
AT_SLOT = AT_DEPTH + 4
AT_DENSE = AT_SLOT + 4 * DEPTH
AT_CORE = AT_DENSE + 64


def rope_tables(depths):
    offset = jnp.arange(BLOCK, dtype=jnp.int32)
    position = (depths[:, None] * BLOCK + offset[None, :]).astype(F32)
    frequency = jnp.exp(jnp.arange(HD // 2, dtype=F32) * (-2.0 * math.log(THETA) / HD))
    angles = (position[:, :, None] * frequency[None, None, :]).reshape(4 * BLOCK, HD // 2)
    cosine, sine = jnp.cos(angles), jnp.sin(angles)
    return (
        jnp.concatenate([cosine, cosine], axis=-1),
        jnp.concatenate([-sine, sine], axis=-1),
    )


def nn(a, b):
    return jnp.dot(a, b, preferred_element_type=F32)


def nt(a, b):
    return lax.dot_general(a, b, (((1,), (1,)), ((), ())), preferred_element_type=F32)


def tn(a, b):
    return lax.dot_general(a, b, (((0,), (0,)), ((), ())), preferred_element_type=F32)


def params(mib):
    return pltpu.CompilerParams(vmem_limit_bytes=mib * 1024 * 1024)


def project_near(place, own, left, right, key_weight, value_weight):
    rows, width = own.shape
    cols = key_weight.shape[1]

    def body(place_ref, a, b, c, ka, kb, kc, va, vb, vc, key_out, value_out):
        key_out[...] = nn(a[...], ka[...]) + nn(b[...], kb[...]) + nn(c[...], kc[...])
        value_out[...] = nn(a[...], va[...]) + nn(b[...], vb[...]) + nn(c[...], vc[...])

    whole = pl.BlockSpec((rows, width), lambda i, p: (0, 0))
    weights = [pl.BlockSpec((width, cols), lambda i, p, k=k: (p[k], 0)) for k in range(3)]
    out = pl.BlockSpec((rows, cols), lambda i, p: (0, 0))
    return pl.pallas_call(
        body,
        grid_spec=pltpu.PrefetchScalarGridSpec(
            num_scalar_prefetch=1,
            grid=(1,),
            in_specs=[whole] * 3 + weights + weights,
            out_specs=[out, out],
        ),
        out_shape=[jax.ShapeDtypeStruct((rows, cols), F32)] * 2,
        compiler_params=params(18),
        name="project_near",
    )(place, own, left, right, *([key_weight] * 3), *([value_weight] * 3))


def project_far(place, top, bottom, key_weight, value_weight, key_sum, value_sum, cosine, sine):
    rows, cols = key_sum.shape
    width = top.shape[1]
    half = rows // 2

    def body(p, a, b, kw, vw, ks, vs, cs, sn, keep, send):
        far = jnp.concatenate([a[...], b[...]], axis=0)
        key = ks[...] + nn(far, kw[...])
        value = vs[...] + nn(far, vw[...])
        heads = []
        for h in range(2):
            part = key[:, h * HD : (h + 1) * HD]
            turned = part * cs[...] + pltpu.roll(part, HD // 2, 1) * sn[...]
            heads.append(
                jnp.concatenate([turned, value[:, h * HD : (h + 1) * HD]], axis=1).astype(BF)
            )
        swap = p[4] == 1
        keep[...] = jnp.where(swap, heads[1], heads[0])
        send[...] = jnp.where(swap, heads[0], heads[1])

    weight = pl.BlockSpec((width, cols), lambda i, p: (p[3], 0))
    part = pl.BlockSpec((half, width), lambda i, p: (0, 0))
    sums = pl.BlockSpec((rows, cols), lambda i, p: (0, 0))
    angle = pl.BlockSpec((rows, HD), lambda i, p: (0, 0))
    return pl.pallas_call(
        body,
        grid_spec=pltpu.PrefetchScalarGridSpec(
            num_scalar_prefetch=1,
            grid=(1,),
            in_specs=[part, part, weight, weight, sums, sums, angle, angle],
            out_specs=[sums, sums],
        ),
        out_shape=[jax.ShapeDtypeStruct((rows, cols), BF)] * 2,
        compiler_params=params(10),
        name="project_far",
    )(place, top, bottom, key_weight, value_weight, key_sum, value_sum, cosine, sine)


def attend(table, queries, query_peer, upstream, upstream_peer, pieces):
    groups = queries.shape[1] // (2 * HD)
    width = groups * HD
    lanes = groups * BLOCK

    def body(t, q_own, q_far, u_own, u_far, *refs):
        parts = refs[:10]
        k_outs = refs[11:15]
        v_outs = refs[15:19]
        out = refs[10]
        kv, total, q_rows, u_rows = refs[19:]
        step = pl.program_id(0)

        @pl.when(step == 0)
        def _():
            for s in range(STACK):
                for index in range(10):

                    @pl.when(t[s] == index)
                    def _(s=s, index=index):
                        kv[s] = parts[index][t[AT_PLACE + s]]

            for r in range(4):
                kv[STACK + r] = parts[0 if r < 2 else 5][r % 2]
            total[...] = jnp.zeros(total.shape, F32)

        own = step < 2
        q = jnp.where(own, q_own[...], q_far[...])
        u = jnp.where(own, u_own[...], u_far[...])
        for h in range(groups):
            q_rows[h * BLOCK : (h + 1) * BLOCK] = q[:, h * HD : (h + 1) * HD]
            u_rows[h * BLOCK : (h + 1) * BLOCK] = u[:, h * HD : (h + 1) * HD]
        q = q_rows[...]
        u = u_rows[...]
        depth = t[AT_DEPTH + step]
        slots = [t[AT_SLOT + step * DEPTH + d] for d in range(DEPTH)]
        keys = jnp.concatenate([kv[s, :, :HD] for s in slots], axis=0)
        values = jnp.concatenate([kv[s, :, HD:] for s in slots], axis=0)
        ahead = lax.broadcasted_iota(jnp.int32, (BLOCK, lanes), 0) - (
            lax.broadcasted_iota(jnp.int32, (BLOCK, lanes), 1) % BLOCK
        )
        raw = nt(keys, q)
        scores = []
        peak = None
        for d in range(DEPTH):
            reach = jnp.where(d < depth, BLOCK, jnp.where(d == depth, 0, -BLOCK))
            tile = jnp.where(
                ahead <= reach, raw[d * BLOCK : (d + 1) * BLOCK] * SCALE, NEGATIVE
            )
            scores.append(tile)
            top = jnp.max(tile, axis=0, keepdims=True)
            peak = top if peak is None else jnp.maximum(peak, top)
        weights = [jnp.exp(tile - peak) for tile in scores]
        mass = None
        for w in weights:
            part = jnp.sum(w, axis=0, keepdims=True)
            mass = part if mass is None else mass + part
        rounded = jnp.concatenate([w.astype(BF) for w in weights], axis=0)
        mixed = (tn(values, rounded) / mass).astype(BF).astype(F32)
        delta = jnp.sum(u.astype(F32).T * mixed, axis=0, keepdims=True)
        for h in range(groups):
            out[:, h * HD : (h + 1) * HD] = mixed[:, h * BLOCK : (h + 1) * BLOCK].T.astype(BF)
        inverse = 1.0 / mass
        slopes = nt(values, u)
        chances = []
        pulls = []
        for d in range(DEPTH):
            p = weights[d] * inverse
            chances.append(p.astype(BF))
            pulls.append((p * (slopes[d * BLOCK : (d + 1) * BLOCK] - delta)).astype(BF))
        chances = jnp.concatenate(chances, axis=0)
        pulls = jnp.concatenate(pulls, axis=0)
        turned = tn(keys, pulls) * SCALE
        for h in range(groups):
            out[:, width + h * HD : width + (h + 1) * HD] = (
                turned[:, h * BLOCK : (h + 1) * BLOCK].T.astype(BF)
            )
        v_part = nn(chances, u)
        k_part = nn(pulls, q) * SCALE
        for d in range(DEPTH):
            low = d * BLOCK
            total[slots[d], :, :HD] += k_part[low : low + BLOCK]
            total[slots[d], :, HD:] += v_part[low : low + BLOCK]

        @pl.when(step == 3)
        def _():
            for outer in range(4):

                def fill(i, carry, outer=outer):
                    k_slot = t[AT_DENSE + outer * 16 + i]
                    v_slot = t[AT_DENSE + (i // 4) * 16 + outer * 4 + i % 4]
                    k = total[k_slot, :, :HD]
                    v = total[v_slot, :, HD:]
                    k_outs[outer][i] = k.astype(k_outs[outer].dtype)
                    v_outs[outer][i] = v.astype(v_outs[outer].dtype)
                    return carry

                lax.fori_loop(0, 16, fill, 0)

    mine = pl.BlockSpec((BLOCK, width), lambda i, t: (jnp.minimum(i, 1), t[AT_CORE]))
    peer = pl.BlockSpec((BLOCK, width), lambda i, t: (jnp.maximum(i - 2, 0), 0))
    rows = pl.BlockSpec((BLOCK, 2 * width), lambda i, t: (i, 0))

    def full(shape):
        return pl.BlockSpec(
            shape, lambda i, t: (0,) * len(shape), pipeline_mode=pl.Buffered(1)
        )

    def held(shape):
        return pl.BlockSpec(shape, lambda i, t: (0,) * len(shape))

    wide = (16, BLOCK, HD)
    grads = [(wide, F32)] + [(wide, BF)] * 3
    return pl.pallas_call(
        body,
        grid_spec=pltpu.PrefetchScalarGridSpec(
            num_scalar_prefetch=1,
            grid=(4,),
            in_specs=[mine, peer, mine, peer] + [full(p.shape) for p in pieces],
            out_specs=[rows] + [held(s) for s, _ in grads + grads],
            scratch_shapes=[
                pltpu.VMEM((SLOTS, BLOCK, 2 * HD), BF),
                pltpu.VMEM((SLOTS + 1, BLOCK, 2 * HD), F32),
                pltpu.VMEM((lanes, HD), BF),
                pltpu.VMEM((lanes, HD), BF),
            ],
        ),
        out_shape=[jax.ShapeDtypeStruct((4 * BLOCK, 2 * width), BF)]
        + [jax.ShapeDtypeStruct(s, d) for s, d in grads + grads],
        compiler_params=params(36),
        name="attend",
    )(table, queries, query_peer, upstream, upstream_peer, *pieces)


def combine(sums):
    def body(*refs):
        for side_of in range(2):
            home, a, b, c = refs[4 * side_of : 4 * side_of + 4]
            outs = refs[8 + 4 * side_of : 12 + 4 * side_of]
            rows = outs[0].shape[0]
            for k in range(4):
                at = slice(k * rows, (k + 1) * rows)
                outs[k][...] = (
                    home[at] + a[at].astype(F32) + b[at].astype(F32) + c[at].astype(F32)
                )

    shape = sums[0].shape
    part = (shape[0] // 4,) + shape[1:]
    return pl.pallas_call(
        body,
        in_specs=[pl.BlockSpec(memory_space=pltpu.VMEM)] * 8,
        out_specs=[pl.BlockSpec(memory_space=pltpu.VMEM)] * 8,
        out_shape=[jax.ShapeDtypeStruct(part, F32)] * 8,
        compiler_params=params(12),
        name="combine",
    )(*sums)


def finish_grads(sums, cosine, sine):
    rows = 4 * BLOCK

    def body(*refs):
        ks, vs = refs[:4], refs[4:8]
        cs, sn, every, away = refs[8:]
        key = (ks[0][...] + ks[1][...] + ks[2][...] + ks[3][...]).reshape(rows, HD)
        value = (vs[0][...] + vs[1][...] + vs[2][...] + vs[3][...]).reshape(rows, HD)
        key = key * cs[...] - pltpu.roll(key, HD // 2, 1) * sn[...]
        both = jnp.concatenate([key.astype(BF), value.astype(BF)], axis=1)
        every[...] = both
        away[...] = both[rows // 2 :]

    return pl.pallas_call(
        body,
        in_specs=[pl.BlockSpec(memory_space=pltpu.VMEM)] * 10,
        out_specs=[pl.BlockSpec(memory_space=pltpu.VMEM)] * 2,
        out_shape=[
            jax.ShapeDtypeStruct((rows, 2 * HD), BF),
            jax.ShapeDtypeStruct((rows // 2, 2 * HD), BF),
        ],
        compiler_params=params(8),
        name="finish_grads",
    )(*sums, cosine, sine)


def finish_weights(sums):
    share = sums[0].shape[1]

    def body(*refs):
        ks, vs = refs[:4], refs[4:8]
        for row, out in enumerate(refs[8:]):
            out[:, :HD] = ks[0][row] + ks[1][row] + ks[2][row] + ks[3][row]
            out[:, HD:] = vs[0][row] + vs[1][row] + vs[2][row] + vs[3][row]

    return pl.pallas_call(
        body,
        in_specs=[pl.BlockSpec(memory_space=pltpu.VMEM)] * 8,
        out_specs=[pl.BlockSpec(memory_space=pltpu.VMEM)] * 2,
        out_shape=[jax.ShapeDtypeStruct((share, 2 * HD), F32)] * 2,
        compiler_params=params(6),
        name="finish_weights",
    )(*sums)


def input_partials(place, mine, other, key_weight, value_weight):
    rows = other.shape[0]
    cols = key_weight.shape[1]
    width = key_weight.shape[0] // 4

    def body(p, a, b, kw, vw, *outs):
        swap = p[4] == 1
        first = jnp.where(swap, b[...], a[...])
        second = jnp.where(swap, a[...], b[...])
        key = jnp.concatenate([first[:, :HD], second[:, :HD]], axis=1)
        value = jnp.concatenate([first[:, HD:], second[:, HD:]], axis=1)
        result = (nt(key, kw[...]) + nt(value, vw[...])).astype(BF)
        for k in range(4):

            @pl.when(pl.program_id(0) == k)
            def _(k=k):
                outs[k][...] = result

    grads = pl.BlockSpec((rows, 2 * HD), lambda i, p: (0, 0))
    weight = pl.BlockSpec((width, cols), lambda i, p: (p[5 + i], 0))
    out = pl.BlockSpec((rows, width), lambda i, p: (0, 0))
    return pl.pallas_call(
        body,
        grid_spec=pltpu.PrefetchScalarGridSpec(
            num_scalar_prefetch=1,
            grid=(4,),
            in_specs=[grads, grads, weight, weight],
            out_specs=[out] * 4,
        ),
        out_shape=[jax.ShapeDtypeStruct((rows, width), BF)] * 4,
        compiler_params=params(10),
        name="input_partials",
    )(place, mine, other, key_weight, value_weight)


def weight_partials(place, grads, own, peer):
    width = own[0].shape[1]
    share = width // 8

    def body(p, g, a0, a1, a2, a3, a4, b0, b1, b2, b3, b4, *refs):
        k_outs, v_outs, result = refs[:4], refs[4:8], refs[8]
        core = p[4]
        grad = g[...]
        half = a3.shape[0]
        for piece in range(4):
            if piece < 3:
                rows = [(a0, b0), (a1, b1), (a2, b2)][piece]
            else:
                rows = (a3, a4, b3, b4)
            features = jnp.concatenate([r[...] for r in rows], axis=0)
            result[...] = tn(features, grad)
            line = p[9 + piece]
            for dx in range(4):
                base = p[13 + dx] * (2 * share)
                for r in range(2):
                    start = pl.multiple_of(base + ((core + r) % 2) * share, 16)
                    value = result[pl.ds(start, share), :]
                    k_outs[dx][line * 2 + r] = value[:, :HD].astype(k_outs[dx].dtype)
                    for dy in range(4):

                        @pl.when(line == dy)
                        def _(dy=dy, dx=dx, r=r, value=value):
                            v_outs[dy][dx * 2 + r] = value[:, HD:].astype(v_outs[dy].dtype)

    wide = (8, share, HD)
    shapes = [(wide, F32)] + [(wide, BF)] * 3
    return pl.pallas_call(
        body,
        in_specs=[pl.BlockSpec(memory_space=pltpu.SMEM)]
        + [pl.BlockSpec(memory_space=pltpu.VMEM)] * 11,
        out_specs=[pl.BlockSpec(memory_space=pltpu.VMEM)] * 8,
        out_shape=[jax.ShapeDtypeStruct(s, d) for s, d in shapes + shapes],
        scratch_shapes=[pltpu.VMEM((width, 2 * HD), F32)],
        compiler_params=params(16),
        name="weight_partials",
    )(place, grads, *own, *peer)


def mover(axis, pairs):
    return lambda value: lax.ppermute(value, axis, pairs)


def ring_gather(value, ahead, behind):
    back = ahead(value)
    forth = behind(value)
    far0 = ahead(back[:, :1])
    far1 = behind(forth[:, 1:])
    return back, forth, far0, far1


def send_all(values, ahead, behind, across):
    home, back, forth, far = values
    return [home, ahead(forth), behind(back), across(far)]


def shards(hidden, queries, key_weight, value_weight, parents, upstream):
    place_ctx = lax.axis_index("ctx")
    tp = lax.axis_index("tp")
    core = place_ctx % 2
    x = (place_ctx // 2) % 4
    y = place_ctx // 8
    xn = mover("ctx", [(i, i // 8 * 8 + (i + 2) % 8) for i in range(32)])
    xb = mover("ctx", [(i, i // 8 * 8 + (i - 2) % 8) for i in range(32)])
    yn = mover("ctx", [(i, (i + 8) % 32) for i in range(32)])
    yb = mover("ctx", [(i, (i - 8) % 32) for i in range(32)])
    swap = mover("ctx", [(i, i ^ 1) for i in range(32)])
    zn = mover("tp", [(i, (i + 1) % 4) for i in range(4)])
    zb = mover("tp", [(i, (i - 1) % 4) for i in range(4)])
    x2 = mover("ctx", [(i, i // 8 * 8 + (i + 4) % 8) for i in range(32)])
    y2 = mover("ctx", [(i, (i + 16) % 32) for i in range(32)])
    z2 = mover("tp", [(i, (i + 2) % 4) for i in range(4)])

    local_rows = hidden.shape[0]
    half_rows = local_rows // 2
    table, place, depths = device_tables(
        parents, jnp.stack([y, x, core, tp]).astype(jnp.int32)
    )
    cosine, sine = rope_tables(depths)

    left = zn(hidden)
    right = zb(hidden)
    far_top = zn(left[:half_rows])
    far_low = zb(right[half_rows:])
    key_sum, value_sum = project_near(place, hidden, left, right, key_weight, value_weight)
    keep, send = project_far(
        place, far_top, far_low, key_weight, value_weight, key_sum, value_sum, cosine, sine
    )
    width = queries.shape[1] // 2
    query_peer = swap(lax.dynamic_slice_in_dim(queries, (1 - core) * width, width, 1))
    upstream_peer = swap(lax.dynamic_slice_in_dim(upstream, (1 - core) * width, width, 1))

    mine = keep.reshape(1, 2, BLOCK, 2 * HD)
    other = swap(send).reshape(1, 2, BLOCK, 2 * HD)
    mine_line = jnp.concatenate([mine, xn(mine), xb(mine), x2(mine)], axis=0)
    other_line = jnp.concatenate([other, yn(other), yb(other), y2(other)], axis=0)
    pieces = [mine_line, *ring_gather(mine_line, yn, yb)]
    pieces += [other_line, *ring_gather(other_line, xn, xb)]
    pieces = [p.reshape(-1, BLOCK, 2 * HD) for p in pieces]

    own_features = [hidden, left, right, far_top, far_low]
    peer_features = [swap(f) for f in own_features]
    pieces, peer_features = lax.optimization_barrier((pieces, peer_features))

    out, *slot_grads = attend(table, queries, query_peer, upstream, upstream_peer, pieces)
    sums = combine(
        send_all(slot_grads[:4], xn, xb, x2) + send_all(slot_grads[4:], yn, yb, y2)
    )
    grads, grads_away = finish_grads(
        send_all(sums[:4], yn, yb, y2) + send_all(sums[4:], xn, xb, x2), cosine, sine
    )
    grads_other = swap(grads_away)
    grads, grads_other = lax.optimization_barrier((grads, grads_other))

    out_other = swap(out[local_rows:])

    def assemble(a, b):
        first = jnp.where(core == 0, a, b)
        second = jnp.where(core == 0, b, a)
        return jnp.concatenate([first, second], axis=1)

    attention = assemble(out[:local_rows, :width], out_other[:, :width])
    query_grad = assemble(out[:local_rows, width:], out_other[:, width:])

    w_parts = weight_partials(place, grads, own_features, peer_features)
    w_sent = send_all(w_parts[:4], xn, xb, x2) + send_all(w_parts[4:], yn, yb, y2)
    parts = input_partials(place, grads, grads_other, key_weight, value_weight)
    from_back = zn(parts[2])
    from_next = zb(parts[1])
    from_far = z2(parts[3])
    hidden_grad = (
        parts[0].astype(F32)
        + from_back.astype(F32)
        + from_next.astype(F32)
        + from_far.astype(F32)
    ).astype(BF)
    *w_sent, _ = lax.optimization_barrier((*w_sent, parts[0]))
    w_sums = combine(w_sent)
    both, both_away = finish_weights(
        send_all(w_sums[:4], yn, yb, y2) + send_all(w_sums[4:], xn, xb, x2)
    )
    both_other = swap(both_away)
    key_weight_grad = assemble(both[:, :HD], both_other[:, :HD])
    value_weight_grad = assemble(both[:, HD:], both_other[:, HD:])
    return (attention, query_grad, hidden_grad, key_weight_grad, value_weight_grad)


def solution(mesh):
    return jax.shard_map(
        shards,
        mesh=mesh,
        in_specs=(
            P("ctx", "tp"),
            P("ctx", "tp"),
            P(None, "tp"),
            P(None, "tp"),
            P(),
            P("ctx", "tp"),
        ),
        out_specs=(P("ctx", "tp"), P("ctx", "tp"), P("ctx", "tp"), P("ctx", "tp"), P("ctx", "tp")),
        check_vma=False,
    )
```

```python
import math

import jax
import jax.numpy as jnp
from jax import lax
from jax.experimental import pallas as pl
from jax.experimental.pallas import tpu as pltpu
from jax.sharding import PartitionSpec as P

HD = 128
BLOCK = 128
DEPTH = 8
THETA = 1000000.0
NEGATIVE = -1e30
BF = jnp.bfloat16
F32 = jnp.float32
SCALE = 1.0 / math.sqrt(HD)
STACK = DEPTH - 1
SLOTS = STACK + 4
OFFSETS = (0, 3, 1, 2)


def side(delta):
    return jnp.where(delta == 0, 0, jnp.where(delta == 3, 1, jnp.where(delta == 1, 2, 3)))


def device_tables(parents, position):
    block_total = parents.shape[0]

    def body(links, where, table, place, depths, level):
        y, x, core, tp = where[0], where[1], where[2], where[3]
        first = 16 * y + 4 * x
        level[0] = 0

        def descend(b, carry):
            level[b] = level[links[b]] + 1
            return carry

        lax.fori_loop(1, block_total, descend, 0)
        place[0] = tp
        place[1] = (tp + 3) % 4
        place[2] = (tp + 1) % 4
        place[3] = (tp + 2) % 4
        place[4] = core
        for k, o in enumerate(OFFSETS):
            place[5 + k] = (tp + o) % 4
            place[9 + k] = side((tp + o - y + 4) % 4)
            place[13 + k] = (x + o) % 4
        table[AT_CORE] = core

        def blank(i, carry):
            table[AT_DENSE + i] = SLOTS
            return carry

        lax.fori_loop(0, 64, blank, 0)
        for r in range(4):
            table[AT_DENSE + r] = STACK + r
            block = first + (2 * core + r) % 4
            own_depth = level[block]
            depths[r] = own_depth
            table[AT_DEPTH + r] = own_depth
            node = block
            for d in range(DEPTH - 1, -1, -1):
                live = d <= own_depth
                slot = jnp.where(node >= first, STACK + (node - first + 4 - 2 * core) % 4, d)
                table[AT_SLOT + r * DEPTH + d] = jnp.where(live, slot, STACK + r)
                node = jnp.where(live, jnp.maximum(links[node], 0), node)
        lead_depth = level[first]
        node = first
        for d in range(STACK - 1, -1, -1):
            live = d < lead_depth
            node = jnp.where(live, jnp.maximum(links[node], 0), node)
            column = side((node // 4 + 4 - x) % 4)
            line = side((node // 16 + 4 - y) % 4)
            same = (node // 2) % 2 == core
            parity = node % 2
            outer = jnp.where(same, line, column)
            inner = jnp.where(same, column, line)
            piece = jnp.where(same, 0, 8) + outer * 2 + parity
            table[d] = jnp.where(live, piece, -1)
            table[AT_PLACE + d] = jnp.where(live, inner, 0)
            spot = AT_DENSE + (column * 4 + line) * 4 + (node + 4 - 2 * core) % 4

            @pl.when(live)
            def _(spot=spot, d=d):
                table[spot] = d

    smem = pl.BlockSpec(memory_space=pltpu.SMEM)
    return pl.pallas_call(
        body,
        in_specs=[smem, smem],
        out_specs=[smem] * 3,
        out_shape=[
            jax.ShapeDtypeStruct((AT_CORE + 1,), jnp.int32),
            jax.ShapeDtypeStruct((17,), jnp.int32),
            jax.ShapeDtypeStruct((4,), jnp.int32),
        ],
        scratch_shapes=[pltpu.SMEM((block_total,), jnp.int32)],
        name="device_tables",
    )(parents, position)


AT_PLACE = STACK
AT_DEPTH = 2 * STACK
AT_SLOT = AT_DEPTH + 4
AT_DENSE = AT_SLOT + 4 * DEPTH
AT_CORE = AT_DENSE + 64


def rope_tables(depths):
    offset = jnp.arange(BLOCK, dtype=jnp.int32)
    position = (depths[:, None] * BLOCK + offset[None, :]).astype(F32)
    frequency = jnp.exp(jnp.arange(HD // 2, dtype=F32) * (-2.0 * math.log(THETA) / HD))
    angles = (position[:, :, None] * frequency[None, None, :]).reshape(4 * BLOCK, HD // 2)
    cosine, sine = jnp.cos(angles), jnp.sin(angles)
    return (
        jnp.concatenate([cosine, cosine], axis=-1),
        jnp.concatenate([-sine, sine], axis=-1),
    )


def nn(a, b):
    return jnp.dot(a, b, preferred_element_type=F32)


def nt(a, b):
    return lax.dot_general(a, b, (((1,), (1,)), ((), ())), preferred_element_type=F32)


def tn(a, b):
    return lax.dot_general(a, b, (((0,), (0,)), ((), ())), preferred_element_type=F32)


def params(mib):
    return pltpu.CompilerParams(vmem_limit_bytes=mib * 1024 * 1024)


def project_near(place, own, left_top, left_low, right_top, right_low, key_weight, value_weight):
    rows, width = own.shape
    cols = key_weight.shape[1]

    def body(place_ref, a, bt, bl, ct, cl, ka, kb, kc, va, vb, vc, key_out, value_out):
        b = jnp.concatenate([bt[...], bl[...]], axis=0)
        c = jnp.concatenate([ct[...], cl[...]], axis=0)
        key_out[...] = nn(a[...], ka[...]) + nn(b, kb[...]) + nn(c, kc[...])
        value_out[...] = nn(a[...], va[...]) + nn(b, vb[...]) + nn(c, vc[...])

    whole = pl.BlockSpec((rows, width), lambda i, p: (0, 0))
    half = pl.BlockSpec((rows // 2, width), lambda i, p: (0, 0))
    weights = [pl.BlockSpec((width, cols), lambda i, p, k=k: (p[k], 0)) for k in range(3)]
    out = pl.BlockSpec((rows, cols), lambda i, p: (0, 0))
    return pl.pallas_call(
        body,
        grid_spec=pltpu.PrefetchScalarGridSpec(
            num_scalar_prefetch=1,
            grid=(1,),
            in_specs=[whole] + [half] * 4 + weights + weights,
            out_specs=[out, out],
        ),
        out_shape=[jax.ShapeDtypeStruct((rows, cols), F32)] * 2,
        compiler_params=params(18),
        name="project_near",
    )(
        place,
        own,
        left_top,
        left_low,
        right_top,
        right_low,
        *([key_weight] * 3),
        *([value_weight] * 3),
    )


def pack(own, back, forth, far):
    def body(a, b, c, d, first, second):
        for k, ref in enumerate((a, b, c, d)):
            first[k] = ref[:BLOCK]
            second[k] = ref[BLOCK:]

    return pl.pallas_call(
        body,
        in_specs=[pl.BlockSpec(memory_space=pltpu.VMEM)] * 4,
        out_specs=[pl.BlockSpec(memory_space=pltpu.VMEM)] * 2,
        out_shape=[jax.ShapeDtypeStruct((4, BLOCK, 2 * HD), BF)] * 2,
        compiler_params=params(6),
        name="pack",
    )(own, back, forth, far)


def join_weights(place, mine, other):
    share = mine.shape[0]

    def body(p, a, b, key, value):
        swap = p[4] == 1
        first = jnp.where(swap, b[...], a[...])
        second = jnp.where(swap, a[...], b[...])
        key[:, :HD] = first[:, :HD]
        key[:, HD:] = second[:, :HD]
        value[:, :HD] = first[:, HD:]
        value[:, HD:] = second[:, HD:]

    return pl.pallas_call(
        body,
        in_specs=[pl.BlockSpec(memory_space=pltpu.SMEM)]
        + [pl.BlockSpec(memory_space=pltpu.VMEM)] * 2,
        out_specs=[pl.BlockSpec(memory_space=pltpu.VMEM)] * 2,
        out_shape=[jax.ShapeDtypeStruct((share, 2 * HD), F32)] * 2,
        compiler_params=params(6),
        name="join_weights",
    )(place, mine, other)


def project_far(place, top, bottom, key_weight, value_weight, key_sum, value_sum, cosine, sine):
    rows, cols = key_sum.shape
    width = top.shape[1]
    half = rows // 2

    def body(p, a, b, kw, vw, ks, vs, cs, sn, keep, send):
        far = jnp.concatenate([a[...], b[...]], axis=0)
        key = ks[...] + nn(far, kw[...])
        value = vs[...] + nn(far, vw[...])
        heads = []
        for h in range(2):
            part = key[:, h * HD : (h + 1) * HD]
            turned = part * cs[...] + pltpu.roll(part, HD // 2, 1) * sn[...]
            heads.append(
                jnp.concatenate([turned, value[:, h * HD : (h + 1) * HD]], axis=1).astype(BF)
            )
        swap = p[4] == 1
        keep[...] = jnp.where(swap, heads[1], heads[0])
        send[...] = jnp.where(swap, heads[0], heads[1])

    weight = pl.BlockSpec((width, cols), lambda i, p: (p[3], 0))
    part = pl.BlockSpec((half, width), lambda i, p: (0, 0))
    sums = pl.BlockSpec((rows, cols), lambda i, p: (0, 0))
    angle = pl.BlockSpec((rows, HD), lambda i, p: (0, 0))
    return pl.pallas_call(
        body,
        grid_spec=pltpu.PrefetchScalarGridSpec(
            num_scalar_prefetch=1,
            grid=(1,),
            in_specs=[part, part, weight, weight, sums, sums, angle, angle],
            out_specs=[sums, sums],
        ),
        out_shape=[jax.ShapeDtypeStruct((rows, cols), BF)] * 2,
        compiler_params=params(10),
        name="project_far",
    )(place, top, bottom, key_weight, value_weight, key_sum, value_sum, cosine, sine)


def attend(table, queries, query_peer, upstream, upstream_peer, pieces):
    groups = queries.shape[1] // (2 * HD)
    width = groups * HD
    lanes = groups * BLOCK

    def body(t, q_own, q_far, u_own, u_far, *refs):
        parts = refs[:16]
        k_outs = refs[17:21]
        v_outs = refs[21:25]
        out = refs[16]
        kv, total, q_rows, u_rows = refs[25:]
        step = pl.program_id(0)

        @pl.when(step == 0)
        def _():
            for s in range(STACK):
                for index in range(16):

                    @pl.when(t[s] == index)
                    def _(s=s, index=index):
                        kv[s] = parts[index][t[AT_PLACE + s]]

            for r in range(4):
                kv[STACK + r] = parts[r if r < 2 else 6 + r][0]
            total[...] = jnp.zeros(total.shape, F32)

        own = step < 2
        q = jnp.where(own, q_own[...], q_far[...])
        u = jnp.where(own, u_own[...], u_far[...])
        for h in range(groups):
            q_rows[h * BLOCK : (h + 1) * BLOCK] = q[:, h * HD : (h + 1) * HD]
            u_rows[h * BLOCK : (h + 1) * BLOCK] = u[:, h * HD : (h + 1) * HD]
        q = q_rows[...]
        u = u_rows[...]
        depth = t[AT_DEPTH + step]
        slots = [t[AT_SLOT + step * DEPTH + d] for d in range(DEPTH)]
        keys = jnp.concatenate([kv[s, :, :HD] for s in slots], axis=0)
        values = jnp.concatenate([kv[s, :, HD:] for s in slots], axis=0)
        ahead = lax.broadcasted_iota(jnp.int32, (BLOCK, lanes), 0) - (
            lax.broadcasted_iota(jnp.int32, (BLOCK, lanes), 1) % BLOCK
        )
        raw = nt(keys, q)
        scores = []
        peak = None
        for d in range(DEPTH):
            reach = jnp.where(d < depth, BLOCK, jnp.where(d == depth, 0, -BLOCK))
            tile = jnp.where(
                ahead <= reach, raw[d * BLOCK : (d + 1) * BLOCK] * SCALE, NEGATIVE
            )
            scores.append(tile)
            top = jnp.max(tile, axis=0, keepdims=True)
            peak = top if peak is None else jnp.maximum(peak, top)
        weights = [jnp.exp(tile - peak) for tile in scores]
        mass = None
        for w in weights:
            part = jnp.sum(w, axis=0, keepdims=True)
            mass = part if mass is None else mass + part
        rounded = jnp.concatenate([w.astype(BF) for w in weights], axis=0)
        mixed = (tn(values, rounded) / mass).astype(BF).astype(F32)
        delta = jnp.sum(u.astype(F32).T * mixed, axis=0, keepdims=True)
        for h in range(groups):
            out[:, h * HD : (h + 1) * HD] = mixed[:, h * BLOCK : (h + 1) * BLOCK].T.astype(BF)
        inverse = 1.0 / mass
        slopes = nt(values, u)
        chances = []
        pulls = []
        for d in range(DEPTH):
            p = weights[d] * inverse
            chances.append(p.astype(BF))
            pulls.append((p * (slopes[d * BLOCK : (d + 1) * BLOCK] - delta)).astype(BF))
        chances = jnp.concatenate(chances, axis=0)
        pulls = jnp.concatenate(pulls, axis=0)
        turned = tn(keys, pulls) * SCALE
        for h in range(groups):
            out[:, width + h * HD : width + (h + 1) * HD] = (
                turned[:, h * BLOCK : (h + 1) * BLOCK].T.astype(BF)
            )
        v_part = nn(chances, u)
        k_part = nn(pulls, q) * SCALE
        for d in range(DEPTH):
            low = d * BLOCK
            total[slots[d], :, :HD] += k_part[low : low + BLOCK]
            total[slots[d], :, HD:] += v_part[low : low + BLOCK]

        @pl.when(step == 3)
        def _():
            for outer in range(4):

                def fill(i, carry, outer=outer):
                    k_slot = t[AT_DENSE + outer * 16 + i]
                    v_slot = t[AT_DENSE + (i // 4) * 16 + outer * 4 + i % 4]
                    k = total[k_slot, :, :HD]
                    v = total[v_slot, :, HD:]
                    k_outs[outer][i] = k.astype(k_outs[outer].dtype)
                    v_outs[outer][i] = v.astype(v_outs[outer].dtype)
                    return carry

                lax.fori_loop(0, 16, fill, 0)

    mine = pl.BlockSpec((BLOCK, width), lambda i, t: (jnp.minimum(i, 1), t[AT_CORE]))
    peer = pl.BlockSpec((BLOCK, width), lambda i, t: (jnp.maximum(i - 2, 0), 0))
    rows = pl.BlockSpec((BLOCK, 2 * width), lambda i, t: (i, 0))

    def full(shape):
        return pl.BlockSpec(
            shape, lambda i, t: (0,) * len(shape), pipeline_mode=pl.Buffered(1)
        )

    def held(shape):
        return pl.BlockSpec(shape, lambda i, t: (0,) * len(shape))

    wide = (16, BLOCK, HD)
    grads = [(wide, F32)] + [(wide, BF)] * 3
    return pl.pallas_call(
        body,
        grid_spec=pltpu.PrefetchScalarGridSpec(
            num_scalar_prefetch=1,
            grid=(4,),
            in_specs=[mine, peer, mine, peer] + [full(p.shape) for p in pieces],
            out_specs=[rows] + [held(s) for s, _ in grads + grads],
            scratch_shapes=[
                pltpu.VMEM((SLOTS, BLOCK, 2 * HD), BF),
                pltpu.VMEM((SLOTS + 1, BLOCK, 2 * HD), F32),
                pltpu.VMEM((lanes, HD), BF),
                pltpu.VMEM((lanes, HD), BF),
            ],
        ),
        out_shape=[jax.ShapeDtypeStruct((4 * BLOCK, 2 * width), BF)]
        + [jax.ShapeDtypeStruct(s, d) for s, d in grads + grads],
        compiler_params=params(36),
        name="attend",
    )(table, queries, query_peer, upstream, upstream_peer, *pieces)


def combine(sums):
    def body(*refs):
        for side_of in range(2):
            home, a, b, c = refs[4 * side_of : 4 * side_of + 4]
            outs = refs[8 + 4 * side_of : 12 + 4 * side_of]
            rows = outs[0].shape[0]
            for k in range(4):
                at = slice(k * rows, (k + 1) * rows)
                outs[k][...] = (
                    home[at] + a[at].astype(F32) + b[at].astype(F32) + c[at].astype(F32)
                )

    shape = sums[0].shape
    part = (shape[0] // 4,) + shape[1:]
    return pl.pallas_call(
        body,
        in_specs=[pl.BlockSpec(memory_space=pltpu.VMEM)] * 8,
        out_specs=[pl.BlockSpec(memory_space=pltpu.VMEM)] * 8,
        out_shape=[jax.ShapeDtypeStruct(part, F32)] * 8,
        compiler_params=params(12),
        name="combine",
    )(*sums)


def finish_grads(sums, cosine, sine):
    rows = 4 * BLOCK

    def body(*refs):
        ks, vs = refs[:4], refs[4:8]
        cs, sn, every, away = refs[8:]
        key = (ks[0][...] + ks[1][...] + ks[2][...] + ks[3][...]).reshape(rows, HD)
        value = (vs[0][...] + vs[1][...] + vs[2][...] + vs[3][...]).reshape(rows, HD)
        key = key * cs[...] - pltpu.roll(key, HD // 2, 1) * sn[...]
        both = jnp.concatenate([key.astype(BF), value.astype(BF)], axis=1)
        every[...] = both
        away[...] = both[rows // 2 :]

    return pl.pallas_call(
        body,
        in_specs=[pl.BlockSpec(memory_space=pltpu.VMEM)] * 10,
        out_specs=[pl.BlockSpec(memory_space=pltpu.VMEM)] * 2,
        out_shape=[
            jax.ShapeDtypeStruct((rows, 2 * HD), BF),
            jax.ShapeDtypeStruct((rows // 2, 2 * HD), BF),
        ],
        compiler_params=params(8),
        name="finish_grads",
    )(*sums, cosine, sine)


def finish_weights(sums):
    share = sums[0].shape[1]

    def body(*refs):
        ks, vs = refs[:4], refs[4:8]
        for row, out in enumerate(refs[8:]):
            out[:, :HD] = ks[0][row] + ks[1][row] + ks[2][row] + ks[3][row]
            out[:, HD:] = vs[0][row] + vs[1][row] + vs[2][row] + vs[3][row]

    return pl.pallas_call(
        body,
        in_specs=[pl.BlockSpec(memory_space=pltpu.VMEM)] * 8,
        out_specs=[pl.BlockSpec(memory_space=pltpu.VMEM)] * 2,
        out_shape=[jax.ShapeDtypeStruct((share, 2 * HD), F32)] * 2,
        compiler_params=params(6),
        name="finish_weights",
    )(*sums)


def input_partials(place, mine, other, key_weight, value_weight):
    rows = other.shape[0]
    cols = key_weight.shape[1]
    width = key_weight.shape[0] // 4

    def body(p, a, b, kw, vw, *outs):
        swap = p[4] == 1
        first = jnp.where(swap, b[...], a[...])
        second = jnp.where(swap, a[...], b[...])
        key = jnp.concatenate([first[:, :HD], second[:, :HD]], axis=1)
        value = jnp.concatenate([first[:, HD:], second[:, HD:]], axis=1)
        result = (nt(key, kw[...]) + nt(value, vw[...])).astype(BF)
        for k in range(4):

            @pl.when(pl.program_id(0) == k)
            def _(k=k):
                outs[k][...] = result

    grads = pl.BlockSpec((rows, 2 * HD), lambda i, p: (0, 0))
    weight = pl.BlockSpec((width, cols), lambda i, p: (p[5 + i], 0))
    out = pl.BlockSpec((rows, width), lambda i, p: (0, 0))
    return pl.pallas_call(
        body,
        grid_spec=pltpu.PrefetchScalarGridSpec(
            num_scalar_prefetch=1,
            grid=(4,),
            in_specs=[grads, grads, weight, weight],
            out_specs=[out] * 4,
        ),
        out_shape=[jax.ShapeDtypeStruct((rows, width), BF)] * 4,
        compiler_params=params(10),
        name="input_partials",
    )(place, mine, other, key_weight, value_weight)


def weight_partials(place, grads, own, peer):
    width = own[0].shape[1]
    share = width // 8

    def body(p, g, *refs):
        mine, other = refs[:7], refs[7:14]
        k_outs, v_outs, result = refs[14:18], refs[18:22], refs[22]
        core = p[4]
        grad = g[...]
        for piece in range(4):
            at = slice(max(2 * piece - 1, 0), 2 * piece + 1)
            rows = mine[at] + other[at]
            features = jnp.concatenate([r[...] for r in rows], axis=0)
            result[...] = tn(features, grad)
            line = p[9 + piece]
            for dx in range(4):
                base = p[13 + dx] * (2 * share)
                for r in range(2):
                    start = pl.multiple_of(base + ((core + r) % 2) * share, 16)
                    value = result[pl.ds(start, share), :]
                    k_outs[dx][line * 2 + r] = value[:, :HD].astype(k_outs[dx].dtype)
                    for dy in range(4):

                        @pl.when(line == dy)
                        def _(dy=dy, dx=dx, r=r, value=value):
                            v_outs[dy][dx * 2 + r] = value[:, HD:].astype(v_outs[dy].dtype)

    wide = (8, share, HD)
    shapes = [(wide, F32)] + [(wide, BF)] * 3
    return pl.pallas_call(
        body,
        in_specs=[pl.BlockSpec(memory_space=pltpu.SMEM)]
        + [pl.BlockSpec(memory_space=pltpu.VMEM)] * 15,
        out_specs=[pl.BlockSpec(memory_space=pltpu.VMEM)] * 8,
        out_shape=[jax.ShapeDtypeStruct(s, d) for s, d in shapes + shapes],
        scratch_shapes=[pltpu.VMEM((width, 2 * HD), F32)],
        compiler_params=params(16),
        name="weight_partials",
    )(place, grads, *own, *peer)


def mover(axis, pairs):
    return lambda value: lax.ppermute(value, axis, pairs)


def ring_gather(first, second, ahead, behind):
    back_first = ahead(first)
    next_second = behind(second)
    back_second = ahead(second)
    next_first = behind(first)
    far_first = ahead(back_first)
    far_second = behind(next_second)
    return [
        first,
        second,
        back_first,
        back_second,
        next_first,
        next_second,
        far_first,
        far_second,
    ]


def send_all(values, ahead, behind, across):
    home, back, forth, far = values
    near = ahead(forth)
    distant = across(far)
    other = behind(back)
    return [home, near, other, distant]


def program(hidden, queries, key_weight, value_weight, parents, upstream):
    place_ctx = lax.axis_index("ctx")
    tp = lax.axis_index("tp")
    core = place_ctx % 2
    x = (place_ctx // 2) % 4
    y = place_ctx // 8
    xn = mover("ctx", [(i, i // 8 * 8 + (i + 2) % 8) for i in range(32)])
    xb = mover("ctx", [(i, i // 8 * 8 + (i - 2) % 8) for i in range(32)])
    yn = mover("ctx", [(i, (i + 8) % 32) for i in range(32)])
    yb = mover("ctx", [(i, (i - 8) % 32) for i in range(32)])
    swap = mover("ctx", [(i, i ^ 1) for i in range(32)])
    zn = mover("tp", [(i, (i + 1) % 4) for i in range(4)])
    zb = mover("tp", [(i, (i - 1) % 4) for i in range(4)])
    x2 = mover("ctx", [(i, i // 8 * 8 + (i + 4) % 8) for i in range(32)])
    y2 = mover("ctx", [(i, (i + 16) % 32) for i in range(32)])
    z2 = mover("tp", [(i, (i + 2) % 4) for i in range(4)])

    local_rows = hidden.shape[0]
    half_rows = local_rows // 2
    table, place, depths = device_tables(
        parents, jnp.stack([y, x, core, tp]).astype(jnp.int32)
    )
    cosine, sine = rope_tables(depths)

    width = queries.shape[1] // 2
    top = hidden[:half_rows]
    low = hidden[half_rows:]
    left_top = zn(top)
    right_low = zb(low)
    left_low = zn(low)
    right_top = zb(top)
    far_top = zn(left_top)
    far_low = zb(right_low)
    query_peer = swap(lax.dynamic_slice_in_dim(queries, (1 - core) * width, width, 1))
    upstream_peer = swap(lax.dynamic_slice_in_dim(upstream, (1 - core) * width, width, 1))
    hidden_peer = swap(hidden)
    place, hidden_peer, query_peer, upstream_peer = lax.optimization_barrier(
        (place, hidden_peer, query_peer, upstream_peer)
    )
    key_sum, value_sum = project_near(
        place, hidden, left_top, left_low, right_top, right_low, key_weight, value_weight
    )
    keep, send = project_far(
        place, far_top, far_low, key_weight, value_weight, key_sum, value_sum, cosine, sine
    )
    other = swap(send)
    mine_line = pack(keep, xn(keep), xb(keep), x2(keep))
    other_line = pack(other, yn(other), yb(other), y2(other))
    pieces = ring_gather(*mine_line, yn, yb) + ring_gather(*other_line, xn, xb)

    near_features = [left_top, left_low, right_top, right_low, far_top, far_low]
    own_features = [hidden, *near_features]
    peer_features = [hidden_peer] + [swap(f) for f in near_features]
    pieces, peer_features = lax.optimization_barrier((pieces, peer_features))

    out, *slot_grads = attend(table, queries, query_peer, upstream, upstream_peer, pieces)
    sums = combine(
        send_all(slot_grads[:4], xn, xb, x2) + send_all(slot_grads[4:], yn, yb, y2)
    )
    grads, grads_away = finish_grads(
        send_all(sums[:4], yn, yb, y2) + send_all(sums[4:], xn, xb, x2), cosine, sine
    )
    grads_other = swap(grads_away)
    grads, grads_other = lax.optimization_barrier((grads, grads_other))

    out_other = swap(out[local_rows:])

    def assemble(a, b):
        first = jnp.where(core == 0, a, b)
        second = jnp.where(core == 0, b, a)
        return jnp.concatenate([first, second], axis=1)

    attention = assemble(out[:local_rows, :width], out_other[:, :width])
    query_grad = assemble(out[:local_rows, width:], out_other[:, width:])

    w_parts = weight_partials(place, grads, own_features, peer_features)
    w_sent = send_all(w_parts[:4], xn, xb, x2) + send_all(w_parts[4:], yn, yb, y2)
    parts = input_partials(place, grads, grads_other, key_weight, value_weight)
    _, from_back, from_next, from_far = send_all(parts, zn, zb, z2)
    hidden_grad = (
        parts[0].astype(F32)
        + from_back.astype(F32)
        + from_next.astype(F32)
        + from_far.astype(F32)
    ).astype(BF)
    w_sums = combine(w_sent)
    both, both_away = finish_weights(
        send_all(w_sums[:4], yn, yb, y2) + send_all(w_sums[4:], xn, xb, x2)
    )
    both_other = swap(both_away)
    key_weight_grad, value_weight_grad = join_weights(place, both, both_other)
    return (attention, query_grad, hidden_grad, key_weight_grad, value_weight_grad)


def solution(mesh):
    return jax.shard_map(
        program,
        mesh=mesh,
        in_specs=(
            P("ctx", "tp"),
            P("ctx", "tp"),
            P(None, "tp"),
            P(None, "tp"),
            P(),
            P("ctx", "tp"),
        ),
        out_specs=(P("ctx", "tp"), P("ctx", "tp"), P("ctx", "tp"), P("ctx", "tp"), P("ctx", "tp")),
        check_vma=False,
    )
```

```python
import math

import jax
import jax.numpy as jnp
from jax import lax
from jax.experimental import pallas as pl
from jax.experimental.pallas import tpu as pltpu
from jax.sharding import PartitionSpec as P

HD = 128
BLOCK = 128
DEPTH = 8
THETA = 1000000.0
NEGATIVE = -1e30
BF = jnp.bfloat16
F32 = jnp.float32
SCALE = 1.0 / math.sqrt(HD)
STACK = DEPTH - 1
SLOTS = STACK + 4
OFFSETS = (0, 3, 1, 2)


def side(delta):
    return jnp.where(delta == 0, 0, jnp.where(delta == 3, 1, jnp.where(delta == 1, 2, 3)))


def device_tables(parents, position):
    block_total = parents.shape[0]

    def body(links, where, table, place, depths, level):
        y, x, core, tp = where[0], where[1], where[2], where[3]
        first = 16 * y + 4 * x
        level[0] = 0

        def descend(b, carry):
            level[b] = level[links[b]] + 1
            return carry

        lax.fori_loop(1, block_total, descend, 0)
        place[0] = tp
        place[1] = (tp + 3) % 4
        place[2] = (tp + 1) % 4
        place[3] = (tp + 2) % 4
        place[4] = core
        for k, o in enumerate(OFFSETS):
            place[5 + k] = (tp + o) % 4
            place[9 + k] = side((tp + o - y + 4) % 4)
            place[13 + k] = (x + o) % 4
        table[AT_CORE] = core

        def blank(i, carry):
            table[AT_DENSE + i] = SLOTS
            return carry

        lax.fori_loop(0, 64, blank, 0)
        for r in range(4):
            table[AT_DENSE + r] = STACK + r
            block = first + (2 * core + r) % 4
            own_depth = level[block]
            depths[r] = own_depth
            table[AT_DEPTH + r] = own_depth
            node = block
            for d in range(DEPTH - 1, -1, -1):
                live = d <= own_depth
                slot = jnp.where(node >= first, STACK + (node - first + 4 - 2 * core) % 4, d)
                table[AT_SLOT + r * DEPTH + d] = jnp.where(live, slot, STACK + r)
                node = jnp.where(live, jnp.maximum(links[node], 0), node)
        lead_depth = level[first]
        node = first
        for d in range(STACK - 1, -1, -1):
            live = d < lead_depth
            node = jnp.where(live, jnp.maximum(links[node], 0), node)
            column = side((node // 4 + 4 - x) % 4)
            line = side((node // 16 + 4 - y) % 4)
            same = (node // 2) % 2 == core
            parity = node % 2
            outer = jnp.where(same, line, column)
            inner = jnp.where(same, column, line)
            piece = jnp.where(same, 0, 8) + outer * 2 + parity
            table[d] = jnp.where(live, piece, -1)
            table[AT_PLACE + d] = jnp.where(live, inner, 0)
            spot = AT_DENSE + (column * 4 + line) * 4 + (node + 4 - 2 * core) % 4

            @pl.when(live)
            def _(spot=spot, d=d):
                table[spot] = d

    smem = pl.BlockSpec(memory_space=pltpu.SMEM)
    return pl.pallas_call(
        body,
        in_specs=[smem, smem],
        out_specs=[smem] * 3,
        out_shape=[
            jax.ShapeDtypeStruct((AT_CORE + 1,), jnp.int32),
            jax.ShapeDtypeStruct((17,), jnp.int32),
            jax.ShapeDtypeStruct((4,), jnp.int32),
        ],
        scratch_shapes=[pltpu.SMEM((block_total,), jnp.int32)],
        name="device_tables",
    )(parents, position)


AT_PLACE = STACK
AT_DEPTH = 2 * STACK
AT_SLOT = AT_DEPTH + 4
AT_DENSE = AT_SLOT + 4 * DEPTH
AT_CORE = AT_DENSE + 64


def rope_tables(depths):
    offset = jnp.arange(BLOCK, dtype=jnp.int32)
    position = (depths[:, None] * BLOCK + offset[None, :]).astype(F32)
    frequency = jnp.exp(jnp.arange(HD // 2, dtype=F32) * (-2.0 * math.log(THETA) / HD))
    angles = (position[:, :, None] * frequency[None, None, :]).reshape(4 * BLOCK, HD // 2)
    cosine, sine = jnp.cos(angles), jnp.sin(angles)
    return (
        jnp.concatenate([cosine, cosine], axis=-1),
        jnp.concatenate([-sine, sine], axis=-1),
    )


def nn(a, b):
    return jnp.dot(a, b, preferred_element_type=F32)


def nt(a, b):
    return lax.dot_general(a, b, (((1,), (1,)), ((), ())), preferred_element_type=F32)


def tn(a, b):
    return lax.dot_general(a, b, (((0,), (0,)), ((), ())), preferred_element_type=F32)


def params(mib):
    return pltpu.CompilerParams(vmem_limit_bytes=mib * 1024 * 1024)


def halve(value):
    half = value.shape[0] // 2

    def body(source, top, low, sems):
        copies = [
            pltpu.make_async_copy(source.at[pl.ds(k * half, half)], out, sems.at[k])
            for k, out in enumerate((top, low))
        ]
        for copy in copies:
            copy.start()
        for copy in copies:
            copy.wait()

    anywhere = pl.BlockSpec(memory_space=pl.ANY)
    return pl.pallas_call(
        body,
        in_specs=[anywhere],
        out_specs=[anywhere] * 2,
        out_shape=[jax.ShapeDtypeStruct((half, value.shape[1]), value.dtype)] * 2,
        scratch_shapes=[pltpu.SemaphoreType.DMA((2,))],
        name="halve",
    )(value)


def project_near(place, own, left_top, left_low, right_top, right_low, key_weight, value_weight):
    rows, width = own.shape
    cols = key_weight.shape[1]

    def body(place_ref, a, bt, bl, ct, cl, ka, kb, kc, va, vb, vc, key_out, value_out):
        b = jnp.concatenate([bt[...], bl[...]], axis=0)
        c = jnp.concatenate([ct[...], cl[...]], axis=0)
        key_out[...] = nn(a[...], ka[...]) + nn(b, kb[...]) + nn(c, kc[...])
        value_out[...] = nn(a[...], va[...]) + nn(b, vb[...]) + nn(c, vc[...])

    whole = pl.BlockSpec((rows, width), lambda i, p: (0, 0))
    half = pl.BlockSpec((rows // 2, width), lambda i, p: (0, 0))
    weights = [pl.BlockSpec((width, cols), lambda i, p, k=k: (p[k], 0)) for k in range(3)]
    out = pl.BlockSpec((rows, cols), lambda i, p: (0, 0))
    return pl.pallas_call(
        body,
        grid_spec=pltpu.PrefetchScalarGridSpec(
            num_scalar_prefetch=1,
            grid=(1,),
            in_specs=[whole] + [half] * 4 + weights + weights,
            out_specs=[out, out],
        ),
        out_shape=[jax.ShapeDtypeStruct((rows, cols), F32)] * 2,
        compiler_params=params(18),
        name="project_near",
    )(
        place,
        own,
        left_top,
        left_low,
        right_top,
        right_low,
        *([key_weight] * 3),
        *([value_weight] * 3),
    )


def pack(own, back, forth, far):
    def body(a, b, c, d, first, second):
        for k, ref in enumerate((a, b, c, d)):
            first[k] = ref[:BLOCK]
            second[k] = ref[BLOCK:]

    return pl.pallas_call(
        body,
        in_specs=[pl.BlockSpec(memory_space=pltpu.VMEM)] * 4,
        out_specs=[pl.BlockSpec(memory_space=pltpu.VMEM)] * 2,
        out_shape=[jax.ShapeDtypeStruct((4, BLOCK, 2 * HD), BF)] * 2,
        compiler_params=params(3),
        name="pack",
    )(own, back, forth, far)


def join_weights(place, mine, other):
    share = mine.shape[0]

    def body(p, a, b, key, value):
        swap = p[4] == 1
        first = jnp.where(swap, b[...], a[...])
        second = jnp.where(swap, a[...], b[...])
        key[:, :HD] = first[:, :HD]
        key[:, HD:] = second[:, :HD]
        value[:, :HD] = first[:, HD:]
        value[:, HD:] = second[:, HD:]

    return pl.pallas_call(
        body,
        in_specs=[pl.BlockSpec(memory_space=pltpu.SMEM)]
        + [pl.BlockSpec(memory_space=pltpu.VMEM)] * 2,
        out_specs=[pl.BlockSpec(memory_space=pltpu.VMEM)] * 2,
        out_shape=[jax.ShapeDtypeStruct((share, 2 * HD), F32)] * 2,
        compiler_params=params(2),
        name="join_weights",
    )(place, mine, other)


def project_far(place, top, bottom, key_weight, value_weight, key_sum, value_sum, cosine, sine):
    rows, cols = key_sum.shape
    width = top.shape[1]
    half = rows // 2

    def body(p, a, b, kw, vw, ks, vs, cs, sn, keep, send):
        far = jnp.concatenate([a[...], b[...]], axis=0)
        key = ks[...] + nn(far, kw[...])
        value = vs[...] + nn(far, vw[...])
        heads = []
        for h in range(2):
            part = key[:, h * HD : (h + 1) * HD]
            turned = part * cs[...] + pltpu.roll(part, HD // 2, 1) * sn[...]
            heads.append(
                jnp.concatenate([turned, value[:, h * HD : (h + 1) * HD]], axis=1).astype(BF)
            )
        swap = p[4] == 1
        keep[...] = jnp.where(swap, heads[1], heads[0])
        send[...] = jnp.where(swap, heads[0], heads[1])

    weight = pl.BlockSpec((width, cols), lambda i, p: (p[3], 0))
    part = pl.BlockSpec((half, width), lambda i, p: (0, 0))
    sums = pl.BlockSpec((rows, cols), lambda i, p: (0, 0))
    angle = pl.BlockSpec((rows, HD), lambda i, p: (0, 0))
    return pl.pallas_call(
        body,
        grid_spec=pltpu.PrefetchScalarGridSpec(
            num_scalar_prefetch=1,
            grid=(1,),
            in_specs=[part, part, weight, weight, sums, sums, angle, angle],
            out_specs=[sums, sums],
        ),
        out_shape=[jax.ShapeDtypeStruct((rows, cols), BF)] * 2,
        compiler_params=params(8),
        name="project_far",
    )(place, top, bottom, key_weight, value_weight, key_sum, value_sum, cosine, sine)


def attend(table, queries, query_peer, upstream, upstream_peer, pieces):
    groups = queries.shape[1] // (2 * HD)
    width = groups * HD
    lanes = groups * BLOCK

    def body(t, q_own, q_far, u_own, u_far, *refs):
        parts = refs[:16]
        k_outs = refs[17:21]
        v_outs = refs[21:25]
        out = refs[16]
        kv, total, q_rows, u_rows = refs[25:]
        step = pl.program_id(0)

        @pl.when(step == 0)
        def _():
            for s in range(STACK):
                for index in range(16):

                    @pl.when(t[s] == index)
                    def _(s=s, index=index):
                        kv[s] = parts[index][t[AT_PLACE + s]]

            for r in range(4):
                kv[STACK + r] = parts[r if r < 2 else 6 + r][0]
            total[...] = jnp.zeros(total.shape, F32)

        own = step < 2
        q = jnp.where(own, q_own[...], q_far[...])
        u = jnp.where(own, u_own[...], u_far[...])
        for h in range(groups):
            q_rows[h * BLOCK : (h + 1) * BLOCK] = q[:, h * HD : (h + 1) * HD]
            u_rows[h * BLOCK : (h + 1) * BLOCK] = u[:, h * HD : (h + 1) * HD]
        q = q_rows[...]
        u = u_rows[...]
        depth = t[AT_DEPTH + step]
        slots = [t[AT_SLOT + step * DEPTH + d] for d in range(DEPTH)]
        keys = jnp.concatenate([kv[s, :, :HD] for s in slots], axis=0)
        values = jnp.concatenate([kv[s, :, HD:] for s in slots], axis=0)
        ahead = lax.broadcasted_iota(jnp.int32, (BLOCK, lanes), 0) - (
            lax.broadcasted_iota(jnp.int32, (BLOCK, lanes), 1) % BLOCK
        )
        raw = nt(keys, q)
        scores = []
        peak = None
        for d in range(DEPTH):
            reach = jnp.where(d < depth, BLOCK, jnp.where(d == depth, 0, -BLOCK))
            tile = jnp.where(
                ahead <= reach, raw[d * BLOCK : (d + 1) * BLOCK] * SCALE, NEGATIVE
            )
            scores.append(tile)
            top = jnp.max(tile, axis=0, keepdims=True)
            peak = top if peak is None else jnp.maximum(peak, top)
        weights = [jnp.exp(tile - peak) for tile in scores]
        mass = None
        for w in weights:
            part = jnp.sum(w, axis=0, keepdims=True)
            mass = part if mass is None else mass + part
        rounded = jnp.concatenate([w.astype(BF) for w in weights], axis=0)
        mixed = (tn(values, rounded) / mass).astype(BF).astype(F32)
        delta = jnp.sum(u.astype(F32).T * mixed, axis=0, keepdims=True)
        for h in range(groups):
            out[:, h * HD : (h + 1) * HD] = mixed[:, h * BLOCK : (h + 1) * BLOCK].T.astype(BF)
        inverse = 1.0 / mass
        slopes = nt(values, u)
        chances = []
        pulls = []
        for d in range(DEPTH):
            p = weights[d] * inverse
            chances.append(p.astype(BF))
            pulls.append((p * (slopes[d * BLOCK : (d + 1) * BLOCK] - delta)).astype(BF))
        chances = jnp.concatenate(chances, axis=0)
        pulls = jnp.concatenate(pulls, axis=0)
        turned = tn(keys, pulls) * SCALE
        for h in range(groups):
            out[:, width + h * HD : width + (h + 1) * HD] = (
                turned[:, h * BLOCK : (h + 1) * BLOCK].T.astype(BF)
            )
        v_part = nn(chances, u)
        k_part = nn(pulls, q) * SCALE
        for d in range(DEPTH):
            low = d * BLOCK
            total[slots[d], :, :HD] += k_part[low : low + BLOCK]
            total[slots[d], :, HD:] += v_part[low : low + BLOCK]

        @pl.when(step == 3)
        def _():
            for outer in range(4):

                def fill(i, carry, outer=outer):
                    k_slot = t[AT_DENSE + outer * 16 + i]
                    v_slot = t[AT_DENSE + (i // 4) * 16 + outer * 4 + i % 4]
                    k = total[k_slot, :, :HD]
                    v = total[v_slot, :, HD:]
                    k_outs[outer][i] = k.astype(k_outs[outer].dtype)
                    v_outs[outer][i] = v.astype(v_outs[outer].dtype)
                    return carry

                lax.fori_loop(0, 16, fill, 0)

    mine = pl.BlockSpec((BLOCK, width), lambda i, t: (jnp.minimum(i, 1), t[AT_CORE]))
    peer = pl.BlockSpec((BLOCK, width), lambda i, t: (jnp.maximum(i - 2, 0), 0))
    rows = pl.BlockSpec((BLOCK, 2 * width), lambda i, t: (i, 0))

    def full(shape):
        return pl.BlockSpec(
            shape, lambda i, t: (0,) * len(shape), pipeline_mode=pl.Buffered(1)
        )

    def held(shape):
        return pl.BlockSpec(shape, lambda i, t: (0,) * len(shape))

    wide = (16, BLOCK, HD)
    grads = [(wide, F32)] + [(wide, BF)] * 3
    return pl.pallas_call(
        body,
        grid_spec=pltpu.PrefetchScalarGridSpec(
            num_scalar_prefetch=1,
            grid=(4,),
            in_specs=[mine, peer, mine, peer] + [full(p.shape) for p in pieces],
            out_specs=[rows] + [held(s) for s, _ in grads + grads],
            scratch_shapes=[
                pltpu.VMEM((SLOTS, BLOCK, 2 * HD), BF),
                pltpu.VMEM((SLOTS + 1, BLOCK, 2 * HD), F32),
                pltpu.VMEM((lanes, HD), BF),
                pltpu.VMEM((lanes, HD), BF),
            ],
        ),
        out_shape=[jax.ShapeDtypeStruct((4 * BLOCK, 2 * width), BF)]
        + [jax.ShapeDtypeStruct(s, d) for s, d in grads + grads],
        compiler_params=params(36),
        name="attend",
    )(table, queries, query_peer, upstream, upstream_peer, *pieces)


def combine(sums):
    def body(*refs):
        for side_of in range(2):
            home, a, b, c = refs[4 * side_of : 4 * side_of + 4]
            outs = refs[8 + 4 * side_of : 12 + 4 * side_of]
            rows = outs[0].shape[0]
            for k in range(4):
                at = slice(k * rows, (k + 1) * rows)
                outs[k][...] = (
                    home[at] + a[at].astype(F32) + b[at].astype(F32) + c[at].astype(F32)
                )

    shape = sums[0].shape
    part = (shape[0] // 4,) + shape[1:]
    return pl.pallas_call(
        body,
        in_specs=[pl.BlockSpec(memory_space=pltpu.VMEM)] * 8,
        out_specs=[pl.BlockSpec(memory_space=pltpu.VMEM)] * 8,
        out_shape=[jax.ShapeDtypeStruct(part, F32)] * 8,
        compiler_params=params(8),
        name="combine",
    )(*sums)


def finish_grads(sums, cosine, sine):
    rows = 4 * BLOCK

    def body(*refs):
        ks, vs = refs[:4], refs[4:8]
        cs, sn, every, away = refs[8:]
        key = (ks[0][...] + ks[1][...] + ks[2][...] + ks[3][...]).reshape(rows, HD)
        value = (vs[0][...] + vs[1][...] + vs[2][...] + vs[3][...]).reshape(rows, HD)
        key = key * cs[...] - pltpu.roll(key, HD // 2, 1) * sn[...]
        both = jnp.concatenate([key.astype(BF), value.astype(BF)], axis=1)
        every[...] = both
        away[...] = both[rows // 2 :]

    return pl.pallas_call(
        body,
        in_specs=[pl.BlockSpec(memory_space=pltpu.VMEM)] * 10,
        out_specs=[pl.BlockSpec(memory_space=pltpu.VMEM)] * 2,
        out_shape=[
            jax.ShapeDtypeStruct((rows, 2 * HD), BF),
            jax.ShapeDtypeStruct((rows // 2, 2 * HD), BF),
        ],
        compiler_params=params(5),
        name="finish_grads",
    )(*sums, cosine, sine)


def finish_weights(sums):
    share = sums[0].shape[1]

    def body(*refs):
        ks, vs = refs[:4], refs[4:8]
        for row, out in enumerate(refs[8:]):
            out[:, :HD] = ks[0][row] + ks[1][row] + ks[2][row] + ks[3][row]
            out[:, HD:] = vs[0][row] + vs[1][row] + vs[2][row] + vs[3][row]

    return pl.pallas_call(
        body,
        in_specs=[pl.BlockSpec(memory_space=pltpu.VMEM)] * 8,
        out_specs=[pl.BlockSpec(memory_space=pltpu.VMEM)] * 2,
        out_shape=[jax.ShapeDtypeStruct((share, 2 * HD), F32)] * 2,
        compiler_params=params(4),
        name="finish_weights",
    )(*sums)


def input_partials(place, mine, other, key_weight, value_weight):
    rows = other.shape[0]
    cols = key_weight.shape[1]
    width = key_weight.shape[0] // 4

    def body(p, a, b, kw, vw, *outs):
        swap = p[4] == 1
        first = jnp.where(swap, b[...], a[...])
        second = jnp.where(swap, a[...], b[...])
        key = jnp.concatenate([first[:, :HD], second[:, :HD]], axis=1)
        value = jnp.concatenate([first[:, HD:], second[:, HD:]], axis=1)
        result = (nt(key, kw[...]) + nt(value, vw[...])).astype(BF)
        for k in range(4):

            @pl.when(pl.program_id(0) == k)
            def _(k=k):
                outs[k][...] = result

    grads = pl.BlockSpec((rows, 2 * HD), lambda i, p: (0, 0))
    weight = pl.BlockSpec((width, cols), lambda i, p: (p[5 + i], 0))
    out = pl.BlockSpec((rows, width), lambda i, p: (0, 0), pipeline_mode=pl.Buffered(1))
    return pl.pallas_call(
        body,
        grid_spec=pltpu.PrefetchScalarGridSpec(
            num_scalar_prefetch=1,
            grid=(4,),
            in_specs=[grads, grads, weight, weight],
            out_specs=[out] * 4,
        ),
        out_shape=[jax.ShapeDtypeStruct((rows, width), BF)] * 4,
        compiler_params=params(7),
        name="input_partials",
    )(place, mine, other, key_weight, value_weight)


def flip(own, peer):
    width = own[0].shape[1]
    rows = 4 * BLOCK

    def body(*refs):
        mine, other, outs = refs[:7], refs[7:14], refs[14:]
        for piece in range(4):
            at = slice(max(2 * piece - 1, 0), 2 * piece + 1)
            features = jnp.concatenate([r[...] for r in mine[at] + other[at]], axis=0)
            outs[piece][...] = features.T

    return pl.pallas_call(
        body,
        in_specs=[pl.BlockSpec(memory_space=pltpu.VMEM)] * 14,
        out_specs=[pl.BlockSpec(memory_space=pltpu.VMEM)] * 4,
        out_shape=[jax.ShapeDtypeStruct((width, rows), BF)] * 4,
        compiler_params=params(12),
        name="flip",
    )(*own, *peer)


def weight_partials(place, grads, features):
    width = features[0].shape[0]
    share = width // 8

    def body(p, g, *refs):
        k_outs, v_outs, result = refs[4:8], refs[8:12], refs[12]
        core = p[4]
        grad = g[...]
        for piece in range(4):
            result[...] = nn(refs[piece][...], grad)
            line = p[9 + piece]
            for dx in range(4):
                base = p[13 + dx] * (2 * share)
                for r in range(2):
                    start = pl.multiple_of(base + ((core + r) % 2) * share, 16)
                    value = result[pl.ds(start, share), :]
                    k_outs[dx][line * 2 + r] = value[:, :HD].astype(k_outs[dx].dtype)
                    for dy in range(4):

                        @pl.when(line == dy)
                        def _(dy=dy, dx=dx, r=r, value=value):
                            v_outs[dy][dx * 2 + r] = value[:, HD:].astype(v_outs[dy].dtype)

    wide = (8, share, HD)
    shapes = [(wide, F32)] + [(wide, BF)] * 3
    return pl.pallas_call(
        body,
        in_specs=[pl.BlockSpec(memory_space=pltpu.SMEM)]
        + [pl.BlockSpec(memory_space=pltpu.VMEM)] * 5,
        out_specs=[pl.BlockSpec(memory_space=pltpu.VMEM)] * 8,
        out_shape=[jax.ShapeDtypeStruct(s, d) for s, d in shapes + shapes],
        scratch_shapes=[pltpu.VMEM((width, 2 * HD), F32)],
        compiler_params=params(11),
        name="weight_partials",
    )(place, grads, *features)


def mover(axis, pairs):
    return lambda value: lax.ppermute(value, axis, pairs)


def ring_gather(first, second, ahead, behind):
    back_first = ahead(first)
    next_second = behind(second)
    back_second = ahead(second)
    next_first = behind(first)
    far_first = ahead(back_first)
    far_second = behind(next_second)
    return [
        first,
        second,
        back_first,
        back_second,
        next_first,
        next_second,
        far_first,
        far_second,
    ]


def send_all(values, ahead, behind, across):
    home, back, forth, far = values
    near = ahead(forth)
    distant = across(far)
    other = behind(back)
    return [home, near, other, distant]


def program(hidden, queries, key_weight, value_weight, parents, upstream):
    place_ctx = lax.axis_index("ctx")
    tp = lax.axis_index("tp")
    core = place_ctx % 2
    x = (place_ctx // 2) % 4
    y = place_ctx // 8
    xn = mover("ctx", [(i, i // 8 * 8 + (i + 2) % 8) for i in range(32)])
    xb = mover("ctx", [(i, i // 8 * 8 + (i - 2) % 8) for i in range(32)])
    yn = mover("ctx", [(i, (i + 8) % 32) for i in range(32)])
    yb = mover("ctx", [(i, (i - 8) % 32) for i in range(32)])
    swap = mover("ctx", [(i, i ^ 1) for i in range(32)])
    zn = mover("tp", [(i, (i + 1) % 4) for i in range(4)])
    zb = mover("tp", [(i, (i - 1) % 4) for i in range(4)])
    x2 = mover("ctx", [(i, i // 8 * 8 + (i + 4) % 8) for i in range(32)])
    y2 = mover("ctx", [(i, (i + 16) % 32) for i in range(32)])
    z2 = mover("tp", [(i, (i + 2) % 4) for i in range(4)])

    local_rows = hidden.shape[0]
    table, place, depths = device_tables(
        parents, jnp.stack([y, x, core, tp]).astype(jnp.int32)
    )
    cosine, sine = rope_tables(depths)

    width = queries.shape[1] // 2
    top, low = halve(hidden)
    left_top = zn(top)
    right_low = zb(low)
    left_low = zn(low)
    right_top = zb(top)
    far_top = zn(left_top)
    far_low = zb(right_low)
    query_peer = swap(lax.dynamic_slice_in_dim(queries, (1 - core) * width, width, 1))
    upstream_peer = swap(lax.dynamic_slice_in_dim(upstream, (1 - core) * width, width, 1))
    hidden_peer = swap(hidden)
    place, hidden_peer, query_peer, upstream_peer = lax.optimization_barrier(
        (place, hidden_peer, query_peer, upstream_peer)
    )
    key_sum, value_sum = project_near(
        place, hidden, left_top, left_low, right_top, right_low, key_weight, value_weight
    )
    keep, send = project_far(
        place, far_top, far_low, key_weight, value_weight, key_sum, value_sum, cosine, sine
    )
    other = swap(send)
    mine_line = pack(keep, xn(keep), xb(keep), x2(keep))
    other_line = pack(other, yn(other), yb(other), y2(other))
    pieces = ring_gather(*mine_line, yn, yb) + ring_gather(*other_line, xn, xb)

    near_features = [left_top, left_low, right_top, right_low, far_top, far_low]
    own_features = [hidden, *near_features]
    peer_features = [hidden_peer]
    for feature in near_features:
        peer_features.append(swap(feature))
    features = flip(own_features, peer_features)

    out, *slot_grads = attend(table, queries, query_peer, upstream, upstream_peer, pieces)
    sums = combine(send_all(slot_grads[:4], xn, xb, x2) + send_all(slot_grads[4:], yn, yb, y2))
    grads, grads_away = finish_grads(
        send_all(sums[:4], yn, yb, y2) + send_all(sums[4:], xn, xb, x2), cosine, sine
    )
    grads_other = swap(grads_away)
    grads, grads_other = lax.optimization_barrier((grads, grads_other))

    out_other = swap(out[local_rows:])

    def assemble(a, b):
        first = jnp.where(core == 0, a, b)
        second = jnp.where(core == 0, b, a)
        return jnp.concatenate([first, second], axis=1)

    attention = assemble(out[:local_rows, :width], out_other[:, :width])
    query_grad = assemble(out[:local_rows, width:], out_other[:, width:])

    w_parts = weight_partials(place, grads, features)
    w_sent = send_all(w_parts[:4], xn, xb, x2) + send_all(w_parts[4:], yn, yb, y2)
    parts = input_partials(place, grads, grads_other, key_weight, value_weight)
    _, from_back, from_next, from_far = send_all(parts, zn, zb, z2)
    hidden_grad = (
        parts[0].astype(F32)
        + from_back.astype(F32)
        + from_next.astype(F32)
        + from_far.astype(F32)
    ).astype(BF)
    w_sums = combine(w_sent)
    both, both_away = finish_weights(
        send_all(w_sums[:4], yn, yb, y2) + send_all(w_sums[4:], xn, xb, x2)
    )
    both_other = swap(both_away)
    key_weight_grad, value_weight_grad = join_weights(place, both, both_other)
    return (attention, query_grad, hidden_grad, key_weight_grad, value_weight_grad)


def solution(mesh):
    return jax.shard_map(
        program,
        mesh=mesh,
        in_specs=(
            P("ctx", "tp"),
            P("ctx", "tp"),
            P(None, "tp"),
            P(None, "tp"),
            P(),
            P("ctx", "tp"),
        ),
        out_specs=(P("ctx", "tp"), P("ctx", "tp"), P("ctx", "tp"), P("ctx", "tp"), P("ctx", "tp")),
        check_vma=False,
    )
```

```python
import math

import jax
import jax.numpy as jnp
from jax import lax
from jax.experimental import pallas as pl
from jax.experimental.pallas import tpu as pltpu
from jax.sharding import PartitionSpec as P

HD = 128
BLOCK = 128
DEPTH = 8
THETA = 1000000.0
NEGATIVE = -1e30
BF = jnp.bfloat16
F32 = jnp.float32
SCALE = 1.0 / math.sqrt(HD)
STACK = DEPTH - 1
SLOTS = STACK + 4
OFFSETS = (0, 3, 1, 2)


def side(delta):
    return jnp.where(delta == 0, 0, jnp.where(delta == 3, 1, jnp.where(delta == 1, 2, 3)))


def device_tables(parents, position):
    block_total = parents.shape[0]

    def body(links, where, table, place, depths, level):
        y, x, core, tp = where[0], where[1], where[2], where[3]
        first = 16 * y + 4 * x
        level[0] = 0

        def descend(b, carry):
            level[b] = level[links[b]] + 1
            return carry

        lax.fori_loop(1, block_total, descend, 0)
        place[0] = tp
        place[1] = (tp + 3) % 4
        place[2] = (tp + 1) % 4
        place[3] = (tp + 2) % 4
        place[4] = core
        for k, o in enumerate(OFFSETS):
            place[5 + k] = (tp + o) % 4
            place[9 + k] = side((y + o - tp + 4) % 4)
            place[13 + k] = (x + o) % 4
        table[AT_CORE] = core

        def blank(i, carry):
            table[AT_DENSE + i] = SLOTS
            return carry

        lax.fori_loop(0, 64, blank, 0)
        for r in range(4):
            table[AT_DENSE + r] = STACK + r
            block = first + (2 * core + r) % 4
            own_depth = level[block]
            depths[r] = own_depth
            table[AT_DEPTH + r] = own_depth
            node = block
            for d in range(DEPTH - 1, -1, -1):
                live = d <= own_depth
                slot = jnp.where(node >= first, STACK + (node - first + 4 - 2 * core) % 4, d)
                table[AT_SLOT + r * DEPTH + d] = jnp.where(live, slot, STACK + r)
                node = jnp.where(live, jnp.maximum(links[node], 0), node)
        lead_depth = level[first]
        node = first
        for d in range(STACK - 1, -1, -1):
            live = d < lead_depth
            node = jnp.where(live, jnp.maximum(links[node], 0), node)
            column = side((node // 4 + 4 - x) % 4)
            line = side((node // 16 + 4 - y) % 4)
            same = (node // 2) % 2 == core
            parity = node % 2
            outer = jnp.where(same, line, column)
            inner = jnp.where(same, column, line)
            piece = jnp.where(same, 0, 8) + outer * 2 + parity
            table[d] = jnp.where(live, piece, -1)
            table[AT_PLACE + d] = jnp.where(live, inner, 0)
            spot = AT_DENSE + (column * 4 + line) * 4 + (node + 4 - 2 * core) % 4

            @pl.when(live)
            def _(spot=spot, d=d):
                table[spot] = d

    smem = pl.BlockSpec(memory_space=pltpu.SMEM)
    return pl.pallas_call(
        body,
        in_specs=[smem, smem],
        out_specs=[smem] * 3,
        out_shape=[
            jax.ShapeDtypeStruct((AT_CORE + 1,), jnp.int32),
            jax.ShapeDtypeStruct((17,), jnp.int32),
            jax.ShapeDtypeStruct((4,), jnp.int32),
        ],
        scratch_shapes=[pltpu.SMEM((block_total,), jnp.int32)],
        name="device_tables",
    )(parents, position)


AT_PLACE = STACK
AT_DEPTH = 2 * STACK
AT_SLOT = AT_DEPTH + 4
AT_DENSE = AT_SLOT + 4 * DEPTH
AT_CORE = AT_DENSE + 64


def rope_tables(depths):
    offset = jnp.arange(BLOCK, dtype=jnp.int32)
    position = (depths[:, None] * BLOCK + offset[None, :]).astype(F32)
    frequency = jnp.exp(jnp.arange(HD // 2, dtype=F32) * (-2.0 * math.log(THETA) / HD))
    angles = (position[:, :, None] * frequency[None, None, :]).reshape(4 * BLOCK, HD // 2)
    cosine, sine = jnp.cos(angles), jnp.sin(angles)
    return (
        jnp.concatenate([cosine, cosine], axis=-1),
        jnp.concatenate([-sine, sine], axis=-1),
    )


def nn(a, b):
    return jnp.dot(a, b, preferred_element_type=F32)


def nt(a, b):
    return lax.dot_general(a, b, (((1,), (1,)), ((), ())), preferred_element_type=F32)


def tn(a, b):
    return lax.dot_general(a, b, (((0,), (0,)), ((), ())), preferred_element_type=F32)


def params(mib):
    return pltpu.CompilerParams(vmem_limit_bytes=mib * 1024 * 1024)


def halve(value):
    half = value.shape[0] // 2

    def body(source, top, low):
        top[...] = source[:half]
        low[...] = source[half:]

    return pl.pallas_call(
        body,
        in_specs=[pl.BlockSpec(memory_space=pltpu.VMEM)],
        out_specs=[pl.BlockSpec(memory_space=pltpu.VMEM)] * 2,
        out_shape=[jax.ShapeDtypeStruct((half, value.shape[1]), value.dtype)] * 2,
        compiler_params=params(3),
        name="halve",
    )(value)


def project_near(place, own, left_top, left_low, right_top, right_low, key_weight, value_weight):
    rows, width = own.shape
    cols = key_weight.shape[1]

    def body(place_ref, a, bt, bl, ct, cl, ka, kb, kc, va, vb, vc, key_out, value_out):
        b = jnp.concatenate([bt[...], bl[...]], axis=0)
        c = jnp.concatenate([ct[...], cl[...]], axis=0)
        key_out[...] = nn(a[...], ka[...]) + nn(b, kb[...]) + nn(c, kc[...])
        value_out[...] = nn(a[...], va[...]) + nn(b, vb[...]) + nn(c, vc[...])

    whole = pl.BlockSpec((rows, width), lambda i, p: (0, 0))
    half = pl.BlockSpec((rows // 2, width), lambda i, p: (0, 0))
    weights = [pl.BlockSpec((width, cols), lambda i, p, k=k: (p[k], 0)) for k in range(3)]
    out = pl.BlockSpec((rows, cols), lambda i, p: (0, 0))
    return pl.pallas_call(
        body,
        grid_spec=pltpu.PrefetchScalarGridSpec(
            num_scalar_prefetch=1,
            grid=(1,),
            in_specs=[whole] + [half] * 4 + weights + weights,
            out_specs=[out, out],
        ),
        out_shape=[jax.ShapeDtypeStruct((rows, cols), F32)] * 2,
        compiler_params=params(18),
        name="project_near",
    )(
        place,
        own,
        left_top,
        left_low,
        right_top,
        right_low,
        *([key_weight] * 3),
        *([value_weight] * 3),
    )


def pack(own, back, forth, far):
    def body(a, b, c, d, first, second):
        for k, ref in enumerate((a, b, c, d)):
            first[k] = ref[:BLOCK]
            second[k] = ref[BLOCK:]

    return pl.pallas_call(
        body,
        in_specs=[pl.BlockSpec(memory_space=pltpu.VMEM)] * 4,
        out_specs=[pl.BlockSpec(memory_space=pltpu.VMEM)] * 2,
        out_shape=[jax.ShapeDtypeStruct((4, BLOCK, 2 * HD), BF)] * 2,
        compiler_params=params(3),
        name="pack",
    )(own, back, forth, far)


def join_weights(place, mine, other):
    share = mine.shape[0]

    def body(p, a, b, key, value):
        swap = p[4] == 1
        first = jnp.where(swap, b[...], a[...])
        second = jnp.where(swap, a[...], b[...])
        key[:, :HD] = first[:, :HD]
        key[:, HD:] = second[:, :HD]
        value[:, :HD] = first[:, HD:]
        value[:, HD:] = second[:, HD:]

    return pl.pallas_call(
        body,
        in_specs=[pl.BlockSpec(memory_space=pltpu.SMEM)]
        + [pl.BlockSpec(memory_space=pltpu.VMEM)] * 2,
        out_specs=[pl.BlockSpec(memory_space=pltpu.VMEM)] * 2,
        out_shape=[jax.ShapeDtypeStruct((share, 2 * HD), F32)] * 2,
        compiler_params=params(2),
        name="join_weights",
    )(place, mine, other)


def project_far(place, top, bottom, key_weight, value_weight, key_sum, value_sum, cosine, sine):
    rows, cols = key_sum.shape
    width = top.shape[1]
    half = rows // 2

    def body(p, a, b, kw, vw, ks, vs, cs, sn, keep, send):
        far = jnp.concatenate([a[...], b[...]], axis=0)
        key = ks[...] + nn(far, kw[...])
        value = vs[...] + nn(far, vw[...])
        heads = []
        for h in range(2):
            part = key[:, h * HD : (h + 1) * HD]
            turned = part * cs[...] + pltpu.roll(part, HD // 2, 1) * sn[...]
            heads.append(
                jnp.concatenate([turned, value[:, h * HD : (h + 1) * HD]], axis=1).astype(BF)
            )
        swap = p[4] == 1
        keep[...] = jnp.where(swap, heads[1], heads[0])
        send[...] = jnp.where(swap, heads[0], heads[1])

    weight = pl.BlockSpec((width, cols), lambda i, p: (p[3], 0))
    part = pl.BlockSpec((half, width), lambda i, p: (0, 0))
    sums = pl.BlockSpec((rows, cols), lambda i, p: (0, 0))
    angle = pl.BlockSpec((rows, HD), lambda i, p: (0, 0))
    return pl.pallas_call(
        body,
        grid_spec=pltpu.PrefetchScalarGridSpec(
            num_scalar_prefetch=1,
            grid=(1,),
            in_specs=[part, part, weight, weight, sums, sums, angle, angle],
            out_specs=[sums, sums],
        ),
        out_shape=[jax.ShapeDtypeStruct((rows, cols), BF)] * 2,
        compiler_params=params(8),
        name="project_far",
    )(place, top, bottom, key_weight, value_weight, key_sum, value_sum, cosine, sine)


def attend(table, queries, query_peer, upstream, upstream_peer, pieces):
    groups = queries.shape[1] // (2 * HD)
    width = groups * HD
    lanes = groups * BLOCK

    def body(t, q_own, q_far, u_own, u_far, *refs):
        parts = refs[:16]
        k_outs = refs[17:21]
        v_outs = refs[21:25]
        out = refs[16]
        kv, total, q_rows, u_rows = refs[25:]
        step = pl.program_id(0)

        @pl.when(step == 0)
        def _():
            for s in range(STACK):
                for index in range(16):

                    @pl.when(t[s] == index)
                    def _(s=s, index=index):
                        kv[s] = parts[index][t[AT_PLACE + s]]

            for r in range(4):
                kv[STACK + r] = parts[r if r < 2 else 6 + r][0]
            total[...] = jnp.zeros(total.shape, F32)

        own = step < 2
        q = jnp.where(own, q_own[...], q_far[...])
        u = jnp.where(own, u_own[...], u_far[...])
        for h in range(groups):
            q_rows[h * BLOCK : (h + 1) * BLOCK] = q[:, h * HD : (h + 1) * HD]
            u_rows[h * BLOCK : (h + 1) * BLOCK] = u[:, h * HD : (h + 1) * HD]
        q = q_rows[...]
        u = u_rows[...]
        depth = t[AT_DEPTH + step]
        slots = [t[AT_SLOT + step * DEPTH + d] for d in range(DEPTH)]
        keys = jnp.concatenate([kv[s, :, :HD] for s in slots], axis=0)
        values = jnp.concatenate([kv[s, :, HD:] for s in slots], axis=0)
        ahead = lax.broadcasted_iota(jnp.int32, (BLOCK, lanes), 0) - (
            lax.broadcasted_iota(jnp.int32, (BLOCK, lanes), 1) % BLOCK
        )
        raw = nt(keys, q)
        scores = []
        peak = None
        for d in range(DEPTH):
            reach = jnp.where(d < depth, BLOCK, jnp.where(d == depth, 0, -BLOCK))
            tile = jnp.where(
                ahead <= reach, raw[d * BLOCK : (d + 1) * BLOCK] * SCALE, NEGATIVE
            )
            scores.append(tile)
            top = jnp.max(tile, axis=0, keepdims=True)
            peak = top if peak is None else jnp.maximum(peak, top)
        weights = [jnp.exp(tile - peak) for tile in scores]
        mass = None
        for w in weights:
            part = jnp.sum(w, axis=0, keepdims=True)
            mass = part if mass is None else mass + part
        rounded = jnp.concatenate([w.astype(BF) for w in weights], axis=0)
        mixed = (tn(values, rounded) / mass).astype(BF).astype(F32)
        delta = jnp.sum(u.astype(F32).T * mixed, axis=0, keepdims=True)
        for h in range(groups):
            out[:, h * HD : (h + 1) * HD] = mixed[:, h * BLOCK : (h + 1) * BLOCK].T.astype(BF)
        inverse = 1.0 / mass
        slopes = nt(values, u)
        chances = []
        pulls = []
        for d in range(DEPTH):
            p = weights[d] * inverse
            chances.append(p.astype(BF))
            pulls.append((p * (slopes[d * BLOCK : (d + 1) * BLOCK] - delta)).astype(BF))
        chances = jnp.concatenate(chances, axis=0)
        pulls = jnp.concatenate(pulls, axis=0)
        turned = tn(keys, pulls) * SCALE
        for h in range(groups):
            out[:, width + h * HD : width + (h + 1) * HD] = (
                turned[:, h * BLOCK : (h + 1) * BLOCK].T.astype(BF)
            )
        v_part = nn(chances, u)
        k_part = nn(pulls, q) * SCALE
        for d in range(DEPTH):
            low = d * BLOCK
            total[slots[d], :, :HD] += k_part[low : low + BLOCK]
            total[slots[d], :, HD:] += v_part[low : low + BLOCK]

        @pl.when(step == 3)
        def _():
            for outer in range(4):

                def fill(i, carry, outer=outer):
                    k_slot = t[AT_DENSE + outer * 16 + i]
                    v_slot = t[AT_DENSE + (i // 4) * 16 + outer * 4 + i % 4]
                    k = total[k_slot, :, :HD]
                    v = total[v_slot, :, HD:]
                    k_outs[outer][i] = k.astype(k_outs[outer].dtype)
                    v_outs[outer][i] = v.astype(v_outs[outer].dtype)
                    return carry

                lax.fori_loop(0, 16, fill, 0)

    mine = pl.BlockSpec((BLOCK, width), lambda i, t: (jnp.minimum(i, 1), t[AT_CORE]))
    peer = pl.BlockSpec((BLOCK, width), lambda i, t: (jnp.maximum(i - 2, 0), 0))
    rows = pl.BlockSpec((BLOCK, 2 * width), lambda i, t: (i, 0))

    def full(shape):
        return pl.BlockSpec(
            shape, lambda i, t: (0,) * len(shape), pipeline_mode=pl.Buffered(1)
        )

    def held(shape):
        return pl.BlockSpec(shape, lambda i, t: (0,) * len(shape))

    wide = (16, BLOCK, HD)
    grads = [(wide, F32)] + [(wide, BF)] * 3
    return pl.pallas_call(
        body,
        grid_spec=pltpu.PrefetchScalarGridSpec(
            num_scalar_prefetch=1,
            grid=(4,),
            in_specs=[mine, peer, mine, peer] + [full(p.shape) for p in pieces],
            out_specs=[rows] + [held(s) for s, _ in grads + grads],
            scratch_shapes=[
                pltpu.VMEM((SLOTS, BLOCK, 2 * HD), BF),
                pltpu.VMEM((SLOTS + 1, BLOCK, 2 * HD), F32),
                pltpu.VMEM((lanes, HD), BF),
                pltpu.VMEM((lanes, HD), BF),
            ],
        ),
        out_shape=[jax.ShapeDtypeStruct((4 * BLOCK, 2 * width), BF)]
        + [jax.ShapeDtypeStruct(s, d) for s, d in grads + grads],
        compiler_params=params(36),
        name="attend",
    )(table, queries, query_peer, upstream, upstream_peer, *pieces)


def combine(sums):
    def body(*refs):
        for side_of in range(2):
            home, a, b, c = refs[4 * side_of : 4 * side_of + 4]
            outs = refs[8 + 4 * side_of : 12 + 4 * side_of]
            rows = outs[0].shape[0]
            for k in range(4):
                at = slice(k * rows, (k + 1) * rows)
                outs[k][...] = (
                    home[at] + a[at].astype(F32) + b[at].astype(F32) + c[at].astype(F32)
                )

    shape = sums[0].shape
    part = (shape[0] // 4,) + shape[1:]
    return pl.pallas_call(
        body,
        in_specs=[pl.BlockSpec(memory_space=pltpu.VMEM)] * 8,
        out_specs=[pl.BlockSpec(memory_space=pltpu.VMEM)] * 8,
        out_shape=[jax.ShapeDtypeStruct(part, F32)] * 8,
        compiler_params=params(8),
        name="combine",
    )(*sums)


def finish_grads(sums, cosine, sine):
    rows = 4 * BLOCK

    def body(*refs):
        ks, vs = refs[:4], refs[4:8]
        cs, sn, every, away = refs[8:]
        key = (ks[0][...] + ks[1][...] + ks[2][...] + ks[3][...]).reshape(rows, HD)
        value = (vs[0][...] + vs[1][...] + vs[2][...] + vs[3][...]).reshape(rows, HD)
        key = key * cs[...] - pltpu.roll(key, HD // 2, 1) * sn[...]
        both = jnp.concatenate([key.astype(BF), value.astype(BF)], axis=1)
        every[...] = both
        away[...] = both[rows // 2 :]

    return pl.pallas_call(
        body,
        in_specs=[pl.BlockSpec(memory_space=pltpu.VMEM)] * 10,
        out_specs=[pl.BlockSpec(memory_space=pltpu.VMEM)] * 2,
        out_shape=[
            jax.ShapeDtypeStruct((rows, 2 * HD), BF),
            jax.ShapeDtypeStruct((rows // 2, 2 * HD), BF),
        ],
        compiler_params=params(5),
        name="finish_grads",
    )(*sums, cosine, sine)


def finish_weights(sums):
    share = sums[0].shape[1]

    def body(*refs):
        ks, vs = refs[:4], refs[4:8]
        for row, out in enumerate(refs[8:]):
            out[:, :HD] = ks[0][row] + ks[1][row] + ks[2][row] + ks[3][row]
            out[:, HD:] = vs[0][row] + vs[1][row] + vs[2][row] + vs[3][row]

    return pl.pallas_call(
        body,
        in_specs=[pl.BlockSpec(memory_space=pltpu.VMEM)] * 8,
        out_specs=[pl.BlockSpec(memory_space=pltpu.VMEM)] * 2,
        out_shape=[jax.ShapeDtypeStruct((share, 2 * HD), F32)] * 2,
        compiler_params=params(4),
        name="finish_weights",
    )(*sums)


def input_partials(place, mine, other, key_weight, value_weight):
    rows = other.shape[0]
    cols = key_weight.shape[1]
    width = key_weight.shape[0] // 4

    def body(p, a, b, kw, vw, *outs):
        swap = p[4] == 1
        first = jnp.where(swap, b[...], a[...])
        second = jnp.where(swap, a[...], b[...])
        key = jnp.concatenate([first[:, :HD], second[:, :HD]], axis=1)
        value = jnp.concatenate([first[:, HD:], second[:, HD:]], axis=1)
        result = (nt(key, kw[...]) + nt(value, vw[...])).astype(BF)
        for k in range(4):

            @pl.when(pl.program_id(0) == k)
            def _(k=k):
                outs[k][...] = result

    grads = pl.BlockSpec((rows, 2 * HD), lambda i, p: (0, 0))
    weight = pl.BlockSpec((width, cols), lambda i, p: (p[5 + i], 0))
    out = pl.BlockSpec((rows, width), lambda i, p: (0, 0), pipeline_mode=pl.Buffered(1))
    return pl.pallas_call(
        body,
        grid_spec=pltpu.PrefetchScalarGridSpec(
            num_scalar_prefetch=1,
            grid=(4,),
            in_specs=[grads, grads, weight, weight],
            out_specs=[out] * 4,
        ),
        out_shape=[jax.ShapeDtypeStruct((rows, width), BF)] * 4,
        compiler_params=params(7),
        name="input_partials",
    )(place, mine, other, key_weight, value_weight)


def flip(own, peer):
    width = own[0].shape[1]
    rows = 4 * BLOCK

    def body(*refs):
        mine, other, out = refs[:7], refs[7:14], refs[14]
        for piece in range(4):
            at = slice(max(2 * piece - 1, 0), 2 * piece + 1)
            features = jnp.concatenate([r[...] for r in mine[at] + other[at]], axis=0)
            out[piece] = features.T

    return pl.pallas_call(
        body,
        in_specs=[pl.BlockSpec(memory_space=pltpu.VMEM)] * 14,
        out_specs=pl.BlockSpec(memory_space=pltpu.VMEM),
        out_shape=jax.ShapeDtypeStruct((4, width, rows), BF),
        compiler_params=params(12),
        name="flip",
    )(*own, *peer)


def weight_partials(place, grads, features):
    width = features.shape[1]
    share = width // 8

    def body(p, g, ft, *refs):
        k_outs, v_outs, result = refs[:4], refs[4:8], refs[8]
        core = p[4]
        grad = g[...]
        for dy in range(4):
            result[...] = nn(ft[p[9 + dy]], grad)
            for dx in range(4):
                base = p[13 + dx] * (2 * share)
                for r in range(2):
                    start = pl.multiple_of(base + ((core + r) % 2) * share, 16)
                    value = result[pl.ds(start, share), :]
                    k_outs[dx][dy * 2 + r] = value[:, :HD].astype(k_outs[dx].dtype)
                    v_outs[dy][dx * 2 + r] = value[:, HD:].astype(v_outs[dy].dtype)

    wide = (8, share, HD)
    shapes = [(wide, F32)] + [(wide, BF)] * 3
    return pl.pallas_call(
        body,
        in_specs=[pl.BlockSpec(memory_space=pltpu.SMEM)]
        + [pl.BlockSpec(memory_space=pltpu.VMEM)] * 2,
        out_specs=[pl.BlockSpec(memory_space=pltpu.VMEM)] * 8,
        out_shape=[jax.ShapeDtypeStruct(s, d) for s, d in shapes + shapes],
        scratch_shapes=[pltpu.VMEM((width, 2 * HD), F32)],
        compiler_params=params(11),
        name="weight_partials",
    )(place, grads, features)


def mover(axis, pairs):
    return lambda value: lax.ppermute(value, axis, pairs)


def ring_gather(first, second, ahead, behind):
    back_first = ahead(first)
    next_second = behind(second)
    back_second = ahead(second)
    next_first = behind(first)
    far_first = ahead(back_first)
    far_second = behind(next_second)
    return [
        first,
        second,
        back_first,
        back_second,
        next_first,
        next_second,
        far_first,
        far_second,
    ]


def send_all(values, ahead, behind, across):
    home, back, forth, far = values
    near = ahead(forth)
    distant = across(far)
    other = behind(back)
    return [home, near, other, distant]


def program(hidden, queries, key_weight, value_weight, parents, upstream):
    place_ctx = lax.axis_index("ctx")
    tp = lax.axis_index("tp")
    core = place_ctx % 2
    x = (place_ctx // 2) % 4
    y = place_ctx // 8
    xn = mover("ctx", [(i, i // 8 * 8 + (i + 2) % 8) for i in range(32)])
    xb = mover("ctx", [(i, i // 8 * 8 + (i - 2) % 8) for i in range(32)])
    yn = mover("ctx", [(i, (i + 8) % 32) for i in range(32)])
    yb = mover("ctx", [(i, (i - 8) % 32) for i in range(32)])
    swap = mover("ctx", [(i, i ^ 1) for i in range(32)])
    zn = mover("tp", [(i, (i + 1) % 4) for i in range(4)])
    zb = mover("tp", [(i, (i - 1) % 4) for i in range(4)])
    x2 = mover("ctx", [(i, i // 8 * 8 + (i + 4) % 8) for i in range(32)])
    y2 = mover("ctx", [(i, (i + 16) % 32) for i in range(32)])
    z2 = mover("tp", [(i, (i + 2) % 4) for i in range(4)])

    local_rows = hidden.shape[0]
    table, place, depths = device_tables(
        parents, jnp.stack([y, x, core, tp]).astype(jnp.int32)
    )
    cosine, sine = rope_tables(depths)

    width = queries.shape[1] // 2
    top, low = halve(hidden)
    left_top = zn(top)
    right_low = zb(low)
    left_low = zn(low)
    right_top = zb(top)
    far_top = zn(left_top)
    far_low = zb(right_low)
    query_away = lax.dynamic_slice_in_dim(queries, (1 - core) * width, width, 1)
    upstream_away = lax.dynamic_slice_in_dim(upstream, (1 - core) * width, width, 1)
    query_peer = swap(query_away)
    upstream_peer = swap(upstream_away)
    hidden_peer = swap(hidden)
    place, hidden_peer, query_peer, upstream_peer = lax.optimization_barrier(
        (place, hidden_peer, query_peer, upstream_peer)
    )
    key_sum, value_sum = project_near(
        place, hidden, left_top, left_low, right_top, right_low, key_weight, value_weight
    )
    keep, send = project_far(
        place, far_top, far_low, key_weight, value_weight, key_sum, value_sum, cosine, sine
    )
    other = swap(send)
    mine_line = pack(keep, xn(keep), xb(keep), x2(keep))
    other_line = pack(other, yn(other), yb(other), y2(other))
    pieces = ring_gather(*mine_line, yn, yb) + ring_gather(*other_line, xn, xb)

    near_features = [left_top, left_low, right_top, right_low, far_top, far_low]
    own_features = [hidden, *near_features]
    peer_features = [hidden_peer]
    for feature in near_features:
        peer_features.append(swap(feature))
    features = flip(own_features, peer_features)

    out, *slot_grads = attend(table, queries, query_peer, upstream, upstream_peer, pieces)
    sums = combine(send_all(slot_grads[:4], xn, xb, x2) + send_all(slot_grads[4:], yn, yb, y2))
    grads, grads_away = finish_grads(
        send_all(sums[:4], yn, yb, y2) + send_all(sums[4:], xn, xb, x2), cosine, sine
    )
    grads_other = swap(grads_away)
    grads, grads_other = lax.optimization_barrier((grads, grads_other))

    out_other = swap(out[local_rows:])

    def assemble(a, b):
        first = jnp.where(core == 0, a, b)
        second = jnp.where(core == 0, b, a)
        return jnp.concatenate([first, second], axis=1)

    attention = assemble(out[:local_rows, :width], out_other[:, :width])
    query_grad = assemble(out[:local_rows, width:], out_other[:, width:])

    w_parts = weight_partials(place, grads, features)
    w_sent = send_all(w_parts[:4], xn, xb, x2) + send_all(w_parts[4:], yn, yb, y2)
    parts = input_partials(place, grads, grads_other, key_weight, value_weight)
    _, from_back, from_next, from_far = send_all(parts, zn, zb, z2)
    hidden_grad = (
        parts[0].astype(F32)
        + from_back.astype(F32)
        + from_next.astype(F32)
        + from_far.astype(F32)
    ).astype(BF)
    w_sums = combine(w_sent)
    both, both_away = finish_weights(
        send_all(w_sums[:4], yn, yb, y2) + send_all(w_sums[4:], xn, xb, x2)
    )
    both_other = swap(both_away)
    key_weight_grad, value_weight_grad = join_weights(place, both, both_other)
    return (attention, query_grad, hidden_grad, key_weight_grad, value_weight_grad)


def solution(mesh):
    return jax.shard_map(
        program,
        mesh=mesh,
        in_specs=(
            P("ctx", "tp"),
            P("ctx", "tp"),
            P(None, "tp"),
            P(None, "tp"),
            P(),
            P("ctx", "tp"),
        ),
        out_specs=(P("ctx", "tp"), P("ctx", "tp"), P("ctx", "tp"), P("ctx", "tp"), P("ctx", "tp")),
        check_vma=False,
    )
```

```python
import math

import jax
import jax.numpy as jnp
from jax import lax
from jax.experimental import pallas as pl
from jax.experimental.pallas import tpu as pltpu
from jax.sharding import PartitionSpec as P

HD = 128
BLOCK = 128
DEPTH = 8
THETA = 1000000.0
NEGATIVE = -1e30
BF = jnp.bfloat16
F32 = jnp.float32
SCALE = 1.0 / math.sqrt(HD)
STACK = DEPTH - 1
SLOTS = STACK + 4
OFFSETS = (0, 3, 1, 2)


def side(delta):
    return jnp.where(delta == 0, 0, jnp.where(delta == 3, 1, jnp.where(delta == 1, 2, 3)))


def device_tables(parents, position):
    block_total = parents.shape[0]

    def body(links, where, table, place, depths, level):
        y, x, core, tp = where[0], where[1], where[2], where[3]
        first = 16 * y + 4 * x
        level[0] = 0

        def descend(b, carry):
            level[b] = level[links[b]] + 1
            return carry

        lax.fori_loop(1, block_total, descend, 0)
        place[0] = tp
        place[1] = (tp + 3) % 4
        place[2] = (tp + 1) % 4
        place[3] = (tp + 2) % 4
        place[4] = core
        for k, o in enumerate(OFFSETS):
            place[5 + k] = (tp + o) % 4
            place[9 + k] = side((y + o - tp + 4) % 4)
            place[13 + k] = (x + o) % 4
        table[AT_CORE] = core

        def blank(i, carry):
            table[AT_DENSE + i] = SLOTS
            return carry

        lax.fori_loop(0, 64, blank, 0)
        for r in range(4):
            table[AT_DENSE + r] = STACK + r
            block = first + (2 * core + r) % 4
            own_depth = level[block]
            depths[r] = own_depth
            table[AT_DEPTH + r] = own_depth
            node = block
            for d in range(DEPTH - 1, -1, -1):
                live = d <= own_depth
                slot = jnp.where(node >= first, STACK + (node - first + 4 - 2 * core) % 4, d)
                table[AT_SLOT + r * DEPTH + d] = jnp.where(live, slot, STACK + r)
                node = jnp.where(live, jnp.maximum(links[node], 0), node)
        lead_depth = level[first]
        node = first
        for d in range(STACK - 1, -1, -1):
            live = d < lead_depth
            node = jnp.where(live, jnp.maximum(links[node], 0), node)
            column = side((node // 4 + 4 - x) % 4)
            line = side((node // 16 + 4 - y) % 4)
            same = (node // 2) % 2 == core
            parity = node % 2
            outer = jnp.where(same, line, column)
            inner = jnp.where(same, column, line)
            piece = jnp.where(same, 0, 8) + outer * 2 + parity
            table[d] = jnp.where(live, piece, -1)
            table[AT_PLACE + d] = jnp.where(live, inner, 0)
            spot = AT_DENSE + (column * 4 + line) * 4 + (node + 4 - 2 * core) % 4

            @pl.when(live)
            def _(spot=spot, d=d):
                table[spot] = d

    smem = pl.BlockSpec(memory_space=pltpu.SMEM)
    return pl.pallas_call(
        body,
        in_specs=[smem, smem],
        out_specs=[smem] * 3,
        out_shape=[
            jax.ShapeDtypeStruct((AT_CORE + 1,), jnp.int32),
            jax.ShapeDtypeStruct((17,), jnp.int32),
            jax.ShapeDtypeStruct((4,), jnp.int32),
        ],
        scratch_shapes=[pltpu.SMEM((block_total,), jnp.int32)],
        compiler_params=params(1),
        name="device_tables",
    )(parents, position)


AT_PLACE = STACK
AT_DEPTH = 2 * STACK
AT_SLOT = AT_DEPTH + 4
AT_DENSE = AT_SLOT + 4 * DEPTH
AT_CORE = AT_DENSE + 64


def rope_tables(depths):
    offset = jnp.arange(BLOCK, dtype=jnp.int32)
    position = (depths[:, None] * BLOCK + offset[None, :]).astype(F32)
    frequency = jnp.exp(jnp.arange(HD // 2, dtype=F32) * (-2.0 * math.log(THETA) / HD))
    angles = (position[:, :, None] * frequency[None, None, :]).reshape(4 * BLOCK, HD // 2)
    cosine, sine = jnp.cos(angles), jnp.sin(angles)
    return (
        jnp.concatenate([cosine, cosine], axis=-1),
        jnp.concatenate([-sine, sine], axis=-1),
    )


def nn(a, b):
    return jnp.dot(a, b, preferred_element_type=F32)


def nt(a, b):
    return lax.dot_general(a, b, (((1,), (1,)), ((), ())), preferred_element_type=F32)


def tn(a, b):
    return lax.dot_general(a, b, (((0,), (0,)), ((), ())), preferred_element_type=F32)


def params(mib):
    return pltpu.CompilerParams(vmem_limit_bytes=mib * 1024 * 1024)


def halve(value):
    half = value.shape[0] // 2

    def body(source, top, low):
        top[...] = source[:half]
        low[...] = source[half:]

    return pl.pallas_call(
        body,
        in_specs=[pl.BlockSpec(memory_space=pltpu.VMEM)],
        out_specs=[pl.BlockSpec(memory_space=pltpu.VMEM)] * 2,
        out_shape=[jax.ShapeDtypeStruct((half, value.shape[1]), value.dtype)] * 2,
        compiler_params=params(3),
        name="halve",
    )(value)


def project_near(place, own, left_top, left_low, right_top, right_low, key_weight, value_weight):
    rows, width = own.shape
    cols = key_weight.shape[1]

    def body(place_ref, a, bt, bl, ct, cl, ka, kb, kc, va, vb, vc, key_out, value_out):
        b = jnp.concatenate([bt[...], bl[...]], axis=0)
        c = jnp.concatenate([ct[...], cl[...]], axis=0)
        key_out[...] = nn(a[...], ka[...]) + nn(b, kb[...]) + nn(c, kc[...])
        value_out[...] = nn(a[...], va[...]) + nn(b, vb[...]) + nn(c, vc[...])

    whole = pl.BlockSpec((rows, width), lambda i, p: (0, 0))
    half = pl.BlockSpec((rows // 2, width), lambda i, p: (0, 0))
    weights = [pl.BlockSpec((width, cols), lambda i, p, k=k: (p[k], 0)) for k in range(3)]
    out = pl.BlockSpec((rows, cols), lambda i, p: (0, 0))
    return pl.pallas_call(
        body,
        grid_spec=pltpu.PrefetchScalarGridSpec(
            num_scalar_prefetch=1,
            grid=(1,),
            in_specs=[whole] + [half] * 4 + weights + weights,
            out_specs=[out, out],
        ),
        out_shape=[jax.ShapeDtypeStruct((rows, cols), F32)] * 2,
        compiler_params=params(18),
        name="project_near",
    )(
        place,
        own,
        left_top,
        left_low,
        right_top,
        right_low,
        *([key_weight] * 3),
        *([value_weight] * 3),
    )


def pack(own, back, forth, far):
    def body(a, b, c, d, first, second):
        for k, ref in enumerate((a, b, c, d)):
            first[k] = ref[:BLOCK]
            second[k] = ref[BLOCK:]

    return pl.pallas_call(
        body,
        in_specs=[pl.BlockSpec(memory_space=pltpu.VMEM)] * 4,
        out_specs=[pl.BlockSpec(memory_space=pltpu.VMEM)] * 2,
        out_shape=[jax.ShapeDtypeStruct((4, BLOCK, 2 * HD), BF)] * 2,
        compiler_params=params(3),
        name="pack",
    )(own, back, forth, far)


def join_rows(place, mine, other):
    rows, cols = other.shape
    width = cols // 2

    def body(p, a, b, out, grad):
        swap = p[4] == 1
        for low, ref in ((0, out), (width, grad)):
            first = a[:rows, low : low + width]
            second = b[:, low : low + width]
            ref[:, :width] = jnp.where(swap, second, first)
            ref[:, width:] = jnp.where(swap, first, second)

    return pl.pallas_call(
        body,
        in_specs=[pl.BlockSpec(memory_space=pltpu.SMEM)]
        + [pl.BlockSpec(memory_space=pltpu.VMEM)] * 2,
        out_specs=[pl.BlockSpec(memory_space=pltpu.VMEM)] * 2,
        out_shape=[jax.ShapeDtypeStruct((rows, cols), BF)] * 2,
        compiler_params=params(5),
        name="join_rows",
    )(place, mine, other)


def join_weights(place, mine, other):
    share = mine.shape[0]

    def body(p, a, b, key, value):
        swap = p[4] == 1
        first = jnp.where(swap, b[...], a[...])
        second = jnp.where(swap, a[...], b[...])
        key[:, :HD] = first[:, :HD]
        key[:, HD:] = second[:, :HD]
        value[:, :HD] = first[:, HD:]
        value[:, HD:] = second[:, HD:]

    return pl.pallas_call(
        body,
        in_specs=[pl.BlockSpec(memory_space=pltpu.SMEM)]
        + [pl.BlockSpec(memory_space=pltpu.VMEM)] * 2,
        out_specs=[pl.BlockSpec(memory_space=pltpu.VMEM)] * 2,
        out_shape=[jax.ShapeDtypeStruct((share, 2 * HD), F32)] * 2,
        compiler_params=params(2),
        name="join_weights",
    )(place, mine, other)


def project_far(place, top, bottom, key_weight, value_weight, key_sum, value_sum, cosine, sine):
    rows, cols = key_sum.shape
    width = top.shape[1]
    half = rows // 2

    def body(p, a, b, kw, vw, ks, vs, cs, sn, keep, send):
        far = jnp.concatenate([a[...], b[...]], axis=0)
        key = ks[...] + nn(far, kw[...])
        value = vs[...] + nn(far, vw[...])
        heads = []
        for h in range(2):
            part = key[:, h * HD : (h + 1) * HD]
            turned = part * cs[...] + pltpu.roll(part, HD // 2, 1) * sn[...]
            heads.append(
                jnp.concatenate([turned, value[:, h * HD : (h + 1) * HD]], axis=1).astype(BF)
            )
        swap = p[4] == 1
        keep[...] = jnp.where(swap, heads[1], heads[0])
        send[...] = jnp.where(swap, heads[0], heads[1])

    weight = pl.BlockSpec((width, cols), lambda i, p: (p[3], 0))
    part = pl.BlockSpec((half, width), lambda i, p: (0, 0))
    sums = pl.BlockSpec((rows, cols), lambda i, p: (0, 0))
    angle = pl.BlockSpec((rows, HD), lambda i, p: (0, 0))
    return pl.pallas_call(
        body,
        grid_spec=pltpu.PrefetchScalarGridSpec(
            num_scalar_prefetch=1,
            grid=(1,),
            in_specs=[part, part, weight, weight, sums, sums, angle, angle],
            out_specs=[sums, sums],
        ),
        out_shape=[jax.ShapeDtypeStruct((rows, cols), BF)] * 2,
        compiler_params=params(8),
        name="project_far",
    )(place, top, bottom, key_weight, value_weight, key_sum, value_sum, cosine, sine)


def attend(table, queries, query_peer, upstream, upstream_peer, pieces):
    groups = queries.shape[1] // (2 * HD)
    width = groups * HD
    lanes = groups * BLOCK

    def body(t, q_own, q_far, u_own, u_far, *refs):
        parts = refs[:16]
        k_outs = refs[17:21]
        v_outs = refs[21:25]
        out = refs[16]
        kv, total, q_rows, u_rows = refs[25:]
        step = pl.program_id(0)

        @pl.when(step == 0)
        def _():
            for s in range(STACK):
                for index in range(16):

                    @pl.when(t[s] == index)
                    def _(s=s, index=index):
                        kv[s] = parts[index][t[AT_PLACE + s]]

            for r in range(4):
                kv[STACK + r] = parts[r if r < 2 else 6 + r][0]
            total[...] = jnp.zeros(total.shape, F32)

        own = step < 2
        q = jnp.where(own, q_own[...], q_far[...])
        u = jnp.where(own, u_own[...], u_far[...])
        for h in range(groups):
            q_rows[h * BLOCK : (h + 1) * BLOCK] = q[:, h * HD : (h + 1) * HD]
            u_rows[h * BLOCK : (h + 1) * BLOCK] = u[:, h * HD : (h + 1) * HD]
        q = q_rows[...]
        u = u_rows[...]
        depth = t[AT_DEPTH + step]
        slots = [t[AT_SLOT + step * DEPTH + d] for d in range(DEPTH)]
        keys = jnp.concatenate([kv[s, :, :HD] for s in slots], axis=0)
        values = jnp.concatenate([kv[s, :, HD:] for s in slots], axis=0)
        ahead = lax.broadcasted_iota(jnp.int32, (BLOCK, lanes), 0) - (
            lax.broadcasted_iota(jnp.int32, (BLOCK, lanes), 1) % BLOCK
        )
        raw = nt(keys, q)
        scores = []
        peak = None
        for d in range(DEPTH):
            reach = jnp.where(d < depth, BLOCK, jnp.where(d == depth, 0, -BLOCK))
            tile = jnp.where(
                ahead <= reach, raw[d * BLOCK : (d + 1) * BLOCK] * SCALE, NEGATIVE
            )
            scores.append(tile)
            top = jnp.max(tile, axis=0, keepdims=True)
            peak = top if peak is None else jnp.maximum(peak, top)
        weights = [jnp.exp(tile - peak) for tile in scores]
        mass = None
        for w in weights:
            part = jnp.sum(w, axis=0, keepdims=True)
            mass = part if mass is None else mass + part
        rounded = jnp.concatenate([w.astype(BF) for w in weights], axis=0)
        mixed = (tn(values, rounded) / mass).astype(BF).astype(F32)
        delta = jnp.sum(u.astype(F32).T * mixed, axis=0, keepdims=True)
        for h in range(groups):
            out[:, h * HD : (h + 1) * HD] = mixed[:, h * BLOCK : (h + 1) * BLOCK].T.astype(BF)
        inverse = 1.0 / mass
        slopes = nt(values, u)
        chances = []
        pulls = []
        for d in range(DEPTH):
            p = weights[d] * inverse
            chances.append(p.astype(BF))
            pulls.append((p * (slopes[d * BLOCK : (d + 1) * BLOCK] - delta)).astype(BF))
        chances = jnp.concatenate(chances, axis=0)
        pulls = jnp.concatenate(pulls, axis=0)
        turned = tn(keys, pulls) * SCALE
        for h in range(groups):
            out[:, width + h * HD : width + (h + 1) * HD] = (
                turned[:, h * BLOCK : (h + 1) * BLOCK].T.astype(BF)
            )
        v_part = nn(chances, u)
        k_part = nn(pulls, q) * SCALE
        for d in range(DEPTH):
            low = d * BLOCK
            total[slots[d], :, :HD] += k_part[low : low + BLOCK]
            total[slots[d], :, HD:] += v_part[low : low + BLOCK]

        @pl.when(step == 3)
        def _():
            for outer in range(4):

                def fill(i, carry, outer=outer):
                    k_slot = t[AT_DENSE + outer * 16 + i]
                    v_slot = t[AT_DENSE + (i // 4) * 16 + outer * 4 + i % 4]
                    k = total[k_slot, :, :HD]
                    v = total[v_slot, :, HD:]
                    k_outs[outer][i] = k.astype(k_outs[outer].dtype)
                    v_outs[outer][i] = v.astype(v_outs[outer].dtype)
                    return carry

                lax.fori_loop(0, 16, fill, 0)

    mine = pl.BlockSpec((BLOCK, width), lambda i, t: (jnp.minimum(i, 1), t[AT_CORE]))
    peer = pl.BlockSpec((BLOCK, width), lambda i, t: (jnp.maximum(i - 2, 0), 0))
    rows = pl.BlockSpec((BLOCK, 2 * width), lambda i, t: (i, 0))

    def full(shape):
        return pl.BlockSpec(
            shape, lambda i, t: (0,) * len(shape), pipeline_mode=pl.Buffered(1)
        )

    def held(shape):
        return pl.BlockSpec(shape, lambda i, t: (0,) * len(shape))

    wide = (16, BLOCK, HD)
    grads = [(wide, F32)] + [(wide, BF)] * 3
    return pl.pallas_call(
        body,
        grid_spec=pltpu.PrefetchScalarGridSpec(
            num_scalar_prefetch=1,
            grid=(4,),
            in_specs=[mine, peer, mine, peer] + [full(p.shape) for p in pieces],
            out_specs=[rows] + [held(s) for s, _ in grads + grads],
            scratch_shapes=[
                pltpu.VMEM((SLOTS, BLOCK, 2 * HD), BF),
                pltpu.VMEM((SLOTS + 1, BLOCK, 2 * HD), F32),
                pltpu.VMEM((lanes, HD), BF),
                pltpu.VMEM((lanes, HD), BF),
            ],
        ),
        out_shape=[jax.ShapeDtypeStruct((4 * BLOCK, 2 * width), BF)]
        + [jax.ShapeDtypeStruct(s, d) for s, d in grads + grads],
        compiler_params=params(36),
        name="attend",
    )(table, queries, query_peer, upstream, upstream_peer, *pieces)


def combine(sums):
    def body(*refs):
        for side_of in range(2):
            home, a, b, c = refs[4 * side_of : 4 * side_of + 4]
            outs = refs[8 + 4 * side_of : 12 + 4 * side_of]
            rows = outs[0].shape[0]
            for k in range(4):
                at = slice(k * rows, (k + 1) * rows)
                outs[k][...] = (
                    home[at] + a[at].astype(F32) + b[at].astype(F32) + c[at].astype(F32)
                )

    shape = sums[0].shape
    part = (shape[0] // 4,) + shape[1:]
    return pl.pallas_call(
        body,
        in_specs=[pl.BlockSpec(memory_space=pltpu.VMEM)] * 8,
        out_specs=[pl.BlockSpec(memory_space=pltpu.VMEM)] * 8,
        out_shape=[jax.ShapeDtypeStruct(part, F32)] * 8,
        compiler_params=params(8),
        name="combine",
    )(*sums)


def finish_grads(sums, cosine, sine):
    rows = 4 * BLOCK

    def body(*refs):
        ks, vs = refs[:4], refs[4:8]
        cs, sn, every, away = refs[8:]
        key = (ks[0][...] + ks[1][...] + ks[2][...] + ks[3][...]).reshape(rows, HD)
        value = (vs[0][...] + vs[1][...] + vs[2][...] + vs[3][...]).reshape(rows, HD)
        key = key * cs[...] - pltpu.roll(key, HD // 2, 1) * sn[...]
        both = jnp.concatenate([key.astype(BF), value.astype(BF)], axis=1)
        every[...] = both
        away[...] = both[rows // 2 :]

    return pl.pallas_call(
        body,
        in_specs=[pl.BlockSpec(memory_space=pltpu.VMEM)] * 10,
        out_specs=[pl.BlockSpec(memory_space=pltpu.VMEM)] * 2,
        out_shape=[
            jax.ShapeDtypeStruct((rows, 2 * HD), BF),
            jax.ShapeDtypeStruct((rows // 2, 2 * HD), BF),
        ],
        compiler_params=params(5),
        name="finish_grads",
    )(*sums, cosine, sine)


def finish_weights(sums):
    share = sums[0].shape[1]

    def body(*refs):
        ks, vs = refs[:4], refs[4:8]
        for row, out in enumerate(refs[8:]):
            out[:, :HD] = ks[0][row] + ks[1][row] + ks[2][row] + ks[3][row]
            out[:, HD:] = vs[0][row] + vs[1][row] + vs[2][row] + vs[3][row]

    return pl.pallas_call(
        body,
        in_specs=[pl.BlockSpec(memory_space=pltpu.VMEM)] * 8,
        out_specs=[pl.BlockSpec(memory_space=pltpu.VMEM)] * 2,
        out_shape=[jax.ShapeDtypeStruct((share, 2 * HD), F32)] * 2,
        compiler_params=params(4),
        name="finish_weights",
    )(*sums)


def input_partials(place, mine, other, key_weight, value_weight):
    rows = other.shape[0]
    cols = key_weight.shape[1]
    width = key_weight.shape[0] // 4

    def body(p, a, b, kw, vw, *outs):
        swap = p[4] == 1
        first = jnp.where(swap, b[...], a[...])
        second = jnp.where(swap, a[...], b[...])
        key = jnp.concatenate([first[:, :HD], second[:, :HD]], axis=1)
        value = jnp.concatenate([first[:, HD:], second[:, HD:]], axis=1)
        result = (nt(key, kw[...]) + nt(value, vw[...])).astype(BF)
        for k in range(4):

            @pl.when(pl.program_id(0) == k)
            def _(k=k):
                outs[k][...] = result

    grads = pl.BlockSpec((rows, 2 * HD), lambda i, p: (0, 0))
    weight = pl.BlockSpec((width, cols), lambda i, p: (p[5 + i], 0))
    out = pl.BlockSpec((rows, width), lambda i, p: (0, 0), pipeline_mode=pl.Buffered(1))
    return pl.pallas_call(
        body,
        grid_spec=pltpu.PrefetchScalarGridSpec(
            num_scalar_prefetch=1,
            grid=(4,),
            in_specs=[grads, grads, weight, weight],
            out_specs=[out] * 4,
        ),
        out_shape=[jax.ShapeDtypeStruct((rows, width), BF)] * 4,
        compiler_params=params(7),
        name="input_partials",
    )(place, mine, other, key_weight, value_weight)


def flip(own, peer):
    width = own[0].shape[1]
    rows = 4 * BLOCK

    def body(*refs):
        mine, other, out = refs[:7], refs[7:14], refs[14]
        for piece in range(4):
            at = slice(max(2 * piece - 1, 0), 2 * piece + 1)
            features = jnp.concatenate([r[...] for r in mine[at] + other[at]], axis=0)
            out[piece] = features.T

    return pl.pallas_call(
        body,
        in_specs=[pl.BlockSpec(memory_space=pltpu.VMEM)] * 14,
        out_specs=pl.BlockSpec(memory_space=pltpu.VMEM),
        out_shape=jax.ShapeDtypeStruct((4, width, rows), BF),
        compiler_params=params(12),
        name="flip",
    )(*own, *peer)


def weight_partials(place, grads, features):
    width = features.shape[1]
    share = width // 8

    def body(p, g, ft, *refs):
        k_outs, v_outs, result = refs[:4], refs[4:8], refs[8]
        core = p[4]
        grad = g[...]
        for dy in range(4):
            result[...] = nn(ft[p[9 + dy]], grad)
            for dx in range(4):
                base = p[13 + dx] * (2 * share)
                for r in range(2):
                    start = pl.multiple_of(base + ((core + r) % 2) * share, 16)
                    value = result[pl.ds(start, share), :]
                    k_outs[dx][dy * 2 + r] = value[:, :HD].astype(k_outs[dx].dtype)
                    v_outs[dy][dx * 2 + r] = value[:, HD:].astype(v_outs[dy].dtype)

    wide = (8, share, HD)
    shapes = [(wide, F32)] + [(wide, BF)] * 3
    return pl.pallas_call(
        body,
        in_specs=[pl.BlockSpec(memory_space=pltpu.SMEM)]
        + [pl.BlockSpec(memory_space=pltpu.VMEM)] * 2,
        out_specs=[pl.BlockSpec(memory_space=pltpu.VMEM)] * 8,
        out_shape=[jax.ShapeDtypeStruct(s, d) for s, d in shapes + shapes],
        scratch_shapes=[pltpu.VMEM((width, 2 * HD), F32)],
        compiler_params=params(11),
        name="weight_partials",
    )(place, grads, features)


def mover(axis, pairs):
    return lambda value: lax.ppermute(value, axis, pairs)


def ring_gather(first, second, ahead, behind):
    back_first = ahead(first)
    next_second = behind(second)
    back_second = ahead(second)
    next_first = behind(first)
    far_first = ahead(back_first)
    far_second = behind(next_second)
    return [
        first,
        second,
        back_first,
        back_second,
        next_first,
        next_second,
        far_first,
        far_second,
    ]


def send_all(values, ahead, behind, across):
    home, back, forth, far = values
    near = ahead(forth)
    distant = across(far)
    other = behind(back)
    return [home, near, other, distant]


def program(hidden, queries, key_weight, value_weight, parents, upstream):
    place_ctx = lax.axis_index("ctx")
    tp = lax.axis_index("tp")
    core = place_ctx % 2
    x = (place_ctx // 2) % 4
    y = place_ctx // 8
    xn = mover("ctx", [(i, i // 8 * 8 + (i + 2) % 8) for i in range(32)])
    xb = mover("ctx", [(i, i // 8 * 8 + (i - 2) % 8) for i in range(32)])
    yn = mover("ctx", [(i, (i + 8) % 32) for i in range(32)])
    yb = mover("ctx", [(i, (i - 8) % 32) for i in range(32)])
    swap = mover("ctx", [(i, i ^ 1) for i in range(32)])
    zn = mover("tp", [(i, (i + 1) % 4) for i in range(4)])
    zb = mover("tp", [(i, (i - 1) % 4) for i in range(4)])
    x2 = mover("ctx", [(i, i // 8 * 8 + (i + 4) % 8) for i in range(32)])
    y2 = mover("ctx", [(i, (i + 16) % 32) for i in range(32)])
    z2 = mover("tp", [(i, (i + 2) % 4) for i in range(4)])

    local_rows = hidden.shape[0]
    table, place, depths = device_tables(
        parents, jnp.stack([y, x, core, tp]).astype(jnp.int32)
    )
    cosine, sine = rope_tables(depths)

    width = queries.shape[1] // 2
    top, low = halve(hidden)
    left_top = zn(top)
    right_low = zb(low)
    left_low = zn(low)
    right_top = zb(top)
    far_top = zn(left_top)
    far_low = zb(right_low)
    query_away = lax.dynamic_slice_in_dim(queries, (1 - core) * width, width, 1)
    upstream_away = lax.dynamic_slice_in_dim(upstream, (1 - core) * width, width, 1)
    query_peer = swap(query_away)
    upstream_peer = swap(upstream_away)
    hidden_peer = swap(hidden)
    place, hidden_peer, query_peer, upstream_peer = lax.optimization_barrier(
        (place, hidden_peer, query_peer, upstream_peer)
    )
    key_sum, value_sum = project_near(
        place, hidden, left_top, left_low, right_top, right_low, key_weight, value_weight
    )
    keep, send = project_far(
        place, far_top, far_low, key_weight, value_weight, key_sum, value_sum, cosine, sine
    )
    other = swap(send)
    mine_line = pack(keep, xn(keep), xb(keep), x2(keep))
    other_line = pack(other, yn(other), yb(other), y2(other))
    pieces = ring_gather(*mine_line, yn, yb) + ring_gather(*other_line, xn, xb)

    near_features = [left_top, left_low, right_top, right_low, far_top, far_low]
    own_features = [hidden, *near_features]
    peer_features = [hidden_peer]
    for feature in near_features:
        peer_features.append(swap(feature))
    features = flip(own_features, peer_features)

    out, *slot_grads = attend(table, queries, query_peer, upstream, upstream_peer, pieces)
    t_sent = send_all(slot_grads[:4], xn, xb, x2) + send_all(slot_grads[4:], yn, yb, y2)
    sums = combine(t_sent)
    t_last = send_all(sums[:4], yn, yb, y2) + send_all(sums[4:], xn, xb, x2)
    grads, grads_away = finish_grads(t_last, cosine, sine)
    grads_other = swap(grads_away)
    grads, grads_other = lax.optimization_barrier((grads, grads_other))

    out_other = swap(out[local_rows:])

    attention, query_grad = join_rows(place, out, out_other)

    w_parts = weight_partials(place, grads, features)
    w_sent = send_all(w_parts[:4], xn, xb, x2) + send_all(w_parts[4:], yn, yb, y2)
    parts = input_partials(place, grads, grads_other, key_weight, value_weight)
    _, from_back, from_next, from_far = send_all(parts, zn, zb, z2)
    hidden_grad = (
        parts[0].astype(F32)
        + from_back.astype(F32)
        + from_next.astype(F32)
        + from_far.astype(F32)
    ).astype(BF)
    w_sums = combine(w_sent)
    both, both_away = finish_weights(
        send_all(w_sums[:4], yn, yb, y2) + send_all(w_sums[4:], xn, xb, x2)
    )
    both_other = swap(both_away)
    key_weight_grad, value_weight_grad = join_weights(place, both, both_other)
    return (attention, query_grad, hidden_grad, key_weight_grad, value_weight_grad)


def solution(mesh):
    return jax.shard_map(
        program,
        mesh=mesh,
        in_specs=(
            P("ctx", "tp"),
            P("ctx", "tp"),
            P(None, "tp"),
            P(None, "tp"),
            P(),
            P("ctx", "tp"),
        ),
        out_specs=(P("ctx", "tp"), P("ctx", "tp"), P("ctx", "tp"), P("ctx", "tp"), P("ctx", "tp")),
        check_vma=False,
    )
```

```python
import math

import jax
import jax.numpy as jnp
from jax import lax
from jax.experimental import pallas as pl
from jax.experimental.pallas import tpu as pltpu
from jax.sharding import PartitionSpec as P

HD = 128
BLOCK = 128
DEPTH = 8
THETA = 1000000.0
NEGATIVE = -1e30
BF = jnp.bfloat16
F32 = jnp.float32
SCALE = 1.0 / math.sqrt(HD)
STACK = DEPTH - 1
SLOTS = STACK + 4
OFFSETS = (0, 3, 1, 2)


def side(delta):
    return jnp.where(delta == 0, 0, jnp.where(delta == 3, 1, jnp.where(delta == 1, 2, 3)))


def device_tables(parents, position):
    block_total = parents.shape[0]

    def body(links, where, table, place, depths, level):
        y, x, core, tp = where[0], where[1], where[2], where[3]
        first = 16 * y + 4 * x
        level[0] = 0

        def descend(b, carry):
            level[b] = level[links[b]] + 1
            return carry

        lax.fori_loop(1, block_total, descend, 0)
        place[0] = tp
        place[1] = (tp + 3) % 4
        place[2] = (tp + 1) % 4
        place[3] = (tp + 2) % 4
        place[4] = core
        for k, o in enumerate(OFFSETS):
            place[5 + k] = (tp + o) % 4
            place[9 + k] = side((y + o - tp + 4) % 4)
            place[13 + k] = (x + o) % 4
        table[AT_CORE] = core

        def blank(i, carry):
            table[AT_DENSE + i] = SLOTS
            return carry

        lax.fori_loop(0, 64, blank, 0)
        for r in range(4):
            table[AT_DENSE + r] = STACK + r
            block = first + (2 * core + r) % 4
            own_depth = level[block]
            depths[r] = own_depth
            table[AT_DEPTH + r] = own_depth
            node = block
            for d in range(DEPTH - 1, -1, -1):
                live = d <= own_depth
                slot = jnp.where(node >= first, STACK + (node - first + 4 - 2 * core) % 4, d)
                table[AT_SLOT + r * DEPTH + d] = jnp.where(live, slot, STACK + r)
                node = jnp.where(live, jnp.maximum(links[node], 0), node)
        lead_depth = level[first]
        node = first
        for d in range(STACK - 1, -1, -1):
            live = d < lead_depth
            node = jnp.where(live, jnp.maximum(links[node], 0), node)
            column = side((node // 4 + 4 - x) % 4)
            line = side((node // 16 + 4 - y) % 4)
            same = (node // 2) % 2 == core
            parity = node % 2
            outer = jnp.where(same, line, column)
            inner = jnp.where(same, column, line)
            piece = jnp.where(same, 0, 8) + outer * 2 + parity
            table[d] = jnp.where(live, piece, -1)
            table[AT_PLACE + d] = jnp.where(live, inner, 0)
            spot = AT_DENSE + (column * 4 + line) * 4 + (node + 4 - 2 * core) % 4

            @pl.when(live)
            def _(spot=spot, d=d):
                table[spot] = d

    smem = pl.BlockSpec(memory_space=pltpu.SMEM)
    return pl.pallas_call(
        body,
        in_specs=[smem, smem],
        out_specs=[smem] * 3,
        out_shape=[
            jax.ShapeDtypeStruct((AT_CORE + 1,), jnp.int32),
            jax.ShapeDtypeStruct((17,), jnp.int32),
            jax.ShapeDtypeStruct((4,), jnp.int32),
        ],
        scratch_shapes=[pltpu.SMEM((block_total,), jnp.int32)],
        compiler_params=params(1),
        name="device_tables",
    )(parents, position)


AT_PLACE = STACK
AT_DEPTH = 2 * STACK
AT_SLOT = AT_DEPTH + 4
AT_DENSE = AT_SLOT + 4 * DEPTH
AT_CORE = AT_DENSE + 64


def rope_tables(depths):
    offset = jnp.arange(BLOCK, dtype=jnp.int32)
    position = (depths[:, None] * BLOCK + offset[None, :]).astype(F32)
    frequency = jnp.exp(jnp.arange(HD // 2, dtype=F32) * (-2.0 * math.log(THETA) / HD))
    angles = (position[:, :, None] * frequency[None, None, :]).reshape(4 * BLOCK, HD // 2)
    cosine, sine = jnp.cos(angles), jnp.sin(angles)
    return (
        jnp.concatenate([cosine, cosine], axis=-1),
        jnp.concatenate([-sine, sine], axis=-1),
    )


def nn(a, b):
    return jnp.dot(a, b, preferred_element_type=F32)


def nt(a, b):
    return lax.dot_general(a, b, (((1,), (1,)), ((), ())), preferred_element_type=F32)


def tn(a, b):
    return lax.dot_general(a, b, (((0,), (0,)), ((), ())), preferred_element_type=F32)


def params(mib):
    return pltpu.CompilerParams(vmem_limit_bytes=mib * 1024 * 1024)


def halve(value):
    half = value.shape[0] // 2

    def body(source, top, low):
        top[...] = source[:half]
        low[...] = source[half:]

    return pl.pallas_call(
        body,
        in_specs=[pl.BlockSpec(memory_space=pltpu.VMEM)],
        out_specs=[pl.BlockSpec(memory_space=pltpu.VMEM)] * 2,
        out_shape=[jax.ShapeDtypeStruct((half, value.shape[1]), value.dtype)] * 2,
        compiler_params=params(3),
        name="halve",
    )(value)


def project_near(place, own, left_top, left_low, right_top, right_low, key_weight, value_weight):
    rows, width = own.shape
    cols = key_weight.shape[1]

    def body(place_ref, a, bt, bl, ct, cl, ka, kb, kc, va, vb, vc, key_out, value_out):
        b = jnp.concatenate([bt[...], bl[...]], axis=0)
        c = jnp.concatenate([ct[...], cl[...]], axis=0)
        key_out[...] = nn(a[...], ka[...]) + nn(b, kb[...]) + nn(c, kc[...])
        value_out[...] = nn(a[...], va[...]) + nn(b, vb[...]) + nn(c, vc[...])

    whole = pl.BlockSpec((rows, width), lambda i, p: (0, 0))
    half = pl.BlockSpec((rows // 2, width), lambda i, p: (0, 0))
    weights = [pl.BlockSpec((width, cols), lambda i, p, k=k: (p[k], 0)) for k in range(3)]
    out = pl.BlockSpec((rows, cols), lambda i, p: (0, 0))
    return pl.pallas_call(
        body,
        grid_spec=pltpu.PrefetchScalarGridSpec(
            num_scalar_prefetch=1,
            grid=(1,),
            in_specs=[whole] + [half] * 4 + weights + weights,
            out_specs=[out, out],
        ),
        out_shape=[jax.ShapeDtypeStruct((rows, cols), F32)] * 2,
        compiler_params=params(18),
        name="project_near",
    )(
        place,
        own,
        left_top,
        left_low,
        right_top,
        right_low,
        *([key_weight] * 3),
        *([value_weight] * 3),
    )


def pack(own, back, forth, far):
    def body(a, b, c, d, first, second):
        for k, ref in enumerate((a, b, c, d)):
            first[k] = ref[:BLOCK]
            second[k] = ref[BLOCK:]

    return pl.pallas_call(
        body,
        in_specs=[pl.BlockSpec(memory_space=pltpu.VMEM)] * 4,
        out_specs=[pl.BlockSpec(memory_space=pltpu.VMEM)] * 2,
        out_shape=[jax.ShapeDtypeStruct((4, BLOCK, 2 * HD), BF)] * 2,
        compiler_params=params(3),
        name="pack",
    )(own, back, forth, far)


def join_rows(place, mine, other):
    rows, cols = other.shape
    width = cols // 2

    def body(p, a, b, out, grad):
        swap = p[4] == 1
        for low, ref in ((0, out), (width, grad)):
            first = a[:rows, low : low + width]
            second = b[:, low : low + width]
            ref[:, :width] = jnp.where(swap, second, first)
            ref[:, width:] = jnp.where(swap, first, second)

    return pl.pallas_call(
        body,
        in_specs=[pl.BlockSpec(memory_space=pltpu.SMEM)]
        + [pl.BlockSpec(memory_space=pltpu.VMEM)] * 2,
        out_specs=[pl.BlockSpec(memory_space=pltpu.VMEM)] * 2,
        out_shape=[jax.ShapeDtypeStruct((rows, cols), BF)] * 2,
        compiler_params=params(5),
        name="join_rows",
    )(place, mine, other)


def join_weights(place, mine, other):
    share = mine.shape[0]

    def body(p, a, b, key, value):
        swap = p[4] == 1
        first = jnp.where(swap, b[...], a[...])
        second = jnp.where(swap, a[...], b[...])
        key[:, :HD] = first[:, :HD]
        key[:, HD:] = second[:, :HD]
        value[:, :HD] = first[:, HD:]
        value[:, HD:] = second[:, HD:]

    return pl.pallas_call(
        body,
        in_specs=[pl.BlockSpec(memory_space=pltpu.SMEM)]
        + [pl.BlockSpec(memory_space=pltpu.VMEM)] * 2,
        out_specs=[pl.BlockSpec(memory_space=pltpu.VMEM)] * 2,
        out_shape=[jax.ShapeDtypeStruct((share, 2 * HD), F32)] * 2,
        compiler_params=params(2),
        name="join_weights",
    )(place, mine, other)


def project_far(place, top, bottom, key_weight, value_weight, key_sum, value_sum, cosine, sine):
    rows, cols = key_sum.shape
    width = top.shape[1]
    half = rows // 2

    def body(p, a, b, kw, vw, ks, vs, cs, sn, keep, send):
        far = jnp.concatenate([a[...], b[...]], axis=0)
        key = ks[...] + nn(far, kw[...])
        value = vs[...] + nn(far, vw[...])
        heads = []
        for h in range(2):
            part = key[:, h * HD : (h + 1) * HD]
            turned = part * cs[...] + pltpu.roll(part, HD // 2, 1) * sn[...]
            heads.append(
                jnp.concatenate([turned, value[:, h * HD : (h + 1) * HD]], axis=1).astype(BF)
            )
        swap = p[4] == 1
        keep[...] = jnp.where(swap, heads[1], heads[0])
        send[...] = jnp.where(swap, heads[0], heads[1])

    weight = pl.BlockSpec((width, cols), lambda i, p: (p[3], 0))
    part = pl.BlockSpec((half, width), lambda i, p: (0, 0))
    sums = pl.BlockSpec((rows, cols), lambda i, p: (0, 0))
    angle = pl.BlockSpec((rows, HD), lambda i, p: (0, 0))
    return pl.pallas_call(
        body,
        grid_spec=pltpu.PrefetchScalarGridSpec(
            num_scalar_prefetch=1,
            grid=(1,),
            in_specs=[part, part, weight, weight, sums, sums, angle, angle],
            out_specs=[sums, sums],
        ),
        out_shape=[jax.ShapeDtypeStruct((rows, cols), BF)] * 2,
        compiler_params=params(8),
        name="project_far",
    )(place, top, bottom, key_weight, value_weight, key_sum, value_sum, cosine, sine)


def attend(table, queries, query_peer, upstream, upstream_peer, pieces):
    groups = queries.shape[1] // (2 * HD)
    width = groups * HD
    lanes = groups * BLOCK

    def body(t, q_own, q_far, u_own, u_far, *refs):
        parts = refs[:16]
        k_outs = refs[17:21]
        v_outs = refs[21:25]
        out = refs[16]
        kv, total, q_rows, u_rows = refs[25:]
        step = pl.program_id(0)

        @pl.when(step == 0)
        def _():
            for s in range(STACK):
                for index in range(16):

                    @pl.when(t[s] == index)
                    def _(s=s, index=index):
                        kv[s] = parts[index][t[AT_PLACE + s]]

            for r in range(4):
                kv[STACK + r] = parts[r if r < 2 else 6 + r][0]
            total[...] = jnp.zeros(total.shape, F32)

        own = step < 2
        q = jnp.where(own, q_own[...], q_far[...])
        u = jnp.where(own, u_own[...], u_far[...])
        for h in range(groups):
            q_rows[h * BLOCK : (h + 1) * BLOCK] = q[:, h * HD : (h + 1) * HD]
            u_rows[h * BLOCK : (h + 1) * BLOCK] = u[:, h * HD : (h + 1) * HD]
        q = q_rows[...]
        u = u_rows[...]
        depth = t[AT_DEPTH + step]
        slots = [t[AT_SLOT + step * DEPTH + d] for d in range(DEPTH)]
        keys = jnp.concatenate([kv[s, :, :HD] for s in slots], axis=0)
        values = jnp.concatenate([kv[s, :, HD:] for s in slots], axis=0)
        ahead = lax.broadcasted_iota(jnp.int32, (BLOCK, lanes), 0) - (
            lax.broadcasted_iota(jnp.int32, (BLOCK, lanes), 1) % BLOCK
        )
        raw = nt(keys, q)
        scores = []
        peak = None
        for d in range(DEPTH):
            reach = jnp.where(d < depth, BLOCK, jnp.where(d == depth, 0, -BLOCK))
            tile = jnp.where(
                ahead <= reach, raw[d * BLOCK : (d + 1) * BLOCK] * SCALE, NEGATIVE
            )
            scores.append(tile)
            top = jnp.max(tile, axis=0, keepdims=True)
            peak = top if peak is None else jnp.maximum(peak, top)
        weights = [jnp.exp(tile - peak) for tile in scores]
        mass = None
        for w in weights:
            part = jnp.sum(w, axis=0, keepdims=True)
            mass = part if mass is None else mass + part
        rounded = jnp.concatenate([w.astype(BF) for w in weights], axis=0)
        mixed = (tn(values, rounded) / mass).astype(BF).astype(F32)
        delta = jnp.sum(u.astype(F32).T * mixed, axis=0, keepdims=True)
        for h in range(groups):
            out[:, h * HD : (h + 1) * HD] = mixed[:, h * BLOCK : (h + 1) * BLOCK].T.astype(BF)
        inverse = 1.0 / mass
        slopes = nt(values, u)
        chances = []
        pulls = []
        for d in range(DEPTH):
            p = weights[d] * inverse
            chances.append(p.astype(BF))
            pulls.append((p * (slopes[d * BLOCK : (d + 1) * BLOCK] - delta)).astype(BF))
        chances = jnp.concatenate(chances, axis=0)
        pulls = jnp.concatenate(pulls, axis=0)
        turned = tn(keys, pulls) * SCALE
        for h in range(groups):
            out[:, width + h * HD : width + (h + 1) * HD] = (
                turned[:, h * BLOCK : (h + 1) * BLOCK].T.astype(BF)
            )
        v_part = nn(chances, u)
        k_part = nn(pulls, q) * SCALE
        for d in range(DEPTH):
            low = d * BLOCK
            total[slots[d], :, :HD] += k_part[low : low + BLOCK]
            total[slots[d], :, HD:] += v_part[low : low + BLOCK]

        @pl.when(step == 3)
        def _():
            for outer in range(4):

                def fill(i, carry, outer=outer):
                    k_slot = t[AT_DENSE + outer * 16 + i]
                    v_slot = t[AT_DENSE + (i // 4) * 16 + outer * 4 + i % 4]
                    k = total[k_slot, :, :HD]
                    v = total[v_slot, :, HD:]
                    k_outs[outer][i] = k.astype(k_outs[outer].dtype)
                    v_outs[outer][i] = v.astype(v_outs[outer].dtype)
                    return carry

                lax.fori_loop(0, 16, fill, 0)

    mine = pl.BlockSpec((BLOCK, width), lambda i, t: (jnp.minimum(i, 1), t[AT_CORE]))
    peer = pl.BlockSpec((BLOCK, width), lambda i, t: (jnp.maximum(i - 2, 0), 0))
    rows = pl.BlockSpec((BLOCK, 2 * width), lambda i, t: (i, 0))

    def full(shape):
        return pl.BlockSpec(
            shape, lambda i, t: (0,) * len(shape), pipeline_mode=pl.Buffered(1)
        )

    def held(shape):
        return pl.BlockSpec(shape, lambda i, t: (0,) * len(shape))

    wide = (16, BLOCK, HD)
    grads = [(wide, F32)] + [(wide, BF)] * 3
    return pl.pallas_call(
        body,
        grid_spec=pltpu.PrefetchScalarGridSpec(
            num_scalar_prefetch=1,
            grid=(4,),
            in_specs=[mine, peer, mine, peer] + [full(p.shape) for p in pieces],
            out_specs=[rows] + [held(s) for s, _ in grads + grads],
            scratch_shapes=[
                pltpu.VMEM((SLOTS, BLOCK, 2 * HD), BF),
                pltpu.VMEM((SLOTS + 1, BLOCK, 2 * HD), F32),
                pltpu.VMEM((lanes, HD), BF),
                pltpu.VMEM((lanes, HD), BF),
            ],
        ),
        out_shape=[jax.ShapeDtypeStruct((4 * BLOCK, 2 * width), BF)]
        + [jax.ShapeDtypeStruct(s, d) for s, d in grads + grads],
        compiler_params=params(36),
        name="attend",
    )(table, queries, query_peer, upstream, upstream_peer, *pieces)


def combine(sums):
    def body(*refs):
        for side_of in range(2):
            home, a, b, c = refs[4 * side_of : 4 * side_of + 4]
            outs = refs[8 + 4 * side_of : 12 + 4 * side_of]
            rows = outs[0].shape[0]
            for k in range(4):
                at = slice(k * rows, (k + 1) * rows)
                outs[k][...] = (
                    home[at] + a[at].astype(F32) + b[at].astype(F32) + c[at].astype(F32)
                )

    shape = sums[0].shape
    part = (shape[0] // 4,) + shape[1:]
    return pl.pallas_call(
        body,
        in_specs=[pl.BlockSpec(memory_space=pltpu.VMEM)] * 8,
        out_specs=[pl.BlockSpec(memory_space=pltpu.VMEM)] * 8,
        out_shape=[jax.ShapeDtypeStruct(part, F32)] * 8,
        compiler_params=params(8),
        name="combine",
    )(*sums)


def finish_grads(sums, cosine, sine):
    rows = 4 * BLOCK

    def body(*refs):
        ks, vs = refs[:4], refs[4:8]
        cs, sn, every, away = refs[8:]
        key = (ks[0][...] + ks[1][...] + ks[2][...] + ks[3][...]).reshape(rows, HD)
        value = (vs[0][...] + vs[1][...] + vs[2][...] + vs[3][...]).reshape(rows, HD)
        key = key * cs[...] - pltpu.roll(key, HD // 2, 1) * sn[...]
        both = jnp.concatenate([key.astype(BF), value.astype(BF)], axis=1)
        every[...] = both
        away[...] = both[rows // 2 :]

    return pl.pallas_call(
        body,
        in_specs=[pl.BlockSpec(memory_space=pltpu.VMEM)] * 10,
        out_specs=[pl.BlockSpec(memory_space=pltpu.VMEM)] * 2,
        out_shape=[
            jax.ShapeDtypeStruct((rows, 2 * HD), BF),
            jax.ShapeDtypeStruct((rows // 2, 2 * HD), BF),
        ],
        compiler_params=params(5),
        name="finish_grads",
    )(*sums, cosine, sine)


def finish_weights(sums):
    share = sums[0].shape[1]

    def body(*refs):
        ks, vs = refs[:4], refs[4:8]
        for row, out in enumerate(refs[8:]):
            out[:, :HD] = ks[0][row] + ks[1][row] + ks[2][row] + ks[3][row]
            out[:, HD:] = vs[0][row] + vs[1][row] + vs[2][row] + vs[3][row]

    return pl.pallas_call(
        body,
        in_specs=[pl.BlockSpec(memory_space=pltpu.VMEM)] * 8,
        out_specs=[pl.BlockSpec(memory_space=pltpu.VMEM)] * 2,
        out_shape=[jax.ShapeDtypeStruct((share, 2 * HD), F32)] * 2,
        compiler_params=params(4),
        name="finish_weights",
    )(*sums)


def input_partials(place, mine, other, key_weight, value_weight):
    rows = other.shape[0]
    cols = key_weight.shape[1]
    width = key_weight.shape[0] // 4

    def body(p, a, b, kw, vw, *outs):
        swap = p[4] == 1
        first = jnp.where(swap, b[...], a[...])
        second = jnp.where(swap, a[...], b[...])
        key = jnp.concatenate([first[:, :HD], second[:, :HD]], axis=1)
        value = jnp.concatenate([first[:, HD:], second[:, HD:]], axis=1)
        result = (nt(key, kw[...]) + nt(value, vw[...])).astype(BF)
        for k in range(4):

            @pl.when(pl.program_id(0) == k)
            def _(k=k):
                outs[k][...] = result

    grads = pl.BlockSpec((rows, 2 * HD), lambda i, p: (0, 0))
    weight = pl.BlockSpec((width, cols), lambda i, p: (p[5 + i], 0))
    out = pl.BlockSpec((rows, width), lambda i, p: (0, 0), pipeline_mode=pl.Buffered(1))
    return pl.pallas_call(
        body,
        grid_spec=pltpu.PrefetchScalarGridSpec(
            num_scalar_prefetch=1,
            grid=(4,),
            in_specs=[grads, grads, weight, weight],
            out_specs=[out] * 4,
        ),
        out_shape=[jax.ShapeDtypeStruct((rows, width), BF)] * 4,
        compiler_params=params(7),
        name="input_partials",
    )(place, mine, other, key_weight, value_weight)


def flip(own, peer):
    width = own[0].shape[1]
    rows = 4 * BLOCK

    def body(*refs):
        mine, other, out = refs[:7], refs[7:14], refs[14]
        for piece in range(4):
            at = slice(max(2 * piece - 1, 0), 2 * piece + 1)
            features = jnp.concatenate([r[...] for r in mine[at] + other[at]], axis=0)
            out[piece] = features.T

    return pl.pallas_call(
        body,
        in_specs=[pl.BlockSpec(memory_space=pltpu.VMEM)] * 14,
        out_specs=pl.BlockSpec(memory_space=pltpu.VMEM),
        out_shape=jax.ShapeDtypeStruct((4, width, rows), BF),
        compiler_params=params(12),
        name="flip",
    )(*own, *peer)


def weight_partials(place, grads, features):
    width = features.shape[1]
    share = width // 8

    def body(p, g, ft, *refs):
        k_outs, v_outs, result = refs[:4], refs[4:8], refs[8]
        core = p[4]
        grad = g[...]
        for dy in range(4):
            result[...] = nn(ft[p[9 + dy]], grad)
            for dx in range(4):
                base = p[13 + dx] * (2 * share)
                for r in range(2):
                    start = pl.multiple_of(base + ((core + r) % 2) * share, 16)
                    value = result[pl.ds(start, share), :]
                    k_outs[dx][dy * 2 + r] = value[:, :HD].astype(k_outs[dx].dtype)
                    v_outs[dy][dx * 2 + r] = value[:, HD:].astype(v_outs[dy].dtype)

    wide = (8, share, HD)
    shapes = [(wide, F32)] + [(wide, BF)] * 3
    return pl.pallas_call(
        body,
        in_specs=[pl.BlockSpec(memory_space=pltpu.SMEM)]
        + [pl.BlockSpec(memory_space=pltpu.VMEM)] * 2,
        out_specs=[pl.BlockSpec(memory_space=pltpu.VMEM)] * 8,
        out_shape=[jax.ShapeDtypeStruct(s, d) for s, d in shapes + shapes],
        scratch_shapes=[pltpu.VMEM((width, 2 * HD), F32)],
        compiler_params=params(11),
        name="weight_partials",
    )(place, grads, features)


def mover(axis, pairs):
    return lambda value: lax.ppermute(value, axis, pairs)


def ring_gather(first, second, ahead, behind):
    back_first = ahead(first)
    next_second = behind(second)
    back_second = ahead(second)
    next_first = behind(first)
    far_first = ahead(back_first)
    far_second = behind(next_second)
    return [
        first,
        second,
        back_first,
        back_second,
        next_first,
        next_second,
        far_first,
        far_second,
    ]


def send_all(values, ahead, behind, across):
    home, back, forth, far = values
    near = ahead(forth)
    distant = across(far)
    other = behind(back)
    return [home, near, other, distant]


def program(hidden, queries, key_weight, value_weight, parents, upstream):
    place_ctx = lax.axis_index("ctx")
    tp = lax.axis_index("tp")
    core = place_ctx % 2
    x = (place_ctx // 2) % 4
    y = place_ctx // 8
    xn = mover("ctx", [(i, i // 8 * 8 + (i + 2) % 8) for i in range(32)])
    xb = mover("ctx", [(i, i // 8 * 8 + (i - 2) % 8) for i in range(32)])
    yn = mover("ctx", [(i, (i + 8) % 32) for i in range(32)])
    yb = mover("ctx", [(i, (i - 8) % 32) for i in range(32)])
    swap = mover("ctx", [(i, i ^ 1) for i in range(32)])
    zn = mover("tp", [(i, (i + 1) % 4) for i in range(4)])
    zb = mover("tp", [(i, (i - 1) % 4) for i in range(4)])
    x2 = mover("ctx", [(i, i // 8 * 8 + (i + 4) % 8) for i in range(32)])
    y2 = mover("ctx", [(i, (i + 16) % 32) for i in range(32)])
    z2 = mover("tp", [(i, (i + 2) % 4) for i in range(4)])

    local_rows = hidden.shape[0]
    table, place, depths = device_tables(
        parents, jnp.stack([y, x, core, tp]).astype(jnp.int32)
    )
    cosine, sine = rope_tables(depths)

    width = queries.shape[1] // 2
    top, low = halve(hidden)
    left_top = zn(top)
    right_low = zb(low)
    left_low = zn(low)
    right_top = zb(top)
    far_top = zn(left_top)
    far_low = zb(right_low)
    query_away = lax.dynamic_slice_in_dim(queries, (1 - core) * width, width, 1)
    upstream_away = lax.dynamic_slice_in_dim(upstream, (1 - core) * width, width, 1)
    query_peer = swap(query_away)
    upstream_peer = swap(upstream_away)
    hidden_peer = swap(hidden)
    place, hidden_peer, query_peer, upstream_peer = lax.optimization_barrier(
        (place, hidden_peer, query_peer, upstream_peer)
    )
    key_sum, value_sum = project_near(
        place, hidden, left_top, left_low, right_top, right_low, key_weight, value_weight
    )
    keep, send = project_far(
        place, far_top, far_low, key_weight, value_weight, key_sum, value_sum, cosine, sine
    )
    other = swap(send)
    mine_line = pack(keep, xn(keep), xb(keep), x2(keep))
    other_line = pack(other, yn(other), yb(other), y2(other))
    pieces = ring_gather(*mine_line, yn, yb) + ring_gather(*other_line, xn, xb)

    near_features = [left_top, left_low, right_top, right_low, far_top, far_low]
    own_features = [hidden, *near_features]
    peer_features = [hidden_peer]
    for feature in near_features:
        peer_features.append(swap(feature))
    features = flip(own_features, peer_features)

    out, *slot_grads = attend(table, queries, query_peer, upstream, upstream_peer, pieces)
    t_sent = send_all(slot_grads[:4], xn, xb, x2) + send_all(slot_grads[4:], yn, yb, y2)
    sums = combine(t_sent)
    t_last = send_all(sums[:4], yn, yb, y2) + send_all(sums[4:], xn, xb, x2)
    grads, grads_away = finish_grads(t_last, cosine, sine)
    grads_other = swap(grads_away)
    grads, grads_other = lax.optimization_barrier((grads, grads_other))

    out_other = swap(out[local_rows:])

    attention, query_grad = join_rows(place, out, out_other)

    w_parts = weight_partials(place, grads, features)
    w_sent = send_all(w_parts[:4], xn, xb, x2) + send_all(w_parts[4:], yn, yb, y2)
    parts = input_partials(place, grads, grads_other, key_weight, value_weight)
    _, from_back, from_next, from_far = send_all(parts, zn, zb, z2)
    hidden_grad = (
        parts[0].astype(F32)
        + from_back.astype(F32)
        + from_next.astype(F32)
        + from_far.astype(F32)
    ).astype(BF)
    w_sums = combine(w_sent)
    w_last = send_all(w_sums[:4], yn, yb, y2) + send_all(w_sums[4:], xn, xb, x2)
    both, both_away = finish_weights(w_last)
    both_other = swap(both_away)
    key_weight_grad, value_weight_grad = join_weights(place, both, both_other)
    return (attention, query_grad, hidden_grad, key_weight_grad, value_weight_grad)


def solution(mesh):
    return jax.shard_map(
        program,
        mesh=mesh,
        in_specs=(
            P("ctx", "tp"),
            P("ctx", "tp"),
            P(None, "tp"),
            P(None, "tp"),
            P(),
            P("ctx", "tp"),
        ),
        out_specs=(P("ctx", "tp"), P("ctx", "tp"), P("ctx", "tp"), P("ctx", "tp"), P("ctx", "tp")),
        check_vma=False,
    )
```

```python
import math

import jax
import jax.numpy as jnp
from jax import lax
from jax.experimental import pallas as pl
from jax.experimental.pallas import tpu as pltpu
from jax.sharding import PartitionSpec as P

HD = 128
BLOCK = 128
DEPTH = 8
THETA = 1000000.0
NEGATIVE = -1e30
BF = jnp.bfloat16
F32 = jnp.float32
SCALE = 1.0 / math.sqrt(HD)
STACK = DEPTH - 1
SLOTS = STACK + 4
OFFSETS = (0, 3, 1, 2)


def side(delta):
    return jnp.where(delta == 0, 0, jnp.where(delta == 3, 1, jnp.where(delta == 1, 2, 3)))


def device_tables(parents, position):
    block_total = parents.shape[0]

    def body(links, where, table, place, depths, level):
        y, x, core, tp = where[0], where[1], where[2], where[3]
        first = 16 * y + 4 * x
        level[0] = 0

        def descend(b, carry):
            level[b] = level[links[b]] + 1
            return carry

        lax.fori_loop(1, block_total, descend, 0)
        place[0] = tp
        place[1] = (tp + 3) % 4
        place[2] = (tp + 1) % 4
        place[3] = (tp + 2) % 4
        place[4] = core
        for k, o in enumerate(OFFSETS):
            place[5 + k] = (tp + o) % 4
            place[9 + k] = side((y + o - tp + 4) % 4)
            place[13 + k] = (x + o) % 4
        table[AT_CORE] = core

        def blank(i, carry):
            table[AT_DENSE + i] = SLOTS
            return carry

        lax.fori_loop(0, 64, blank, 0)
        for r in range(4):
            table[AT_DENSE + r] = STACK + r
            block = first + (2 * core + r) % 4
            own_depth = level[block]
            depths[r] = own_depth
            table[AT_DEPTH + r] = own_depth
            node = block
            for d in range(DEPTH - 1, -1, -1):
                live = d <= own_depth
                slot = jnp.where(node >= first, STACK + (node - first + 4 - 2 * core) % 4, d)
                table[AT_SLOT + r * DEPTH + d] = jnp.where(live, slot, STACK + r)
                node = jnp.where(live, jnp.maximum(links[node], 0), node)
        lead_depth = level[first]
        node = first
        for d in range(STACK - 1, -1, -1):
            live = d < lead_depth
            node = jnp.where(live, jnp.maximum(links[node], 0), node)
            column = side((node // 4 + 4 - x) % 4)
            line = side((node // 16 + 4 - y) % 4)
            same = (node // 2) % 2 == core
            parity = node % 2
            outer = jnp.where(same, line, column)
            inner = jnp.where(same, column, line)
            piece = jnp.where(same, 0, 8) + outer * 2 + parity
            table[d] = jnp.where(live, piece, -1)
            table[AT_PLACE + d] = jnp.where(live, inner, 0)
            spot = AT_DENSE + (column * 4 + line) * 4 + (node + 4 - 2 * core) % 4

            @pl.when(live)
            def _(spot=spot, d=d):
                table[spot] = d

    smem = pl.BlockSpec(memory_space=pltpu.SMEM)
    return pl.pallas_call(
        body,
        in_specs=[smem, smem],
        out_specs=[smem] * 3,
        out_shape=[
            jax.ShapeDtypeStruct((AT_CORE + 1,), jnp.int32),
            jax.ShapeDtypeStruct((17,), jnp.int32),
            jax.ShapeDtypeStruct((4,), jnp.int32),
        ],
        scratch_shapes=[pltpu.SMEM((block_total,), jnp.int32)],
        compiler_params=params(1),
        name="device_tables",
    )(parents, position)


AT_PLACE = STACK
AT_DEPTH = 2 * STACK
AT_SLOT = AT_DEPTH + 4
AT_DENSE = AT_SLOT + 4 * DEPTH
AT_CORE = AT_DENSE + 64


def rope_tables(depths):
    offset = jnp.arange(BLOCK, dtype=jnp.int32)
    position = (depths[:, None] * BLOCK + offset[None, :]).astype(F32)
    frequency = jnp.exp(jnp.arange(HD // 2, dtype=F32) * (-2.0 * math.log(THETA) / HD))
    angles = (position[:, :, None] * frequency[None, None, :]).reshape(4 * BLOCK, HD // 2)
    cosine, sine = jnp.cos(angles), jnp.sin(angles)
    return (
        jnp.concatenate([cosine, cosine], axis=-1),
        jnp.concatenate([-sine, sine], axis=-1),
    )


def nn(a, b):
    return jnp.dot(a, b, preferred_element_type=F32)


def nt(a, b):
    return lax.dot_general(a, b, (((1,), (1,)), ((), ())), preferred_element_type=F32)


def tn(a, b):
    return lax.dot_general(a, b, (((0,), (0,)), ((), ())), preferred_element_type=F32)


def params(mib):
    return pltpu.CompilerParams(vmem_limit_bytes=mib * 1024 * 1024)


def halve(value):
    half = value.shape[0] // 2

    def body(source, top, low):
        top[...] = source[:half]
        low[...] = source[half:]

    return pl.pallas_call(
        body,
        in_specs=[pl.BlockSpec(memory_space=pltpu.VMEM)],
        out_specs=[pl.BlockSpec(memory_space=pltpu.VMEM)] * 2,
        out_shape=[jax.ShapeDtypeStruct((half, value.shape[1]), value.dtype)] * 2,
        compiler_params=params(3),
        name="halve",
    )(value)


def project_near(place, own, left_top, left_low, right_top, right_low, key_weight, value_weight):
    rows, width = own.shape
    cols = key_weight.shape[1]

    def body(place_ref, a, bt, bl, ct, cl, ka, kb, kc, va, vb, vc, key_out, value_out):
        b = jnp.concatenate([bt[...], bl[...]], axis=0)
        c = jnp.concatenate([ct[...], cl[...]], axis=0)
        key_out[...] = nn(a[...], ka[...]) + nn(b, kb[...]) + nn(c, kc[...])
        value_out[...] = nn(a[...], va[...]) + nn(b, vb[...]) + nn(c, vc[...])

    whole = pl.BlockSpec((rows, width), lambda i, p: (0, 0))
    half = pl.BlockSpec((rows // 2, width), lambda i, p: (0, 0))
    weights = [pl.BlockSpec((width, cols), lambda i, p, k=k: (p[k], 0)) for k in range(3)]
    out = pl.BlockSpec((rows, cols), lambda i, p: (0, 0))
    return pl.pallas_call(
        body,
        grid_spec=pltpu.PrefetchScalarGridSpec(
            num_scalar_prefetch=1,
            grid=(1,),
            in_specs=[whole] + [half] * 4 + weights + weights,
            out_specs=[out, out],
        ),
        out_shape=[jax.ShapeDtypeStruct((rows, cols), F32)] * 2,
        compiler_params=params(18),
        name="project_near",
    )(
        place,
        own,
        left_top,
        left_low,
        right_top,
        right_low,
        *([key_weight] * 3),
        *([value_weight] * 3),
    )


def pack(own, back, forth, far):
    def body(a, b, c, d, first, second):
        for k, ref in enumerate((a, b, c, d)):
            first[k] = ref[:BLOCK]
            second[k] = ref[BLOCK:]

    return pl.pallas_call(
        body,
        in_specs=[pl.BlockSpec(memory_space=pltpu.VMEM)] * 4,
        out_specs=[pl.BlockSpec(memory_space=pltpu.VMEM)] * 2,
        out_shape=[jax.ShapeDtypeStruct((4, BLOCK, 2 * HD), BF)] * 2,
        compiler_params=params(3),
        name="pack",
    )(own, back, forth, far)


def join_rows(place, mine, other):
    rows, cols = other.shape
    width = cols // 2

    def body(p, a, b, out, grad):
        swap = p[4] == 1
        for low, ref in ((0, out), (width, grad)):
            first = a[:rows, low : low + width]
            second = b[:, low : low + width]
            ref[:, :width] = jnp.where(swap, second, first)
            ref[:, width:] = jnp.where(swap, first, second)

    return pl.pallas_call(
        body,
        in_specs=[pl.BlockSpec(memory_space=pltpu.SMEM)]
        + [pl.BlockSpec(memory_space=pltpu.VMEM)] * 2,
        out_specs=[pl.BlockSpec(memory_space=pltpu.VMEM)] * 2,
        out_shape=[jax.ShapeDtypeStruct((rows, cols), BF)] * 2,
        compiler_params=params(5),
        name="join_rows",
    )(place, mine, other)


def add_partials(*parts):
    def body(a, b, c, d, out):
        out[...] = (
            a[...].astype(F32) + b[...].astype(F32) + c[...].astype(F32) + d[...].astype(F32)
        ).astype(BF)

    return pl.pallas_call(
        body,
        in_specs=[pl.BlockSpec(memory_space=pltpu.VMEM)] * 4,
        out_specs=pl.BlockSpec(memory_space=pltpu.VMEM),
        out_shape=jax.ShapeDtypeStruct(parts[0].shape, BF),
        compiler_params=params(5),
        name="add_partials",
    )(*parts)


def join_weights(place, mine, other):
    share = mine.shape[0]

    def body(p, a, b, key, value):
        swap = p[4] == 1
        first = jnp.where(swap, b[...], a[...])
        second = jnp.where(swap, a[...], b[...])
        key[:, :HD] = first[:, :HD]
        key[:, HD:] = second[:, :HD]
        value[:, :HD] = first[:, HD:]
        value[:, HD:] = second[:, HD:]

    return pl.pallas_call(
        body,
        in_specs=[pl.BlockSpec(memory_space=pltpu.SMEM)]
        + [pl.BlockSpec(memory_space=pltpu.VMEM)] * 2,
        out_specs=[pl.BlockSpec(memory_space=pltpu.VMEM)] * 2,
        out_shape=[jax.ShapeDtypeStruct((share, 2 * HD), F32)] * 2,
        compiler_params=params(2),
        name="join_weights",
    )(place, mine, other)


def project_far(place, top, bottom, key_weight, value_weight, key_sum, value_sum, cosine, sine):
    rows, cols = key_sum.shape
    width = top.shape[1]
    half = rows // 2

    def body(p, a, b, kw, vw, ks, vs, cs, sn, keep, send):
        far = jnp.concatenate([a[...], b[...]], axis=0)
        key = ks[...] + nn(far, kw[...])
        value = vs[...] + nn(far, vw[...])
        heads = []
        for h in range(2):
            part = key[:, h * HD : (h + 1) * HD]
            turned = part * cs[...] + pltpu.roll(part, HD // 2, 1) * sn[...]
            heads.append(
                jnp.concatenate([turned, value[:, h * HD : (h + 1) * HD]], axis=1).astype(BF)
            )
        swap = p[4] == 1
        keep[...] = jnp.where(swap, heads[1], heads[0])
        send[...] = jnp.where(swap, heads[0], heads[1])

    weight = pl.BlockSpec((width, cols), lambda i, p: (p[3], 0))
    part = pl.BlockSpec((half, width), lambda i, p: (0, 0))
    sums = pl.BlockSpec((rows, cols), lambda i, p: (0, 0))
    angle = pl.BlockSpec((rows, HD), lambda i, p: (0, 0))
    return pl.pallas_call(
        body,
        grid_spec=pltpu.PrefetchScalarGridSpec(
            num_scalar_prefetch=1,
            grid=(1,),
            in_specs=[part, part, weight, weight, sums, sums, angle, angle],
            out_specs=[sums, sums],
        ),
        out_shape=[jax.ShapeDtypeStruct((rows, cols), BF)] * 2,
        compiler_params=params(8),
        name="project_far",
    )(place, top, bottom, key_weight, value_weight, key_sum, value_sum, cosine, sine)


def attend(table, queries, query_peer, upstream, upstream_peer, pieces):
    groups = queries.shape[1] // (2 * HD)
    width = groups * HD
    lanes = groups * BLOCK

    def body(t, q_own, q_far, u_own, u_far, *refs):
        parts = refs[:16]
        k_outs = refs[17:21]
        v_outs = refs[21:25]
        out = refs[16]
        kv, total, q_rows, u_rows = refs[25:]
        step = pl.program_id(0)

        @pl.when(step == 0)
        def _():
            for s in range(STACK):
                for index in range(16):

                    @pl.when(t[s] == index)
                    def _(s=s, index=index):
                        kv[s] = parts[index][t[AT_PLACE + s]]

            for r in range(4):
                kv[STACK + r] = parts[r if r < 2 else 6 + r][0]
            total[...] = jnp.zeros(total.shape, F32)

        own = step < 2
        q = jnp.where(own, q_own[...], q_far[...])
        u = jnp.where(own, u_own[...], u_far[...])
        for h in range(groups):
            q_rows[h * BLOCK : (h + 1) * BLOCK] = q[:, h * HD : (h + 1) * HD]
            u_rows[h * BLOCK : (h + 1) * BLOCK] = u[:, h * HD : (h + 1) * HD]
        q = q_rows[...]
        u = u_rows[...]
        depth = t[AT_DEPTH + step]
        slots = [t[AT_SLOT + step * DEPTH + d] for d in range(DEPTH)]
        keys = jnp.concatenate([kv[s, :, :HD] for s in slots], axis=0)
        values = jnp.concatenate([kv[s, :, HD:] for s in slots], axis=0)
        ahead = lax.broadcasted_iota(jnp.int32, (BLOCK, lanes), 0) - (
            lax.broadcasted_iota(jnp.int32, (BLOCK, lanes), 1) % BLOCK
        )
        raw = nt(keys, q)
        scores = []
        peak = None
        for d in range(DEPTH):
            reach = jnp.where(d < depth, BLOCK, jnp.where(d == depth, 0, -BLOCK))
            tile = jnp.where(
                ahead <= reach, raw[d * BLOCK : (d + 1) * BLOCK] * SCALE, NEGATIVE
            )
            scores.append(tile)
            top = jnp.max(tile, axis=0, keepdims=True)
            peak = top if peak is None else jnp.maximum(peak, top)
        weights = [jnp.exp(tile - peak) for tile in scores]
        mass = None
        for w in weights:
            part = jnp.sum(w, axis=0, keepdims=True)
            mass = part if mass is None else mass + part
        rounded = jnp.concatenate([w.astype(BF) for w in weights], axis=0)
        mixed = (tn(values, rounded) / mass).astype(BF).astype(F32)
        delta = jnp.sum(u.astype(F32).T * mixed, axis=0, keepdims=True)
        for h in range(groups):
            out[:, h * HD : (h + 1) * HD] = mixed[:, h * BLOCK : (h + 1) * BLOCK].T.astype(BF)
        inverse = 1.0 / mass
        slopes = nt(values, u)
        chances = []
        pulls = []
        for d in range(DEPTH):
            p = weights[d] * inverse
            chances.append(p.astype(BF))
            pulls.append((p * (slopes[d * BLOCK : (d + 1) * BLOCK] - delta)).astype(BF))
        chances = jnp.concatenate(chances, axis=0)
        pulls = jnp.concatenate(pulls, axis=0)
        turned = tn(keys, pulls) * SCALE
        for h in range(groups):
            out[:, width + h * HD : width + (h + 1) * HD] = (
                turned[:, h * BLOCK : (h + 1) * BLOCK].T.astype(BF)
            )
        v_part = nn(chances, u)
        k_part = nn(pulls, q) * SCALE
        for d in range(DEPTH):
            low = d * BLOCK
            total[slots[d], :, :HD] += k_part[low : low + BLOCK]
            total[slots[d], :, HD:] += v_part[low : low + BLOCK]

        @pl.when(step == 3)
        def _():
            for outer in range(4):

                def fill(i, carry, outer=outer):
                    k_slot = t[AT_DENSE + outer * 16 + i]
                    v_slot = t[AT_DENSE + (i // 4) * 16 + outer * 4 + i % 4]
                    k = total[k_slot, :, :HD]
                    v = total[v_slot, :, HD:]
                    k_outs[outer][i] = k.astype(k_outs[outer].dtype)
                    v_outs[outer][i] = v.astype(v_outs[outer].dtype)
                    return carry

                lax.fori_loop(0, 16, fill, 0)

    mine = pl.BlockSpec((BLOCK, width), lambda i, t: (jnp.minimum(i, 1), t[AT_CORE]))
    peer = pl.BlockSpec((BLOCK, width), lambda i, t: (jnp.maximum(i - 2, 0), 0))
    rows = pl.BlockSpec((BLOCK, 2 * width), lambda i, t: (i, 0))

    def full(shape):
        return pl.BlockSpec(
            shape, lambda i, t: (0,) * len(shape), pipeline_mode=pl.Buffered(1)
        )

    def held(shape):
        return pl.BlockSpec(shape, lambda i, t: (0,) * len(shape))

    wide = (16, BLOCK, HD)
    grads = [(wide, F32)] + [(wide, BF)] * 3
    return pl.pallas_call(
        body,
        grid_spec=pltpu.PrefetchScalarGridSpec(
            num_scalar_prefetch=1,
            grid=(4,),
            in_specs=[mine, peer, mine, peer] + [full(p.shape) for p in pieces],
            out_specs=[rows] + [held(s) for s, _ in grads + grads],
            scratch_shapes=[
                pltpu.VMEM((SLOTS, BLOCK, 2 * HD), BF),
                pltpu.VMEM((SLOTS + 1, BLOCK, 2 * HD), F32),
                pltpu.VMEM((lanes, HD), BF),
                pltpu.VMEM((lanes, HD), BF),
            ],
        ),
        out_shape=[jax.ShapeDtypeStruct((4 * BLOCK, 2 * width), BF)]
        + [jax.ShapeDtypeStruct(s, d) for s, d in grads + grads],
        compiler_params=pltpu.CompilerParams(vmem_limit_bytes=36 * 1024 * 1024),
        name="attend",
    )(table, queries, query_peer, upstream, upstream_peer, *pieces)


def combine(sums):
    def body(*refs):
        for side_of in range(2):
            home, a, b, c = refs[4 * side_of : 4 * side_of + 4]
            outs = refs[8 + 4 * side_of : 12 + 4 * side_of]
            rows = outs[0].shape[0]
            for k in range(4):
                at = slice(k * rows, (k + 1) * rows)
                outs[k][...] = (
                    home[at] + a[at].astype(F32) + b[at].astype(F32) + c[at].astype(F32)
                )

    shape = sums[0].shape
    part = (shape[0] // 4,) + shape[1:]
    return pl.pallas_call(
        body,
        in_specs=[pl.BlockSpec(memory_space=pltpu.VMEM)] * 8,
        out_specs=[pl.BlockSpec(memory_space=pltpu.VMEM)] * 8,
        out_shape=[jax.ShapeDtypeStruct(part, F32)] * 8,
        compiler_params=params(8),
        name="combine",
    )(*sums)


def finish_grads(sums, cosine, sine):
    rows = 4 * BLOCK

    def body(*refs):
        ks, vs = refs[:4], refs[4:8]
        cs, sn, every, away = refs[8:]
        key = (ks[0][...] + ks[1][...] + ks[2][...] + ks[3][...]).reshape(rows, HD)
        value = (vs[0][...] + vs[1][...] + vs[2][...] + vs[3][...]).reshape(rows, HD)
        key = key * cs[...] - pltpu.roll(key, HD // 2, 1) * sn[...]
        both = jnp.concatenate([key.astype(BF), value.astype(BF)], axis=1)
        every[...] = both
        away[...] = both[rows // 2 :]

    return pl.pallas_call(
        body,
        in_specs=[pl.BlockSpec(memory_space=pltpu.VMEM)] * 10,
        out_specs=[pl.BlockSpec(memory_space=pltpu.VMEM)] * 2,
        out_shape=[
            jax.ShapeDtypeStruct((rows, 2 * HD), BF),
            jax.ShapeDtypeStruct((rows // 2, 2 * HD), BF),
        ],
        compiler_params=params(5),
        name="finish_grads",
    )(*sums, cosine, sine)


def finish_weights(sums):
    share = sums[0].shape[1]

    def body(*refs):
        ks, vs = refs[:4], refs[4:8]
        for row, out in enumerate(refs[8:]):
            out[:, :HD] = ks[0][row] + ks[1][row] + ks[2][row] + ks[3][row]
            out[:, HD:] = vs[0][row] + vs[1][row] + vs[2][row] + vs[3][row]

    return pl.pallas_call(
        body,
        in_specs=[pl.BlockSpec(memory_space=pltpu.VMEM)] * 8,
        out_specs=[pl.BlockSpec(memory_space=pltpu.VMEM)] * 2,
        out_shape=[jax.ShapeDtypeStruct((share, 2 * HD), F32)] * 2,
        compiler_params=params(4),
        name="finish_weights",
    )(*sums)


def input_partials(place, mine, other, key_weight, value_weight):
    rows = other.shape[0]
    cols = key_weight.shape[1]
    width = key_weight.shape[0] // 4

    def body(p, a, b, kw, vw, *outs):
        swap = p[4] == 1
        first = jnp.where(swap, b[...], a[...])
        second = jnp.where(swap, a[...], b[...])
        key = jnp.concatenate([first[:, :HD], second[:, :HD]], axis=1)
        value = jnp.concatenate([first[:, HD:], second[:, HD:]], axis=1)
        result = (nt(key, kw[...]) + nt(value, vw[...])).astype(BF)
        for k in range(4):

            @pl.when(pl.program_id(0) == k)
            def _(k=k):
                outs[k][...] = result

    grads = pl.BlockSpec((rows, 2 * HD), lambda i, p: (0, 0))
    weight = pl.BlockSpec((width, cols), lambda i, p: (p[5 + i], 0))
    out = pl.BlockSpec((rows, width), lambda i, p: (0, 0), pipeline_mode=pl.Buffered(1))
    return pl.pallas_call(
        body,
        grid_spec=pltpu.PrefetchScalarGridSpec(
            num_scalar_prefetch=1,
            grid=(4,),
            in_specs=[grads, grads, weight, weight],
            out_specs=[out] * 4,
        ),
        out_shape=[jax.ShapeDtypeStruct((rows, width), BF)] * 4,
        compiler_params=params(7),
        name="input_partials",
    )(place, mine, other, key_weight, value_weight)


def flip(own, peer):
    width = own[0].shape[1]
    rows = 4 * BLOCK

    def body(*refs):
        mine, other, out = refs[:7], refs[7:14], refs[14]
        for piece in range(4):
            at = slice(max(2 * piece - 1, 0), 2 * piece + 1)
            features = jnp.concatenate([r[...] for r in mine[at] + other[at]], axis=0)
            out[piece] = features.T

    return pl.pallas_call(
        body,
        in_specs=[pl.BlockSpec(memory_space=pltpu.VMEM)] * 14,
        out_specs=pl.BlockSpec(memory_space=pltpu.VMEM),
        out_shape=jax.ShapeDtypeStruct((4, width, rows), BF),
        compiler_params=params(12),
        name="flip",
    )(*own, *peer)


def weight_partials(place, grads, features):
    width = features.shape[1]
    share = width // 8

    def body(p, g, ft, *refs):
        k_outs, v_outs, result = refs[:4], refs[4:8], refs[8]
        core = p[4]
        grad = g[...]
        for dy in range(4):
            result[...] = nn(ft[p[9 + dy]], grad)
            for dx in range(4):
                base = p[13 + dx] * (2 * share)
                for r in range(2):
                    start = pl.multiple_of(base + ((core + r) % 2) * share, 16)
                    value = result[pl.ds(start, share), :]
                    k_outs[dx][dy * 2 + r] = value[:, :HD].astype(k_outs[dx].dtype)
                    v_outs[dy][dx * 2 + r] = value[:, HD:].astype(v_outs[dy].dtype)

    wide = (8, share, HD)
    shapes = [(wide, F32)] + [(wide, BF)] * 3
    return pl.pallas_call(
        body,
        in_specs=[pl.BlockSpec(memory_space=pltpu.SMEM)]
        + [pl.BlockSpec(memory_space=pltpu.VMEM)] * 2,
        out_specs=[pl.BlockSpec(memory_space=pltpu.VMEM)] * 8,
        out_shape=[jax.ShapeDtypeStruct(s, d) for s, d in shapes + shapes],
        scratch_shapes=[pltpu.VMEM((width, 2 * HD), F32)],
        compiler_params=params(11),
        name="weight_partials",
    )(place, grads, features)


def mover(axis, pairs):
    return lambda value: lax.ppermute(value, axis, pairs)


def spread(value, ahead, behind, across):
    far = across(value)
    back = ahead(value)
    forth = behind(value)
    return [value, back, forth, far]


def ring_gather(first, second, ahead, behind):
    back_first = ahead(first)
    next_second = behind(second)
    back_second = ahead(second)
    next_first = behind(first)
    far_first = ahead(back_first)
    far_second = behind(next_second)
    return [
        first,
        second,
        back_first,
        back_second,
        next_first,
        next_second,
        far_first,
        far_second,
    ]


def send_all(values, ahead, behind, across):
    home, back, forth, far = values
    near = ahead(forth)
    distant = across(far)
    other = behind(back)
    return [home, near, other, distant]


def program(hidden, queries, key_weight, value_weight, parents, upstream):
    place_ctx = lax.axis_index("ctx")
    tp = lax.axis_index("tp")
    core = place_ctx % 2
    x = (place_ctx // 2) % 4
    y = place_ctx // 8
    xn = mover("ctx", [(i, i // 8 * 8 + (i + 2) % 8) for i in range(32)])
    xb = mover("ctx", [(i, i // 8 * 8 + (i - 2) % 8) for i in range(32)])
    yn = mover("ctx", [(i, (i + 8) % 32) for i in range(32)])
    yb = mover("ctx", [(i, (i - 8) % 32) for i in range(32)])
    swap = mover("ctx", [(i, i ^ 1) for i in range(32)])
    zn = mover("tp", [(i, (i + 1) % 4) for i in range(4)])
    zb = mover("tp", [(i, (i - 1) % 4) for i in range(4)])
    x2 = mover("ctx", [(i, i // 8 * 8 + (i + 4) % 8) for i in range(32)])
    y2 = mover("ctx", [(i, (i + 16) % 32) for i in range(32)])
    z2 = mover("tp", [(i, (i + 2) % 4) for i in range(4)])

    local_rows = hidden.shape[0]
    table, place, depths = device_tables(
        parents, jnp.stack([y, x, core, tp]).astype(jnp.int32)
    )
    cosine, sine = rope_tables(depths)

    width = queries.shape[1] // 2
    top, low = halve(hidden)
    left_top = zn(top)
    right_low = zb(low)
    left_low = zn(low)
    right_top = zb(top)
    far_top = zn(left_top)
    far_low = zb(right_low)
    query_away = lax.dynamic_slice_in_dim(queries, (1 - core) * width, width, 1)
    upstream_away = lax.dynamic_slice_in_dim(upstream, (1 - core) * width, width, 1)
    query_peer = swap(query_away)
    upstream_peer = swap(upstream_away)
    hidden_peer = swap(hidden)
    place, hidden_peer, query_peer, upstream_peer = lax.optimization_barrier(
        (place, hidden_peer, query_peer, upstream_peer)
    )
    key_sum, value_sum = project_near(
        place, hidden, left_top, left_low, right_top, right_low, key_weight, value_weight
    )
    keep, send = project_far(
        place, far_top, far_low, key_weight, value_weight, key_sum, value_sum, cosine, sine
    )
    other = swap(send)
    mine_line = pack(*spread(keep, xn, xb, x2))
    other_line = pack(*spread(other, yn, yb, y2))
    pieces = ring_gather(*mine_line, yn, yb) + ring_gather(*other_line, xn, xb)

    near_features = [left_top, left_low, right_top, right_low, far_top, far_low]
    own_features = [hidden, *near_features]
    peer_features = [hidden_peer]
    for feature in near_features:
        peer_features.append(swap(feature))
    features = flip(own_features, peer_features)

    out, *slot_grads = attend(table, queries, query_peer, upstream, upstream_peer, pieces)
    t_sent = send_all(slot_grads[:4], xn, xb, x2) + send_all(slot_grads[4:], yn, yb, y2)
    sums = combine(t_sent)
    t_last = send_all(sums[:4], yn, yb, y2) + send_all(sums[4:], xn, xb, x2)
    grads, grads_away = finish_grads(t_last, cosine, sine)
    grads_other = swap(grads_away)

    out_other = swap(out[local_rows:])

    attention, query_grad = join_rows(place, out, out_other)

    w_parts = weight_partials(place, grads, features)
    w_sent = send_all(w_parts[:4], xn, xb, x2) + send_all(w_parts[4:], yn, yb, y2)
    parts = input_partials(place, grads, grads_other, key_weight, value_weight)
    _, from_back, from_next, from_far = send_all(parts, zn, zb, z2)
    hidden_grad = add_partials(parts[0], from_back, from_next, from_far)
    w_sums = combine(w_sent)
    w_last = send_all(w_sums[:4], yn, yb, y2) + send_all(w_sums[4:], xn, xb, x2)
    both, both_away = finish_weights(w_last)
    both_other = swap(both_away)
    key_weight_grad, value_weight_grad = join_weights(place, both, both_other)
    return (attention, query_grad, hidden_grad, key_weight_grad, value_weight_grad)


def solution(mesh):
    return jax.shard_map(
        program,
        mesh=mesh,
        in_specs=(
            P("ctx", "tp"),
            P("ctx", "tp"),
            P(None, "tp"),
            P(None, "tp"),
            P(),
            P("ctx", "tp"),
        ),
        out_specs=(P("ctx", "tp"), P("ctx", "tp"), P("ctx", "tp"), P("ctx", "tp"), P("ctx", "tp")),
        check_vma=False,
    )
```

```python
import math

import jax
import jax.numpy as jnp
from jax import lax
from jax.experimental import pallas as pl
from jax.experimental.pallas import tpu as pltpu
from jax.sharding import PartitionSpec as P

HD = 128
BLOCK = 128
DEPTH = 8
THETA = 1000000.0
NEGATIVE = -1e30
BF = jnp.bfloat16
F32 = jnp.float32
SCALE = 1.0 / math.sqrt(HD)
STACK = DEPTH - 1
SLOTS = STACK + 4
OFFSETS = (0, 3, 1, 2)


def side(delta):
    return jnp.where(delta == 0, 0, jnp.where(delta == 3, 1, jnp.where(delta == 1, 2, 3)))


def device_tables(parents, position):
    block_total = parents.shape[0]

    def body(links, where, table, place, depths, level):
        y, x, core, tp = where[0], where[1], where[2], where[3]
        first = 16 * y + 4 * x
        level[0] = 0

        def descend(b, carry):
            level[b] = level[links[b]] + 1
            return carry

        lax.fori_loop(1, block_total, descend, 0)
        place[0] = tp
        place[1] = (tp + 3) % 4
        place[2] = (tp + 1) % 4
        place[3] = (tp + 2) % 4
        place[4] = core
        for k, o in enumerate(OFFSETS):
            place[5 + k] = (tp + o) % 4
            place[9 + k] = side((y + o - tp + 4) % 4)
            place[13 + k] = (x + o) % 4
        table[AT_CORE] = core

        def blank(i, carry):
            table[AT_DENSE + i] = SLOTS
            return carry

        lax.fori_loop(0, 64, blank, 0)
        for r in range(4):
            table[AT_DENSE + r] = STACK + r
            block = first + (2 * core + r) % 4
            own_depth = level[block]
            depths[r] = own_depth
            table[AT_DEPTH + r] = own_depth
            node = block
            for d in range(DEPTH - 1, -1, -1):
                live = d <= own_depth
                slot = jnp.where(node >= first, STACK + (node - first + 4 - 2 * core) % 4, d)
                table[AT_SLOT + r * DEPTH + d] = jnp.where(live, slot, STACK + r)
                node = jnp.where(live, jnp.maximum(links[node], 0), node)
        lead_depth = level[first]
        node = first
        for d in range(STACK - 1, -1, -1):
            live = d < lead_depth
            node = jnp.where(live, jnp.maximum(links[node], 0), node)
            column = side((node // 4 + 4 - x) % 4)
            line = side((node // 16 + 4 - y) % 4)
            same = (node // 2) % 2 == core
            parity = node % 2
            outer = jnp.where(same, line, column)
            inner = jnp.where(same, column, line)
            piece = jnp.where(same, 0, 8) + outer * 2 + parity
            table[d] = jnp.where(live, piece, -1)
            table[AT_PLACE + d] = jnp.where(live, inner, 0)
            spot = AT_DENSE + (column * 4 + line) * 4 + (node + 4 - 2 * core) % 4

            @pl.when(live)
            def _(spot=spot, d=d):
                table[spot] = d

    smem = pl.BlockSpec(memory_space=pltpu.SMEM)
    return pl.pallas_call(
        body,
        in_specs=[smem, smem],
        out_specs=[smem] * 3,
        out_shape=[
            jax.ShapeDtypeStruct((AT_CORE + 1,), jnp.int32),
            jax.ShapeDtypeStruct((17,), jnp.int32),
            jax.ShapeDtypeStruct((4,), jnp.int32),
        ],
        scratch_shapes=[pltpu.SMEM((block_total,), jnp.int32)],
        compiler_params=params(1),
        name="device_tables",
    )(parents, position)


AT_PLACE = STACK
AT_DEPTH = 2 * STACK
AT_SLOT = AT_DEPTH + 4
AT_DENSE = AT_SLOT + 4 * DEPTH
AT_CORE = AT_DENSE + 64


def rope_tables(depths):
    offset = jnp.arange(BLOCK, dtype=jnp.int32)
    position = (depths[:, None] * BLOCK + offset[None, :]).astype(F32)
    frequency = jnp.exp(jnp.arange(HD // 2, dtype=F32) * (-2.0 * math.log(THETA) / HD))
    angles = (position[:, :, None] * frequency[None, None, :]).reshape(4 * BLOCK, HD // 2)
    cosine, sine = jnp.cos(angles), jnp.sin(angles)
    return (
        jnp.concatenate([cosine, cosine], axis=-1),
        jnp.concatenate([-sine, sine], axis=-1),
    )


def nn(a, b):
    return jnp.dot(a, b, preferred_element_type=F32)


def nt(a, b):
    return lax.dot_general(a, b, (((1,), (1,)), ((), ())), preferred_element_type=F32)


def tn(a, b):
    return lax.dot_general(a, b, (((0,), (0,)), ((), ())), preferred_element_type=F32)


def params(mib):
    return pltpu.CompilerParams(vmem_limit_bytes=mib * 1024 * 1024)


def halve(value):
    half = value.shape[0] // 2

    def body(source, top, low):
        top[...] = source[:half]
        low[...] = source[half:]

    return pl.pallas_call(
        body,
        in_specs=[pl.BlockSpec(memory_space=pltpu.VMEM)],
        out_specs=[pl.BlockSpec(memory_space=pltpu.VMEM)] * 2,
        out_shape=[jax.ShapeDtypeStruct((half, value.shape[1]), value.dtype)] * 2,
        compiler_params=params(3),
        name="halve",
    )(value)


def project_near(place, own, left_top, left_low, right_top, right_low, key_weight, value_weight):
    rows, width = own.shape
    cols = key_weight.shape[1]

    def body(place_ref, a, bt, bl, ct, cl, ka, kb, kc, va, vb, vc, key_out, value_out):
        b = jnp.concatenate([bt[...], bl[...]], axis=0)
        c = jnp.concatenate([ct[...], cl[...]], axis=0)
        key_out[...] = nn(a[...], ka[...]) + nn(b, kb[...]) + nn(c, kc[...])
        value_out[...] = nn(a[...], va[...]) + nn(b, vb[...]) + nn(c, vc[...])

    whole = pl.BlockSpec((rows, width), lambda i, p: (0, 0))
    half = pl.BlockSpec((rows // 2, width), lambda i, p: (0, 0))
    weights = [pl.BlockSpec((width, cols), lambda i, p, k=k: (p[k], 0)) for k in range(3)]
    out = pl.BlockSpec((rows, cols), lambda i, p: (0, 0))
    return pl.pallas_call(
        body,
        grid_spec=pltpu.PrefetchScalarGridSpec(
            num_scalar_prefetch=1,
            grid=(1,),
            in_specs=[whole] + [half] * 4 + weights + weights,
            out_specs=[out, out],
        ),
        out_shape=[jax.ShapeDtypeStruct((rows, cols), F32)] * 2,
        compiler_params=params(18),
        name="project_near",
    )(
        place,
        own,
        left_top,
        left_low,
        right_top,
        right_low,
        *([key_weight] * 3),
        *([value_weight] * 3),
    )


def pack(own, back, forth, far):
    def body(a, b, c, d, first, second):
        for k, ref in enumerate((a, b, c, d)):
            first[k] = ref[:BLOCK]
            second[k] = ref[BLOCK:]

    return pl.pallas_call(
        body,
        in_specs=[pl.BlockSpec(memory_space=pltpu.VMEM)] * 4,
        out_specs=[pl.BlockSpec(memory_space=pltpu.VMEM)] * 2,
        out_shape=[jax.ShapeDtypeStruct((4, BLOCK, 2 * HD), BF)] * 2,
        compiler_params=params(3),
        name="pack",
    )(own, back, forth, far)


def join_rows(place, mine, other):
    rows, cols = other.shape
    width = cols // 2

    def body(p, a, b, out, grad):
        swap = p[4] == 1
        for low, ref in ((0, out), (width, grad)):
            first = a[:rows, low : low + width]
            second = b[:, low : low + width]
            ref[:, :width] = jnp.where(swap, second, first)
            ref[:, width:] = jnp.where(swap, first, second)

    return pl.pallas_call(
        body,
        in_specs=[pl.BlockSpec(memory_space=pltpu.SMEM)]
        + [pl.BlockSpec(memory_space=pltpu.VMEM)] * 2,
        out_specs=[pl.BlockSpec(memory_space=pltpu.VMEM)] * 2,
        out_shape=[jax.ShapeDtypeStruct((rows, cols), BF)] * 2,
        compiler_params=params(5),
        name="join_rows",
    )(place, mine, other)


def add_partials(*parts):
    def body(a, b, c, d, out):
        out[...] = (
            a[...].astype(F32) + b[...].astype(F32) + c[...].astype(F32) + d[...].astype(F32)
        ).astype(BF)

    return pl.pallas_call(
        body,
        in_specs=[pl.BlockSpec(memory_space=pltpu.VMEM)] * 4,
        out_specs=pl.BlockSpec(memory_space=pltpu.VMEM),
        out_shape=jax.ShapeDtypeStruct(parts[0].shape, BF),
        compiler_params=params(5),
        name="add_partials",
    )(*parts)


def join_weights(place, mine, other):
    share = mine.shape[0]

    def body(p, a, b, key, value):
        swap = p[4] == 1
        first = jnp.where(swap, b[...], a[...])
        second = jnp.where(swap, a[...], b[...])
        key[:, :HD] = first[:, :HD]
        key[:, HD:] = second[:, :HD]
        value[:, :HD] = first[:, HD:]
        value[:, HD:] = second[:, HD:]

    return pl.pallas_call(
        body,
        in_specs=[pl.BlockSpec(memory_space=pltpu.SMEM)]
        + [pl.BlockSpec(memory_space=pltpu.VMEM)] * 2,
        out_specs=[pl.BlockSpec(memory_space=pltpu.VMEM)] * 2,
        out_shape=[jax.ShapeDtypeStruct((share, 2 * HD), F32)] * 2,
        compiler_params=params(2),
        name="join_weights",
    )(place, mine, other)


def project_far(place, top, bottom, key_weight, value_weight, key_sum, value_sum, cosine, sine):
    rows, cols = key_sum.shape
    width = top.shape[1]
    half = rows // 2

    def body(p, a, b, kw, vw, ks, vs, cs, sn, keep, send):
        far = jnp.concatenate([a[...], b[...]], axis=0)
        key = ks[...] + nn(far, kw[...])
        value = vs[...] + nn(far, vw[...])
        heads = []
        for h in range(2):
            part = key[:, h * HD : (h + 1) * HD]
            turned = part * cs[...] + pltpu.roll(part, HD // 2, 1) * sn[...]
            heads.append(
                jnp.concatenate([turned, value[:, h * HD : (h + 1) * HD]], axis=1).astype(BF)
            )
        swap = p[4] == 1
        keep[...] = jnp.where(swap, heads[1], heads[0])
        send[...] = jnp.where(swap, heads[0], heads[1])

    weight = pl.BlockSpec((width, cols), lambda i, p: (p[3], 0))
    part = pl.BlockSpec((half, width), lambda i, p: (0, 0))
    sums = pl.BlockSpec((rows, cols), lambda i, p: (0, 0))
    angle = pl.BlockSpec((rows, HD), lambda i, p: (0, 0))
    return pl.pallas_call(
        body,
        grid_spec=pltpu.PrefetchScalarGridSpec(
            num_scalar_prefetch=1,
            grid=(1,),
            in_specs=[part, part, weight, weight, sums, sums, angle, angle],
            out_specs=[sums, sums],
        ),
        out_shape=[jax.ShapeDtypeStruct((rows, cols), BF)] * 2,
        compiler_params=params(8),
        name="project_far",
    )(place, top, bottom, key_weight, value_weight, key_sum, value_sum, cosine, sine)


def attend(table, queries, query_peer, upstream, upstream_peer, pieces):
    groups = queries.shape[1] // (2 * HD)
    width = groups * HD
    lanes = groups * BLOCK

    def body(t, q_own, q_far, u_own, u_far, *refs):
        parts = refs[:16]
        k_outs = refs[17:21]
        v_outs = refs[21:25]
        out = refs[16]
        kv, total, q_rows, u_rows = refs[25:]
        step = pl.program_id(0)

        @pl.when(step == 0)
        def _():
            for s in range(STACK):
                for index in range(16):

                    @pl.when(t[s] == index)
                    def _(s=s, index=index):
                        kv[s] = parts[index][t[AT_PLACE + s]]

            for r in range(4):
                kv[STACK + r] = parts[r if r < 2 else 6 + r][0]
            total[...] = jnp.zeros(total.shape, F32)

        own = step < 2
        q = jnp.where(own, q_own[...], q_far[...])
        u = jnp.where(own, u_own[...], u_far[...])
        for h in range(groups):
            q_rows[h * BLOCK : (h + 1) * BLOCK] = q[:, h * HD : (h + 1) * HD]
            u_rows[h * BLOCK : (h + 1) * BLOCK] = u[:, h * HD : (h + 1) * HD]
        q = q_rows[...]
        u = u_rows[...]
        depth = t[AT_DEPTH + step]
        slots = [t[AT_SLOT + step * DEPTH + d] for d in range(DEPTH)]
        keys = jnp.concatenate([kv[s, :, :HD] for s in slots], axis=0)
        values = jnp.concatenate([kv[s, :, HD:] for s in slots], axis=0)
        ahead = lax.broadcasted_iota(jnp.int32, (BLOCK, lanes), 0) - (
            lax.broadcasted_iota(jnp.int32, (BLOCK, lanes), 1) % BLOCK
        )
        raw = nt(keys, q)
        scores = []
        peak = None
        for d in range(DEPTH):
            reach = jnp.where(d < depth, BLOCK, jnp.where(d == depth, 0, -BLOCK))
            tile = jnp.where(
                ahead <= reach, raw[d * BLOCK : (d + 1) * BLOCK] * SCALE, NEGATIVE
            )
            scores.append(tile)
            top = jnp.max(tile, axis=0, keepdims=True)
            peak = top if peak is None else jnp.maximum(peak, top)
        weights = [jnp.exp(tile - peak) for tile in scores]
        mass = None
        for w in weights:
            part = jnp.sum(w, axis=0, keepdims=True)
            mass = part if mass is None else mass + part
        rounded = jnp.concatenate([w.astype(BF) for w in weights], axis=0)
        mixed = (tn(values, rounded) / mass).astype(BF).astype(F32)
        delta = jnp.sum(u.astype(F32).T * mixed, axis=0, keepdims=True)
        for h in range(groups):
            out[:, h * HD : (h + 1) * HD] = mixed[:, h * BLOCK : (h + 1) * BLOCK].T.astype(BF)
        inverse = 1.0 / mass
        slopes = nt(values, u)
        chances = []
        pulls = []
        for d in range(DEPTH):
            p = weights[d] * inverse
            chances.append(p.astype(BF))
            pulls.append((p * (slopes[d * BLOCK : (d + 1) * BLOCK] - delta)).astype(BF))
        chances = jnp.concatenate(chances, axis=0)
        pulls = jnp.concatenate(pulls, axis=0)
        turned = tn(keys, pulls) * SCALE
        for h in range(groups):
            out[:, width + h * HD : width + (h + 1) * HD] = (
                turned[:, h * BLOCK : (h + 1) * BLOCK].T.astype(BF)
            )
        v_part = nn(chances, u)
        k_part = nn(pulls, q) * SCALE
        for d in range(DEPTH):
            low = d * BLOCK
            total[slots[d], :, :HD] += k_part[low : low + BLOCK]
            total[slots[d], :, HD:] += v_part[low : low + BLOCK]

        @pl.when(step == 3)
        def _():
            for outer in range(4):

                def fill(i, carry, outer=outer):
                    k_slot = t[AT_DENSE + outer * 16 + i]
                    v_slot = t[AT_DENSE + (i // 4) * 16 + outer * 4 + i % 4]
                    k = total[k_slot, :, :HD]
                    v = total[v_slot, :, HD:]
                    k_outs[outer][i] = k.astype(k_outs[outer].dtype)
                    v_outs[outer][i] = v.astype(v_outs[outer].dtype)
                    return carry

                lax.fori_loop(0, 16, fill, 0)

    mine = pl.BlockSpec((BLOCK, width), lambda i, t: (jnp.minimum(i, 1), t[AT_CORE]))
    peer = pl.BlockSpec((BLOCK, width), lambda i, t: (jnp.maximum(i - 2, 0), 0))
    rows = pl.BlockSpec((BLOCK, 2 * width), lambda i, t: (i, 0))

    def full(shape):
        return pl.BlockSpec(
            shape, lambda i, t: (0,) * len(shape), pipeline_mode=pl.Buffered(1)
        )

    def held(shape):
        return pl.BlockSpec(shape, lambda i, t: (0,) * len(shape))

    wide = (16, BLOCK, HD)
    grads = [(wide, F32)] + [(wide, BF)] * 3
    return pl.pallas_call(
        body,
        grid_spec=pltpu.PrefetchScalarGridSpec(
            num_scalar_prefetch=1,
            grid=(4,),
            in_specs=[mine, peer, mine, peer] + [full(p.shape) for p in pieces],
            out_specs=[rows] + [held(s) for s, _ in grads + grads],
            scratch_shapes=[
                pltpu.VMEM((SLOTS, BLOCK, 2 * HD), BF),
                pltpu.VMEM((SLOTS + 1, BLOCK, 2 * HD), F32),
                pltpu.VMEM((lanes, HD), BF),
                pltpu.VMEM((lanes, HD), BF),
            ],
        ),
        out_shape=[jax.ShapeDtypeStruct((4 * BLOCK, 2 * width), BF)]
        + [jax.ShapeDtypeStruct(s, d) for s, d in grads + grads],
        compiler_params=params(36),
        name="attend",
    )(table, queries, query_peer, upstream, upstream_peer, *pieces)


def combine(sums):
    def body(*refs):
        for side_of in range(2):
            home, a, b, c = refs[4 * side_of : 4 * side_of + 4]
            outs = refs[8 + 4 * side_of : 12 + 4 * side_of]
            rows = outs[0].shape[0]
            for k in range(4):
                at = slice(k * rows, (k + 1) * rows)
                outs[k][...] = (
                    home[at] + a[at].astype(F32) + b[at].astype(F32) + c[at].astype(F32)
                )

    shape = sums[0].shape
    part = (shape[0] // 4,) + shape[1:]
    return pl.pallas_call(
        body,
        in_specs=[pl.BlockSpec(memory_space=pltpu.VMEM)] * 8,
        out_specs=[pl.BlockSpec(memory_space=pltpu.VMEM)] * 8,
        out_shape=[jax.ShapeDtypeStruct(part, F32)] * 8,
        compiler_params=params(8),
        name="combine",
    )(*sums)


def finish_grads(sums, cosine, sine):
    rows = 4 * BLOCK

    def body(*refs):
        ks, vs = refs[:4], refs[4:8]
        cs, sn, every, away = refs[8:]
        key = (ks[0][...] + ks[1][...] + ks[2][...] + ks[3][...]).reshape(rows, HD)
        value = (vs[0][...] + vs[1][...] + vs[2][...] + vs[3][...]).reshape(rows, HD)
        key = key * cs[...] - pltpu.roll(key, HD // 2, 1) * sn[...]
        both = jnp.concatenate([key.astype(BF), value.astype(BF)], axis=1)
        every[...] = both
        away[...] = both[rows // 2 :]

    return pl.pallas_call(
        body,
        in_specs=[pl.BlockSpec(memory_space=pltpu.VMEM)] * 10,
        out_specs=[pl.BlockSpec(memory_space=pltpu.VMEM)] * 2,
        out_shape=[
            jax.ShapeDtypeStruct((rows, 2 * HD), BF),
            jax.ShapeDtypeStruct((rows // 2, 2 * HD), BF),
        ],
        compiler_params=params(5),
        name="finish_grads",
    )(*sums, cosine, sine)


def finish_weights(sums):
    share = sums[0].shape[1]

    def body(*refs):
        ks, vs = refs[:4], refs[4:8]
        for row, out in enumerate(refs[8:]):
            out[:, :HD] = ks[0][row] + ks[1][row] + ks[2][row] + ks[3][row]
            out[:, HD:] = vs[0][row] + vs[1][row] + vs[2][row] + vs[3][row]

    return pl.pallas_call(
        body,
        in_specs=[pl.BlockSpec(memory_space=pltpu.VMEM)] * 8,
        out_specs=[pl.BlockSpec(memory_space=pltpu.VMEM)] * 2,
        out_shape=[jax.ShapeDtypeStruct((share, 2 * HD), F32)] * 2,
        compiler_params=params(4),
        name="finish_weights",
    )(*sums)


def input_partials(place, mine, other, key_weight, value_weight):
    rows = other.shape[0]
    cols = key_weight.shape[1]
    width = key_weight.shape[0] // 4

    def body(p, a, b, kw, vw, *outs):
        swap = p[4] == 1
        first = jnp.where(swap, b[...], a[...])
        second = jnp.where(swap, a[...], b[...])
        key = jnp.concatenate([first[:, :HD], second[:, :HD]], axis=1)
        value = jnp.concatenate([first[:, HD:], second[:, HD:]], axis=1)
        result = (nt(key, kw[...]) + nt(value, vw[...])).astype(BF)
        for k in range(4):

            @pl.when(pl.program_id(0) == k)
            def _(k=k):
                outs[k][...] = result

    grads = pl.BlockSpec((rows, 2 * HD), lambda i, p: (0, 0))
    weight = pl.BlockSpec((width, cols), lambda i, p: (p[5 + i], 0))
    out = pl.BlockSpec((rows, width), lambda i, p: (0, 0), pipeline_mode=pl.Buffered(1))
    return pl.pallas_call(
        body,
        grid_spec=pltpu.PrefetchScalarGridSpec(
            num_scalar_prefetch=1,
            grid=(4,),
            in_specs=[grads, grads, weight, weight],
            out_specs=[out] * 4,
        ),
        out_shape=[jax.ShapeDtypeStruct((rows, width), BF)] * 4,
        compiler_params=params(7),
        name="input_partials",
    )(place, mine, other, key_weight, value_weight)


def flip(own, peer):
    width = own[0].shape[1]
    rows = 4 * BLOCK

    def body(*refs):
        mine, other, out = refs[:7], refs[7:14], refs[14]
        for piece in range(4):
            at = slice(max(2 * piece - 1, 0), 2 * piece + 1)
            features = jnp.concatenate([r[...] for r in mine[at] + other[at]], axis=0)
            out[piece] = features.T

    return pl.pallas_call(
        body,
        in_specs=[pl.BlockSpec(memory_space=pltpu.VMEM)] * 14,
        out_specs=pl.BlockSpec(memory_space=pltpu.VMEM),
        out_shape=jax.ShapeDtypeStruct((4, width, rows), BF),
        compiler_params=params(12),
        name="flip",
    )(*own, *peer)


def weight_partials(place, grads, features):
    width = features.shape[1]
    share = width // 8

    def body(p, g, ft, *refs):
        k_outs, v_outs, result = refs[:4], refs[4:8], refs[8]
        core = p[4]
        grad = g[...]
        for dy in range(4):
            result[...] = nn(ft[p[9 + dy]], grad)
            for dx in range(4):
                base = p[13 + dx] * (2 * share)
                for r in range(2):
                    start = pl.multiple_of(base + ((core + r) % 2) * share, 16)
                    value = result[pl.ds(start, share), :]
                    k_outs[dx][dy * 2 + r] = value[:, :HD].astype(k_outs[dx].dtype)
                    v_outs[dy][dx * 2 + r] = value[:, HD:].astype(v_outs[dy].dtype)

    wide = (8, share, HD)
    shapes = [(wide, F32)] + [(wide, BF)] * 3
    return pl.pallas_call(
        body,
        in_specs=[pl.BlockSpec(memory_space=pltpu.SMEM)]
        + [pl.BlockSpec(memory_space=pltpu.VMEM)] * 2,
        out_specs=[pl.BlockSpec(memory_space=pltpu.VMEM)] * 8,
        out_shape=[jax.ShapeDtypeStruct(s, d) for s, d in shapes + shapes],
        scratch_shapes=[pltpu.VMEM((width, 2 * HD), F32)],
        compiler_params=params(11),
        name="weight_partials",
    )(place, grads, features)


def mover(axis, pairs):
    return lambda value: lax.ppermute(value, axis, pairs)


def ring_gather(first, second, ahead, behind):
    back_first = ahead(first)
    next_second = behind(second)
    back_second = ahead(second)
    next_first = behind(first)
    far_first = ahead(back_first)
    far_second = behind(next_second)
    return [
        first,
        second,
        back_first,
        back_second,
        next_first,
        next_second,
        far_first,
        far_second,
    ]


def send_all(values, ahead, behind, across):
    home, back, forth, far = values
    near = ahead(forth)
    distant = across(far)
    other = behind(back)
    return [home, near, other, distant]


def program(hidden, queries, key_weight, value_weight, parents, upstream):
    place_ctx = lax.axis_index("ctx")
    tp = lax.axis_index("tp")
    core = place_ctx % 2
    x = (place_ctx // 2) % 4
    y = place_ctx // 8
    xn = mover("ctx", [(i, i // 8 * 8 + (i + 2) % 8) for i in range(32)])
    xb = mover("ctx", [(i, i // 8 * 8 + (i - 2) % 8) for i in range(32)])
    yn = mover("ctx", [(i, (i + 8) % 32) for i in range(32)])
    yb = mover("ctx", [(i, (i - 8) % 32) for i in range(32)])
    swap = mover("ctx", [(i, i ^ 1) for i in range(32)])
    zn = mover("tp", [(i, (i + 1) % 4) for i in range(4)])
    zb = mover("tp", [(i, (i - 1) % 4) for i in range(4)])
    x2 = mover("ctx", [(i, i // 8 * 8 + (i + 4) % 8) for i in range(32)])
    y2 = mover("ctx", [(i, (i + 16) % 32) for i in range(32)])
    z2 = mover("tp", [(i, (i + 2) % 4) for i in range(4)])

    local_rows = hidden.shape[0]
    table, place, depths = device_tables(
        parents, jnp.stack([y, x, core, tp]).astype(jnp.int32)
    )
    cosine, sine = rope_tables(depths)

    width = queries.shape[1] // 2
    top, low = halve(hidden)
    left_top = zn(top)
    right_low = zb(low)
    left_low = zn(low)
    right_top = zb(top)
    far_top = zn(left_top)
    far_low = zb(right_low)
    query_away = lax.dynamic_slice_in_dim(queries, (1 - core) * width, width, 1)
    upstream_away = lax.dynamic_slice_in_dim(upstream, (1 - core) * width, width, 1)
    query_peer = swap(query_away)
    upstream_peer = swap(upstream_away)
    hidden_peer = swap(hidden)
    place, hidden_peer, query_peer, upstream_peer = lax.optimization_barrier(
        (place, hidden_peer, query_peer, upstream_peer)
    )
    key_sum, value_sum = project_near(
        place, hidden, left_top, left_low, right_top, right_low, key_weight, value_weight
    )
    keep, send = project_far(
        place, far_top, far_low, key_weight, value_weight, key_sum, value_sum, cosine, sine
    )
    other = swap(send)
    mine_line = pack(keep, xn(keep), xb(keep), x2(keep))
    other_line = pack(other, yn(other), yb(other), y2(other))
    pieces = ring_gather(*mine_line, yn, yb) + ring_gather(*other_line, xn, xb)

    near_features = [left_top, left_low, right_top, right_low, far_top, far_low]
    own_features = [hidden, *near_features]
    peer_features = [hidden_peer]
    for feature in near_features:
        peer_features.append(swap(feature))
    features = flip(own_features, peer_features)

    out, *slot_grads = attend(table, queries, query_peer, upstream, upstream_peer, pieces)
    t_sent = send_all(slot_grads[:4], xn, xb, x2) + send_all(slot_grads[4:], yn, yb, y2)
    sums = combine(t_sent)
    t_last = send_all(sums[:4], yn, yb, y2) + send_all(sums[4:], xn, xb, x2)
    grads, grads_away = finish_grads(t_last, cosine, sine)
    grads_other = swap(grads_away)
    grads, grads_other = lax.optimization_barrier((grads, grads_other))

    out_other = swap(out[local_rows:])

    attention, query_grad = join_rows(place, out, out_other)

    w_parts = weight_partials(place, grads, features)
    w_sent = send_all(w_parts[:4], xn, xb, x2) + send_all(w_parts[4:], yn, yb, y2)
    parts = input_partials(place, grads, grads_other, key_weight, value_weight)
    _, from_back, from_next, from_far = send_all(parts, zn, zb, z2)
    hidden_grad = add_partials(parts[0], from_back, from_next, from_far)
    w_sums = combine(w_sent)
    w_last = send_all(w_sums[:4], yn, yb, y2) + send_all(w_sums[4:], xn, xb, x2)
    both, both_away = finish_weights(w_last)
    both_other = swap(both_away)
    key_weight_grad, value_weight_grad = join_weights(place, both, both_other)
    return (attention, query_grad, hidden_grad, key_weight_grad, value_weight_grad)


def solution(mesh):
    return jax.shard_map(
        program,
        mesh=mesh,
        in_specs=(
            P("ctx", "tp"),
            P("ctx", "tp"),
            P(None, "tp"),
            P(None, "tp"),
            P(),
            P("ctx", "tp"),
        ),
        out_specs=(P("ctx", "tp"), P("ctx", "tp"), P("ctx", "tp"), P("ctx", "tp"), P("ctx", "tp")),
        check_vma=False,
    )
```
